32 devices in a mesh: dp: 8 (over z, y), tensor: 4 (over x, core).
Axes of the slice: x: 2, y: 2, z: 4, core: 2. Of those that a mesh axis runs over, the one named last changes fastest.
Arguments:
- tokens: bfloat16 [16384, 768], P(('dp', 'tensor')), may hold values from -6 to 6
- lengths: int32 [8], P('dp'), may hold values from 512 to 2048, as said below
- arrival_slots: int32 [8, 2048], P('dp'), may hold values from 0 to 2047, each once within a row
- w_qkv: float32 [3, 768, 768], P(None, 'dp', 'tensor'), may hold values from -0.21875 to 0.21875
- w_out: float32 [768, 768], P('tensor', 'dp'), may hold values from -1.75 to 1.75
- w_up: float32 [768, 3072], P('dp', 'tensor'), may hold values from -0.21875 to 0.21875
- w_down: float32 [3072, 768], P('tensor', 'dp'), may hold values from -0.109375 to 0.109375
- w_proj: float32 [768, 128], P('dp'), may hold values from -0.21875 to 0.21875
- norm_gains: float32 [2, 768], P(None, 'dp'), may hold values from 0.1 to 1.9
- biases: float32 [6, 768], P(None, 'dp'), may hold values from -4 to 4
- up_bias: float32 [3072], P('dp'), may hold values from -4 to 4
- cotangent: bfloat16 [16384, 128], P(('dp', 'tensor')), may hold values from -6 to 6
Outputs:
- embeddings: float32 [16384, 128], P(('dp', 'tensor'))
- grad_tokens: float32 [16384, 768], P(('dp', 'tensor'))
- grad_qkv: float32 [3, 768, 768], P(None, 'dp', 'tensor')
- grad_out: float32 [768, 768], P('tensor', 'dp')
- grad_up: float32 [768, 3072], P('dp', 'tensor')
- grad_down: float32 [3072, 768], P('tensor', 'dp')
- grad_proj: float32 [768, 128], P('dp')
- grad_gains: float32 [2, 768], P(None, 'dp')
- grad_biases: float32 [6, 768], P(None, 'dp')
- grad_up_bias: float32 [3072], P('dp')
The draws below stay inside these ranges and needn't reach their ends.
Inputs may be any that keep to these rules, and one draw needn't show every extreme that they name: `lengths`: some passage fills its whole slot of 2048 positions. `arrival_slots`: each row names every slot of its group once.
All inputs are finite; a program needn't handle non-finite values.
Results may differ from the reference program's by a relative error of at most 0.02.
Values may be sent and summed in bfloat16 or wider, within the bound.
A program may use at most 128 MiB of HBM per device.

```python
import jax
import jax.numpy as jnp
from jax import lax

D = 768
HEADS = 12
HEAD_DIM = 64
FF = 3072
PROJ = 128
SLOT = 2048
SEQS = 1
GROUP = 2048
GROUPS = 8
PASSAGES = 8
TOKENS = 16384


def draw_lengths(key, part):
    first_key, second_key = jax.random.split(jax.random.fold_in(key, 11))
    values = jax.random.randint(first_key, (PASSAGES,), SLOT // 4, SLOT + 1)
    chosen = jax.random.randint(second_key, (), 0, PASSAGES)
    return jnp.where(jnp.arange(PASSAGES) == chosen, SLOT, values).astype(jnp.int32)


def raised(array, key, source, target, shards_of, factor):
    owner, partner = [(jnp.arange(array.shape[dim]) // (array.shape[dim] // shards_of)).reshape([-1 if axis == dim else 1 for axis in range(array.ndim)]) for dim in (source, target)]
    chosen = jax.random.permutation(key, shards_of)[partner]
    strong = (owner == chosen) | (owner == (partner + shards_of // 2) % shards_of)
    return jnp.where(strong, factor * array, array)


def block_levels(stream_key, dims, cuts, smallest, high):
    loudness, own = 1.0, jax.random.fold_in(stream_key, 6)
    for position, parts in cuts:
        heights = jnp.exp(jax.random.uniform(jax.random.fold_in(own, position), (parts,), jnp.float32, smallest / len(cuts), high / len(cuts)))
        loudness = loudness * jnp.repeat(heights, dims[position] // parts).reshape([-1 if axis == position else 1 for axis in range(len(dims))])
    return loudness


def bell_draw(rng, extent, scale, bound, pieces=(), held_as=jnp.bfloat16):
    drawn = scale * jax.random.normal(rng, extent, jnp.float32)
    if pieces:
        drawn = drawn * block_levels(rng, extent, pieces, -0.22, 0.18)
    return jnp.clip(drawn, -bound, bound).astype(held_as)


def bell_draw_with(key, shape, width, most, cuts, heavy, kind=jnp.bfloat16):
    result = width * jax.random.normal(key, shape, jnp.float32)
    if cuts:
        result = result * block_levels(key, shape, cuts, -0.22, 0.18)
    return jnp.clip(raised(result, jax.random.fold_in(key, 3), *heavy), -most, most).astype(kind)


def setup_inputs(seed: int = 0) -> dict:
    key_of = jax.random.split(jax.random.key(seed), 13)
    tokens = bell_draw_with(key_of[0], (TOKENS, D), 1.0, 6.0, ((0, 32),), (0, 1, 32, 2.75))
    lengths = draw_lengths(jax.random.fold_in(key_of[12], 71), 0)
    arrival_slots = jax.vmap(lambda own: jax.random.permutation(own, GROUP))(jax.random.split(key_of[2], GROUPS)).reshape((GROUPS, GROUP)).astype(jnp.int32)
    w_qkv = bell_draw(key_of[3], (3, D, D), D ** -0.5, 0.21875, ((1, 8), (2, 4)), jnp.float32)
    w_out = bell_draw(key_of[4], (D, D), (D // 64) ** -0.5, 1.75, ((0, 4), (1, 8)), jnp.float32)
    w_up = bell_draw(key_of[5], (D, FF), D ** -0.5, 0.21875, ((0, 8), (1, 4)), jnp.float32)
    w_down = bell_draw(key_of[6], (FF, D), FF ** -0.5, 0.109375, ((0, 4), (1, 8)), jnp.float32)
    w_proj = bell_draw(key_of[7], (D, PROJ), D ** -0.5, 0.21875, ((0, 8),), jnp.float32)
    norm_gains = jnp.clip(1.0 + 0.18 * jax.random.normal(key_of[8], (2, D), jnp.float32), 0.1, 1.9)
    biases = bell_draw(key_of[9], (6, D), 0.3, 4.0, ((1, 8),), jnp.float32)
    up_bias = bell_draw(key_of[10], (FF,), 0.3, 4.0, ((0, 8),), jnp.float32)
    cotangent = bell_draw(key_of[11], (TOKENS, PROJ), 1.0, 6.0, ((0, 32),))
    return {"tokens": tokens, "lengths": lengths, "arrival_slots": arrival_slots, "w_qkv": w_qkv, "w_out": w_out, "w_up": w_up, "w_down": w_down, "w_proj": w_proj, "norm_gains": norm_gains, "biases": biases, "up_bias": up_bias, "cotangent": cotangent}


EPS_NORM = 1e-06
EPS_UNIT = 1e-06
NEG_FILL = -1e+30
HIGHEST = lax.Precision.HIGHEST

@jax.custom_vjp
def low(v):
    return lax.optimization_barrier(v.astype(jnp.bfloat16)).astype(jnp.float32)

@jax.custom_vjp
def low_back(v):
    return v

def low_keep(v):
    return (low(v), None)

def low_pass(kept, grad):
    return (grad,)

def back_keep(v):
    return (v, None)

def back_low(kept, grad):
    return (low(grad),)
low.defvjp(low_keep, low_pass)
low_back.defvjp(back_keep, back_low)

def norm_rows(values, gain, shift):
    center = values - lax.optimization_barrier(jnp.mean(values, axis=-1, keepdims=True))
    spread = lax.optimization_barrier(jnp.mean(center * center, axis=-1, keepdims=True))
    return center * lax.rsqrt(spread + EPS_NORM) * gain + shift

def matmul(left, right):
    return jnp.dot(left, right, precision=HIGHEST, preferred_element_type=jnp.float32)

def group_forward(weight_set, arrived, slot_order, passage_len):
    w_qkv, w_out, w_up, w_down, w_proj, norm_gains, biases, up_bias = weight_set
    inverse = jnp.zeros((GROUP,), jnp.int32).at[slot_order].set(jnp.arange(GROUP, dtype=jnp.int32))
    slotted = arrived[inverse]
    zero_row = jnp.zeros((D,), jnp.float32)
    qkv_bias = jnp.stack([biases[0], zero_row, biases[1]])
    qkv_all = jnp.einsum('gd,cde->cge', slotted, w_qkv, precision=HIGHEST) + qkv_bias[:, None, :]
    qkv_all = low(low_back(qkv_all))
    head_view = qkv_all.reshape(3, SEQS, SLOT, HEADS, HEAD_DIM)
    key_mask = jnp.arange(SLOT, dtype=jnp.int32)[None, :] < passage_len[:, None]

    def passage(passage_item):
        queries, key_rows, value_rows, mask_row = passage_item
        scores = jnp.einsum('qhe,khe->hqk', queries, key_rows, precision=HIGHEST) * HEAD_DIM ** (-0.5)
        scores = low_back(scores)
        scores = jnp.where(mask_row[None, None, :], scores, NEG_FILL)
        soft_probs = low(jax.nn.softmax(scores, axis=-1))
        return jnp.einsum('hqk,khe->qhe', soft_probs, value_rows, precision=HIGHEST)
    context = lax.map(jax.checkpoint(passage), (head_view[0], head_view[1], head_view[2], key_mask))
    context = low(low_back(context.reshape(GROUP, D)))
    first_sum = slotted + low_back(matmul(context, w_out)) + biases[2]
    first_norm = norm_rows(first_sum, norm_gains[0], biases[3])
    ffn_pre = low_back(matmul(low(first_norm), w_up) + up_bias)
    hidden = low(jax.nn.gelu(ffn_pre, approximate=False))
    second_sum = first_norm + low_back(matmul(hidden, w_down)) + biases[4]
    second_norm = norm_rows(second_sum, norm_gains[1], biases[5])
    projected = low_back(matmul(low(second_norm), w_proj))
    positions = jnp.arange(GROUP, dtype=jnp.int32)
    row_keep = (positions % SLOT < passage_len[positions // SLOT]).astype(jnp.float32)
    unit_scale = lax.rsqrt(lax.optimization_barrier(jnp.sum(projected * projected, axis=-1, keepdims=True)) + EPS_UNIT)
    return projected * unit_scale * row_keep[:, None]

def reference(tokens, lengths, arrival_slots, w_qkv, w_out, w_up, w_down, w_proj, norm_gains, biases, up_bias, cotangent):
    weight_set = (w_qkv, w_out, w_up, w_down, w_proj, norm_gains, biases, up_bias)
    arrived_all = tokens.astype(jnp.float32)
    passage_len = lengths.reshape(GROUPS, SEQS)

    def forward(token_rows, weight_group):
        rounded = tuple((low(member) for member in weight_group))

        def one_group(group_item):
            rows_in, order_row, length_row = group_item
            return group_forward(rounded, rows_in, order_row, length_row)
        outputs = lax.map(jax.checkpoint(one_group), (token_rows.reshape(GROUPS, GROUP, D), arrival_slots, passage_len))
        return outputs.reshape(GROUPS * GROUP, PROJ)
    embeddings, pull_back = jax.vjp(forward, arrived_all, weight_set)
    grad_tokens, grads = pull_back(cotangent.astype(jnp.float32))
    return (embeddings, grad_tokens, grads[0], grads[1], grads[2], grads[3], grads[4], grads[5], grads[6], grads[7])
```

```python
import functools

import jax
import jax.numpy as jnp
from jax import lax
from jax.experimental import pallas as pl
from jax.experimental.pallas import tpu as pltpu
from jax.sharding import PartitionSpec as P

HEAD_DIM = 64
SLOT = 2048


EPS_NORM = 1e-06
EPS_UNIT = 1e-06
NEG_FILL = -1e30


def norm_rows(values, gain, shift):
    center = values - jnp.mean(values, axis=-1, keepdims=True)
    spread = jnp.mean(center * center, axis=-1, keepdims=True)
    return center * lax.rsqrt(spread + EPS_NORM) * gain + shift


def gelu_exact(values):
    return jax.nn.gelu(values, approximate=False)


def contract_rows(left, right):
    return lax.dot_general(
        left, right, (((0,), (0,)), ((), ())), preferred_element_type=jnp.float32
    )


def times_transposed(left, right):
    return lax.dot_general(
        left, right, (((1,), (1,)), ((), ())), preferred_element_type=jnp.float32
    )


def attend(query_heads, key_heads, value_heads, key_mask, num_blocks, factor):

    def one_block(position):
        passage_idx = position // num_blocks
        block_idx = position % num_blocks
        query_block = query_heads[passage_idx, block_idx]
        scores = (
            jnp.einsum(
                "qhe,khe->hqk",
                query_block,
                key_heads[passage_idx],
                preferred_element_type=jnp.float32,
            )
            * factor
        )
        scores = jnp.where(key_mask[passage_idx][None, None, :], scores, NEG_FILL)
        row_top = jnp.max(scores, axis=-1, keepdims=True)
        shifted = jnp.exp(scores - row_top)
        row_total = jnp.sum(shifted, axis=-1, keepdims=True)
        soft_low = (shifted / row_total).astype(jnp.bfloat16)
        result = jnp.einsum(
            "hqk,khe->qhe", soft_low, value_heads[passage_idx], preferred_element_type=jnp.float32
        )
        return (result, (row_top + jnp.log(row_total))[..., 0])

    return lax.map(one_block, jnp.arange(query_heads.shape[0] * num_blocks))


def attend_back(
    query_heads, key_heads, value_heads, dcontext_heads, log_total, key_mask, num_blocks, factor
):

    def passage(passage_idx):
        key_rows = key_heads[passage_idx]
        value_rows = value_heads[passage_idx]
        mask_row = key_mask[passage_idx][None, None, :]

        def step(carry, block_idx):
            dkey_sum, dvalue_sum = carry
            query_block = query_heads[passage_idx, block_idx]
            dout_block = dcontext_heads[passage_idx, block_idx]
            total_block = log_total[passage_idx * num_blocks + block_idx]
            scores = (
                jnp.einsum(
                    "qhe,khe->hqk", query_block, key_rows, preferred_element_type=jnp.float32
                )
                * factor
            )
            scores = jnp.where(mask_row, scores, NEG_FILL)
            soft_probs = jnp.exp(scores - total_block[..., None])
            dvalue_sum = dvalue_sum + jnp.einsum(
                "hqk,qhe->khe",
                soft_probs.astype(jnp.bfloat16),
                dout_block,
                preferred_element_type=jnp.float32,
            )
            dsoft = jnp.einsum(
                "qhe,khe->hqk", dout_block, value_rows, preferred_element_type=jnp.float32
            )
            dscore = (
                soft_probs * (dsoft - jnp.sum(soft_probs * dsoft, axis=-1, keepdims=True))
            ).astype(jnp.bfloat16)
            dquery = (
                jnp.einsum("hqk,khe->qhe", dscore, key_rows, preferred_element_type=jnp.float32)
                * factor
            )
            dkey_sum = (
                dkey_sum
                + jnp.einsum(
                    "hqk,qhe->khe", dscore, query_block, preferred_element_type=jnp.float32
                )
                * factor
            )
            return ((dkey_sum, dvalue_sum), dquery)

        zero_grad = jnp.zeros(key_rows.shape, jnp.float32)
        (dkey_sum, dvalue_sum), dquery = lax.scan(
            step, (zero_grad, zero_grad), jnp.arange(num_blocks)
        )
        return (dquery, dkey_sum, dvalue_sum)

    return lax.map(passage, jnp.arange(key_heads.shape[0]))


MESH = pl.DeviceIdType.MESH
VMEM = pl.BlockSpec(memory_space=pltpu.VMEM)
RING_MAX = 8
ROW_PIECES = 4


def ring_place(position, size):
    far = position // (size // 2)
    return 2 * ((1 - far) * position + far * (size - 1 - position)) + far


def ring_position(index, size):
    row, far = index // 2, index % 2
    return (1 - far) * row + far * (size - 1 - row)


def ring_hops(index, size):
    longer, shorter = size // 2, size - 1 - size // 2
    return (longer, shorter) if index % 2 == 0 else (shorter, longer)


class Ring:
    def __init__(self, size):
        self.size = size
        self.me = lax.axis_index("dp")
        self.position = ring_position(self.me, size)
        self.targets = (self.at(1), self.at(-1))

    def at(self, offset):
        return ring_place(lax.rem(self.position + (offset + self.size), self.size), self.size)


class Chip:
    def __init__(self):
        self.me = lax.axis_index("tensor")
        chip, core = self.me // 2, self.me % 2
        self.mate = 2 * chip + (1 - core)
        self.peer = 2 * (1 - chip) + core
        self.across = 2 * (1 - chip) + (1 - core)


def greet(devices):
    barrier = pltpu.get_barrier_semaphore()
    for device in devices:
        pl.semaphore_signal(barrier, inc=1, device_id=device, device_id_type=MESH)
    pl.semaphore_wait(barrier, len(devices))


def remote(source, target, send, recv, device):
    return pltpu.make_async_remote_copy(
        src_ref=source,
        dst_ref=target,
        send_sem=send,
        recv_sem=recv,
        device_id=device,
        device_id_type=MESH,
    )


class RingGather:
    def __init__(self, ring, shards, outs, send, recv):
        self.ring, self.shards, self.outs, self.send, self.recv = ring, shards, outs, send, recv

    def copy(self, i, way, hop):
        owner = self.ring.at(-hop if way == 0 else hop)
        target = self.outs[i].at[owner]
        return remote(
            self.shards[i] if hop == 0 else target,
            target,
            self.send.at[i, way, hop],
            self.recv.at[i, way, hop],
            {"dp": self.ring.targets[way]},
        )

    def each(self, hop):
        for i in range(len(self.shards)):
            for way in (0, 1):
                if hop < ring_hops(i, self.ring.size)[way]:
                    yield i, way

    def start(self):
        for i, way in self.each(0):
            self.copy(i, way, 0).start()
        for shard, out in zip(self.shards, self.outs):
            out[self.ring.me] = shard[...]

    def relay(self, hop):
        for i, way in self.each(hop - 1):
            self.copy(i, way, hop - 1).wait_recv()
            if hop < ring_hops(i, self.ring.size)[way]:
                self.copy(i, way, hop).start()

    def finish(self):
        for hop in range(self.ring.size // 2):
            for i, way in self.each(hop):
                self.copy(i, way, hop).wait_send()


class RingScatter:
    def __init__(self, ring, parts, landing, send, recv):
        self.ring, self.parts, self.landing, self.send, self.recv = ring, parts, landing, send, recv

    def slot(self, i, way, hop):
        return self.landing[i].at[hop + (0 if way == 0 else ring_hops(i, self.ring.size)[0])]

    def owner(self, i, way, hop):
        left = ring_hops(i, self.ring.size)[way] - hop
        return self.ring.at(left if way == 0 else -left)

    def copy(self, i, way, hop):
        source = self.parts[i].at[self.owner(i, way, 0)] if hop == 0 else self.slot(i, way, hop - 1)
        return remote(
            source,
            self.slot(i, way, hop),
            self.send.at[i, way, hop],
            self.recv.at[i, way, hop],
            {"dp": self.ring.targets[way]},
        )

    def each(self, hop):
        for i in range(len(self.parts)):
            for way in (0, 1):
                if hop < ring_hops(i, self.ring.size)[way]:
                    yield i, way

    def start(self):
        for i, way in self.each(0):
            self.copy(i, way, 0).start()

    def relay(self, hop):
        for i, way in self.each(hop - 1):
            self.copy(i, way, hop - 1).wait_recv()
            if hop < ring_hops(i, self.ring.size)[way]:
                slot = self.slot(i, way, hop - 1)
                own = self.parts[i][self.owner(i, way, hop)]
                slot[...] = (slot[...].astype(jnp.float32) + own.astype(jnp.float32)).astype(slot.dtype)
                self.copy(i, way, hop).start()

    def total(self, i):
        up, down = ring_hops(i, self.ring.size)
        return (
            self.parts[i][self.ring.me].astype(jnp.float32)
            + self.slot(i, 0, up - 1)[...].astype(jnp.float32)
            + self.slot(i, 1, down - 1)[...].astype(jnp.float32)
        )

    def finish(self):
        for hop in range(self.ring.size // 2):
            for i, way in self.each(hop):
                self.copy(i, way, hop).wait_send()


class RowGather:
    def __init__(self, chip, own, out, send, recv):
        self.chip, self.own, self.out, self.send, self.recv = chip, own, out, send, recv
        self.step = own.shape[0] // ROW_PIECES

    def copy(self, kind, piece):
        rows = pl.ds(piece * self.step, self.step)
        chip = self.chip
        owner = chip.peer if kind == 2 else chip.me
        target = self.out.at[owner, rows]
        device = chip.peer if kind == 0 else chip.mate
        return remote(
            target if kind == 2 else self.own.at[rows],
            target,
            self.send.at[kind, piece],
            self.recv.at[kind, piece],
            {"tensor": device},
        )

    def start(self):
        for kind in (0, 1):
            for piece in range(ROW_PIECES):
                self.copy(kind, piece).start()
        self.out[self.chip.me] = self.own[...]

    def relay(self, piece):
        self.copy(0, piece).wait_recv()
        self.copy(2, piece).start()

    def finish(self):
        for kind in (1, 2):
            for piece in range(ROW_PIECES):
                self.copy(kind, piece).wait_recv()
        for kind in (0, 1, 2):
            for piece in range(ROW_PIECES):
                self.copy(kind, piece).wait_send()


class RowScatter:
    def __init__(self, chip, parts, landing, send, recv):
        self.chip, self.parts, self.landing, self.send, self.recv = chip, parts, landing, send, recv
        self.step = parts.shape[1] // ROW_PIECES

    def rows(self, piece):
        return pl.ds(piece * self.step, self.step)

    def copy(self, kind, piece):
        chip, rows = self.chip, self.rows(piece)
        source = (
            self.parts.at[chip.across, rows],
            self.landing.at[0, rows],
            self.parts.at[chip.mate, rows],
        )[kind]
        return remote(
            source,
            self.landing.at[kind, rows],
            self.send.at[kind, piece],
            self.recv.at[kind, piece],
            {"tensor": chip.peer if kind == 1 else chip.mate},
        )

    def start(self):
        for kind in (0, 2):
            for piece in range(ROW_PIECES):
                self.copy(kind, piece).start()

    def relay(self, piece):
        rows = self.rows(piece)
        self.copy(0, piece).wait_recv()
        total = self.landing[0, rows].astype(jnp.float32) + self.parts[self.chip.peer, rows].astype(
            jnp.float32
        )
        self.landing[0, rows] = total.astype(self.landing.dtype)
        self.copy(1, piece).start()

    def total(self, piece):
        rows = self.rows(piece)
        self.copy(2, piece).wait_recv()
        self.copy(1, piece).wait_recv()
        return (
            self.parts[self.chip.me, rows].astype(jnp.float32)
            + self.landing[1, rows].astype(jnp.float32)
            + self.landing[2, rows].astype(jnp.float32)
        )

    def finish(self):
        for kind in (0, 1, 2):
            for piece in range(ROW_PIECES):
                self.copy(kind, piece).wait_send()


def row_sems():
    return [pltpu.SemaphoreType.DMA((3, ROW_PIECES))] * 2


def ring_sems(count, size):
    return [pltpu.SemaphoreType.DMA((count, 2, size // 2))] * 2


def comm_params(collective_id):
    return pltpu.CompilerParams(collective_id=collective_id, has_side_effects=True)


def gather_rows(own, collective_id):
    def kernel(own_ref, out_ref, send, recv):
        chip = Chip()
        greet(({"tensor": chip.mate}, {"tensor": chip.peer}))
        rows = RowGather(chip, own_ref, out_ref, send, recv)
        rows.start()
        for piece in range(ROW_PIECES):
            rows.relay(piece)
        rows.finish()

    out = pl.pallas_call(
        kernel,
        out_shape=jax.ShapeDtypeStruct((4, *own.shape), own.dtype),
        in_specs=[VMEM],
        out_specs=VMEM,
        scratch_shapes=row_sems(),
        compiler_params=comm_params(collective_id),
        name="gather_rows",
    )(own)
    return out.reshape(4 * own.shape[0], own.shape[1])


def scatter_rows(parts, collective_id):
    parts = parts.reshape(4, parts.shape[0] // 4, parts.shape[1])

    def kernel(parts_ref, out_ref, landing, send, recv):
        chip = Chip()
        greet(({"tensor": chip.mate}, {"tensor": chip.peer}))
        rows = RowScatter(chip, parts_ref, landing, send, recv)
        rows.start()
        for piece in range(ROW_PIECES):
            rows.relay(piece)
        for piece in range(ROW_PIECES):
            out_ref[rows.rows(piece)] = rows.total(piece)
        rows.finish()

    return pl.pallas_call(
        kernel,
        out_shape=jax.ShapeDtypeStruct(parts.shape[1:], jnp.float32),
        in_specs=[VMEM],
        out_specs=VMEM,
        scratch_shapes=[pltpu.VMEM((3, *parts.shape[1:]), parts.dtype)] + row_sems(),
        compiler_params=comm_params(collective_id),
        name="scatter_rows",
    )(parts)


def gather_all(shards, own, size, collective_id):
    if size > RING_MAX:
        return [lax.all_gather(shard, "dp") for shard in shards], gather_rows(own, collective_id)
    count = len(shards)

    def kernel(*refs):
        shard_refs, own_ref = refs[:count], refs[count]
        out_refs, rows_ref = refs[count + 1 : 2 * count + 1], refs[2 * count + 1]
        ring_send, ring_recv, row_send, row_recv = refs[2 * count + 2 :]
        ring, chip = Ring(size), Chip()
        greet(
            (
                {"dp": ring.targets[0]},
                {"dp": ring.targets[1]},
                {"tensor": chip.mate},
                {"tensor": chip.peer},
            )
        )
        rows = RowGather(chip, own_ref, rows_ref, row_send, row_recv)
        weights = RingGather(ring, shard_refs, out_refs, ring_send, ring_recv)
        rows.start()
        weights.start()
        for hop in range(1, size // 2 + 1):
            for piece in range(ROW_PIECES):
                if piece * (size // 2) // ROW_PIECES == hop - 1:
                    rows.relay(piece)
            weights.relay(hop)
        rows.finish()
        weights.finish()

    *gathered, arrived = pl.pallas_call(
        kernel,
        out_shape=[jax.ShapeDtypeStruct((size, *s.shape), s.dtype) for s in shards]
        + [jax.ShapeDtypeStruct((4, *own.shape), own.dtype)],
        in_specs=[VMEM] * (count + 1),
        out_specs=[VMEM] * (count + 1),
        scratch_shapes=ring_sems(count, size) + row_sems(),
        compiler_params=comm_params(collective_id),
        name="gather_all",
    )(*shards, own)
    return gathered, arrived.reshape(4 * own.shape[0], own.shape[1])


def scatter_all(parts, shared, rows_part, size, collective_id):
    if size > RING_MAX:
        summed = [lax.psum_scatter(p.astype(jnp.float32), "dp", scatter_dimension=0) for p in parts]
        summed[-shared:] = [lax.psum(s, "tensor") for s in summed[-shared:]]
        return summed, scatter_rows(rows_part, collective_id)
    count = len(parts)
    rows_part = rows_part.reshape(4, rows_part.shape[0] // 4, rows_part.shape[1])

    def kernel(*refs):
        part_refs, rows_ref = refs[:count], refs[count]
        out_refs, own_ref = refs[count + 1 : 2 * count + 1], refs[2 * count + 1]
        scratch = refs[2 * count + 2 :]
        landing, row_landing = scratch[:count], scratch[count]
        meets = scratch[count + 1 : count + 1 + shared]
        ring_send, ring_recv, row_send, row_recv, meet_send, meet_recv = scratch[count + 1 + shared :]
        ring, chip = Ring(size), Chip()
        others = (chip.mate, chip.peer, chip.across)
        greet(
            ({"dp": ring.targets[0]}, {"dp": ring.targets[1]})
            + tuple({"tensor": other} for other in others)
        )
        rows = RowScatter(chip, rows_ref, row_landing, row_send, row_recv)
        grads = RingScatter(ring, part_refs, landing, ring_send, ring_recv)
        rows.start()
        grads.start()
        for hop in range(1, size // 2 + 1):
            for piece in range(ROW_PIECES):
                if piece * (size // 2) // ROW_PIECES == hop - 1:
                    rows.relay(piece)
            grads.relay(hop)
        copies = []
        for j in range(shared):
            meets[j][chip.me] = grads.total(count - shared + j)
            for k, other in enumerate(others):
                copy = remote(
                    meets[j].at[chip.me],
                    meets[j].at[chip.me],
                    meet_send.at[j, k],
                    meet_recv.at[j, k],
                    {"tensor": other},
                )
                copy.start()
                copies.append(copy)
        for i in range(count - shared):
            out_refs[i][...] = grads.total(i)
        for piece in range(ROW_PIECES):
            own_ref[rows.rows(piece)] = rows.total(piece)
        for copy in copies:
            copy.wait_recv()
        for j in range(shared):
            out_refs[count - shared + j][...] = (meets[j][0] + meets[j][1]) + (meets[j][2] + meets[j][3])
        rows.finish()
        grads.finish()
        for copy in copies:
            copy.wait_send()

    f32 = jnp.float32
    *summed, own = pl.pallas_call(
        kernel,
        out_shape=[jax.ShapeDtypeStruct(p.shape[1:], f32) for p in parts]
        + [jax.ShapeDtypeStruct(rows_part.shape[1:], f32)],
        in_specs=[VMEM] * (count + 1),
        out_specs=[VMEM] * (count + 1),
        scratch_shapes=[pltpu.VMEM((size - 1, *p.shape[1:]), p.dtype) for p in parts]
        + [pltpu.VMEM((3, *rows_part.shape[1:]), rows_part.dtype)]
        + [pltpu.VMEM((4, *p.shape[1:]), f32) for p in parts[-shared:]]
        + ring_sems(count, size)
        + row_sems()
        + [pltpu.SemaphoreType.DMA((shared, 3))] * 2,
        compiler_params=comm_params(collective_id),
        name="scatter_all",
    )(*parts, rows_part)
    return summed, own


def enter_slots(slots, arrived, weight, shift):
    group, width = arrived.shape
    block = 256

    def kernel(slots_ref, arrived_ref, weight_ref, shift_ref, rows_ref, out_ref):
        first = pl.program_id(0) * block
        wanted = first + lax.broadcasted_iota(jnp.int32, (block, group), 0)
        pick = jnp.where(slots_ref[...] == wanted, 1.0, 0.0).astype(jnp.bfloat16)
        rows = jnp.dot(pick, arrived_ref[...], preferred_element_type=jnp.float32).astype(jnp.bfloat16)
        rows_ref[...] = rows
        out = jnp.dot(rows, weight_ref[...], preferred_element_type=jnp.float32) + shift_ref[...]
        out_ref[...] = out.astype(jnp.bfloat16)

    return pl.pallas_call(
        kernel,
        grid=(group // block,),
        in_specs=[VMEM] * 4,
        out_specs=[
            pl.BlockSpec((block, width), lambda i: (i, 0)),
            pl.BlockSpec((block, weight.shape[1]), lambda i: (i, 0)),
        ],
        out_shape=[
            jax.ShapeDtypeStruct((group, width), jnp.bfloat16),
            jax.ShapeDtypeStruct((group, weight.shape[1]), jnp.bfloat16),
        ],
        name="enter_slots",
    )(slots.reshape(1, group), arrived, weight, shift.reshape(1, -1))


def leave_slots(slots, rows):
    group, width = rows.shape
    block = 256

    def kernel(slots_ref, rows_ref, out_ref):
        slot = lax.broadcasted_iota(jnp.int32, (block, group), 1)
        pick = jnp.where(slots_ref[...] == slot, 1.0, 0.0).astype(jnp.bfloat16)
        out_ref[...] = jnp.dot(pick, rows_ref[...], preferred_element_type=jnp.float32).astype(
            jnp.bfloat16
        )

    return pl.pallas_call(
        kernel,
        grid=(group // block,),
        in_specs=[pl.BlockSpec((block, 1), lambda i: (i, 0)), VMEM],
        out_specs=pl.BlockSpec((block, width), lambda i: (i, 0)),
        out_shape=jax.ShapeDtypeStruct((group, width), jnp.bfloat16),
        name="leave_slots",
    )(slots.reshape(group, 1), rows)


def body(
    tokens,
    lengths,
    arrival_slots,
    w_qkv,
    w_out,
    w_up,
    w_down,
    w_proj,
    norm_gains,
    biases,
    up_bias,
    cotangent,
):
    tensor_size = lax.axis_size("tensor")
    tensor_pos = lax.axis_index("tensor")
    own_rows = tokens.shape[0]
    group_rows = own_rows * tensor_size
    passages = group_rows // SLOT
    block_rows = min(512, SLOT)
    num_blocks = SLOT // block_rows
    factor = HEAD_DIM ** (-0.5)
    slot_order = arrival_slots[0]
    size = lax.axis_size("dp")
    part_rows, width_local = w_qkv.shape[1:]
    low = jnp.bfloat16
    shards = [
        w_qkv.astype(low).transpose(1, 0, 2).reshape(part_rows, 3 * width_local),
        w_up.astype(low),
        w_out.astype(low).T,
        w_down.astype(low).T,
        w_proj.astype(low),
        jnp.concatenate(
            [norm_gains.astype(low), biases.astype(low), up_bias.astype(low).reshape(-1, part_rows)]
        ),
    ]
    gathered, arrived = gather_all(shards, tokens, size, 0)
    width = size * part_rows
    qkv_weight, up_weight, out_weight, down_weight, proj_weight = (
        g.reshape(width, g.shape[2]) for g in gathered[:5]
    )
    small = gathered[5].astype(jnp.float32)
    side = small[:, :8].transpose(1, 0, 2).reshape(8, width)
    gain_full, bias_full = side[:2], side[2:]
    upbias_full = small[:, 8:].reshape(-1)
    hidden_local = up_weight.shape[1]
    heads_local = width_local // HEAD_DIM
    col_start = tensor_pos * width_local
    query_bias = lax.dynamic_slice_in_dim(bias_full[0], col_start, width_local)
    value_bias = lax.dynamic_slice_in_dim(bias_full[1], col_start, width_local)
    qkv_bias = jnp.concatenate([query_bias, jnp.zeros_like(query_bias), value_bias])
    slotted, qkv_all = enter_slots(slot_order, arrived, qkv_weight, qkv_bias)
    row_start = tensor_pos * own_rows
    resid_input = lax.dynamic_slice_in_dim(slotted, row_start, own_rows, 0).astype(jnp.float32)
    positions = row_start + jnp.arange(own_rows, dtype=jnp.int32)
    row_keep = (positions % SLOT < lengths[positions // SLOT]).astype(jnp.float32)
    key_mask = jnp.arange(SLOT, dtype=jnp.int32)[None, :] < lengths[:, None]
    block_shape = (passages, num_blocks, block_rows, heads_local, HEAD_DIM)
    slot_shape = (passages, SLOT, heads_local, HEAD_DIM)
    query_heads = qkv_all[:, 0 * width_local : 1 * width_local].reshape(block_shape)
    key_heads = qkv_all[:, 1 * width_local : 2 * width_local].reshape(slot_shape)
    value_heads = qkv_all[:, 2 * width_local : 3 * width_local].reshape(slot_shape)
    attended, log_total = attend(query_heads, key_heads, value_heads, key_mask, num_blocks, factor)
    context = attended.reshape(group_rows, width_local).astype(jnp.bfloat16)
    attn_part = scatter_rows(times_transposed(context, out_weight).astype(low), 1)
    first_sum = resid_input + attn_part + bias_full[2]
    first_norm, back_first = jax.vjp(norm_rows, first_sum, gain_full[0], bias_full[3])
    first_low = first_norm.astype(jnp.bfloat16)
    mid_rows = gather_rows(first_low, 2)
    upbias_own = lax.dynamic_slice_in_dim(upbias_full, tensor_pos * hidden_local, hidden_local)
    ffn_pre = jnp.dot(mid_rows, up_weight, preferred_element_type=jnp.float32) + upbias_own
    hidden = gelu_exact(ffn_pre).astype(jnp.bfloat16)
    ffn_part = scatter_rows(times_transposed(hidden, down_weight).astype(low), 3)
    second_sum = first_norm + ffn_part + bias_full[4]
    second_norm, back_second = jax.vjp(norm_rows, second_sum, gain_full[1], bias_full[5])
    second_low = second_norm.astype(jnp.bfloat16)
    projected = jnp.dot(second_low, proj_weight, preferred_element_type=jnp.float32)

    def unit_rows(values):
        return (
            values
            * lax.rsqrt(jnp.sum(values * values, axis=-1, keepdims=True) + EPS_UNIT)
            * row_keep[:, None]
        )

    embeddings, back_unit = jax.vjp(unit_rows, projected)
    (dproj,) = back_unit(cotangent.astype(jnp.float32))
    dproj_low = dproj.astype(jnp.bfloat16)
    grad_proj = contract_rows(second_low, dproj_low)
    dsecond_norm = times_transposed(dproj_low, proj_weight)
    dsecond, grad_gain_two, grad_shift_two = back_second(dsecond_norm)
    dsecond_low = dsecond.astype(jnp.bfloat16)
    dsecond_rows = gather_rows(dsecond_low, 4)
    dhidden = jnp.dot(dsecond_rows, down_weight, preferred_element_type=jnp.float32)
    grad_down = contract_rows(dsecond_rows, hidden)
    (dpre,) = jax.vjp(gelu_exact, ffn_pre)[1](dhidden)
    dpre_low = dpre.astype(jnp.bfloat16)
    grad_upbias = lax.dynamic_update_slice_in_dim(
        jnp.zeros(upbias_full.shape, jnp.float32),
        jnp.sum(dpre_low.astype(jnp.float32), axis=0),
        tensor_pos * hidden_local,
        0,
    )
    grad_up = contract_rows(mid_rows, dpre_low)
    dfirst_norm = scatter_rows(times_transposed(dpre_low, up_weight).astype(low), 5)
    dfirst, grad_gain_one, grad_shift_one = back_first(dfirst_norm + dsecond)
    dfirst_low = dfirst.astype(jnp.bfloat16)
    dfirst_rows = gather_rows(dfirst_low, 6)
    dcontext = jnp.dot(dfirst_rows, out_weight, preferred_element_type=jnp.float32).astype(low)
    grad_out = contract_rows(dfirst_rows, context)
    dquery, dkey, dvalue = attend_back(
        query_heads,
        key_heads,
        value_heads,
        dcontext.reshape(block_shape),
        log_total,
        key_mask,
        num_blocks,
        factor,
    )
    dqkv = jnp.concatenate(
        [
            dquery.reshape(group_rows, width_local),
            dkey.reshape(group_rows, width_local),
            dvalue.reshape(group_rows, width_local),
        ],
        axis=1,
    ).astype(low)
    grad_qkv = contract_rows(slotted, dqkv)
    column_sums = jnp.sum(dqkv.astype(jnp.float32), axis=0).reshape(3, width_local)
    through = times_transposed(dqkv, qkv_weight)
    own_through = lax.dynamic_slice_in_dim(through, row_start, own_rows, 0) + dfirst
    through = lax.dynamic_update_slice_in_dim(through, own_through, row_start, 0).astype(low)
    leaving = leave_slots(slot_order, through)
    zero_row = jnp.zeros((bias_full.shape[1],), jnp.float32)
    grad_biases = jnp.stack(
        [
            lax.dynamic_update_slice_in_dim(zero_row, column_sums[0], col_start, 0),
            lax.dynamic_update_slice_in_dim(zero_row, column_sums[2], col_start, 0),
            jnp.sum(dfirst, axis=0),
            grad_shift_one,
            jnp.sum(dsecond, axis=0),
            grad_shift_two,
        ]
    )
    grad_gains = jnp.stack([grad_gain_one, grad_gain_two])
    small_grad = jnp.concatenate([grad_gains, grad_biases]).reshape(8, size, part_rows).transpose(1, 0, 2)
    small_grad = jnp.concatenate([small_grad, grad_upbias.reshape(size, -1, part_rows)], axis=1)
    parts = [
        grad.astype(low).reshape(size, part_rows, grad.shape[1])
        for grad in (grad_qkv, grad_up, grad_out, grad_down, grad_proj)
    ]
    summed, grad_tokens = scatter_all([*parts, small_grad], 2, leaving, size, 7)
    sum_qkv, sum_up, sum_out, sum_down, sum_proj, sum_small = summed
    return (
        embeddings,
        grad_tokens,
        sum_qkv.reshape(part_rows, 3, width_local).transpose(1, 0, 2),
        sum_out.T,
        sum_up,
        sum_down.T,
        sum_proj,
        sum_small[:2],
        sum_small[2:8],
        sum_small[8:].reshape(-1),
    )


def solution(mesh):
    return jax.shard_map(
        body,
        mesh=mesh,
        in_specs=(
            P(("dp", "tensor"), None),
            P("dp"),
            P("dp", None),
            P(None, "dp", "tensor"),
            P("tensor", "dp"),
            P("dp", "tensor"),
            P("tensor", "dp"),
            P("dp", None),
            P(None, "dp"),
            P(None, "dp"),
            P("dp"),
            P(("dp", "tensor"), None),
        ),
        out_specs=(
            P(("dp", "tensor"), None),
            P(("dp", "tensor"), None),
            P(None, "dp", "tensor"),
            P("tensor", "dp"),
            P("dp", "tensor"),
            P("tensor", "dp"),
            P("dp", None),
            P(None, "dp"),
            P(None, "dp"),
            P("dp"),
        ),
        check_vma=False,
    )
```

```python
import functools

import jax
import jax.numpy as jnp
from jax import lax
from jax.experimental import pallas as pl
from jax.experimental.pallas import tpu as pltpu
from jax.sharding import PartitionSpec as P

HEAD_DIM = 64
SLOT = 2048


EPS_NORM = 1e-06
EPS_UNIT = 1e-06
NEG_FILL = -1e30


def norm_rows(values, gain, shift):
    center = values - jnp.mean(values, axis=-1, keepdims=True)
    spread = jnp.mean(center * center, axis=-1, keepdims=True)
    return center * lax.rsqrt(spread + EPS_NORM) * gain + shift


def gelu_exact(values):
    return jax.nn.gelu(values, approximate=False)


def contract_rows(left, right):
    return lax.dot_general(
        left, right, (((0,), (0,)), ((), ())), preferred_element_type=jnp.float32
    )


def times_transposed(left, right):
    return lax.dot_general(
        left, right, (((1,), (1,)), ((), ())), preferred_element_type=jnp.float32
    )


MESH = pl.DeviceIdType.MESH
VMEM = pl.BlockSpec(memory_space=pltpu.VMEM)
WIDE = 128


def lane_index(rows):
    return lax.broadcasted_iota(jnp.int32, (rows, WIDE - HEAD_DIM), 1)


def thirds(column):
    parts = []
    for _ in range(3):
        part = column.astype(jnp.bfloat16).astype(jnp.float32)
        parts.append(part)
        column = column - part
    return parts


def beside(rows, columns):
    lane = lane_index(rows)
    out = jnp.zeros(lane.shape, jnp.float32)
    for i, column in enumerate(columns):
        out = jnp.where(lane == i, column, out)
    return out.astype(jnp.bfloat16)


def key_fill(length, keys):
    position = lax.broadcasted_iota(jnp.int32, (keys, 1), 0)
    return jnp.where(position < length, 0.0, NEG_FILL)


def attend(qkv, lengths, passages):
    rows, width = qkv.shape[0], qkv.shape[1] // 3
    keys, heads = rows // passages, width // HEAD_DIM
    block = 512
    steps = keys // block
    factor = HEAD_DIM ** (-0.5)

    def kernel(len_ref, query_ref, kv_ref, out_ref, exact_ref, total_ref, key_side, value_side):
        passage, step = pl.program_id(0), pl.program_id(1)

        @pl.when(step == 0)
        def _():
            fill = key_fill(len_ref[passage], keys)
            for h in range(heads):
                at = width + h * HEAD_DIM
                key_side[h, :, :HEAD_DIM] = kv_ref[:, at : at + HEAD_DIM]
                key_side[h, :, HEAD_DIM:] = beside(keys, [fill])
                value_side[h, :, :HEAD_DIM] = kv_ref[:, at + width : at + width + HEAD_DIM]
                value_side[h, :, HEAD_DIM:] = beside(keys, [1.0])

        ones = beside(block, [1.0])
        totals = jnp.zeros((block, WIDE), jnp.float32)
        lane = lax.broadcasted_iota(jnp.int32, (block, WIDE), 1)
        for h in range(heads):
            query = query_ref[:, h * HEAD_DIM : (h + 1) * HEAD_DIM] * jnp.bfloat16(factor)
            query = jnp.concatenate([query, ones], axis=1)
            scores = lax.dot_general(
                query, key_side[h], (((1,), (1,)), ((), ())), preferred_element_type=jnp.float32
            )
            top = jnp.max(scores, axis=-1, keepdims=True)
            soft = jnp.exp(scores - top).astype(jnp.bfloat16)
            mixed = jnp.dot(soft, value_side[h], preferred_element_type=jnp.float32)
            total = mixed[:, HEAD_DIM : HEAD_DIM + 1]
            result = mixed[:, :HEAD_DIM] / total
            exact_ref[:, h * HEAD_DIM : (h + 1) * HEAD_DIM] = result
            out_ref[:, h * HEAD_DIM : (h + 1) * HEAD_DIM] = result.astype(jnp.bfloat16)
            totals = jnp.where(lane == h, top + jnp.log(total), totals)
        total_ref[...] = totals

    def tile(columns):
        return pl.BlockSpec((block, columns), lambda p, i: (p * steps + i, 0))

    return pl.pallas_call(
        kernel,
        grid=(passages, steps),
        in_specs=[
            pl.BlockSpec(memory_space=pltpu.SMEM),
            tile(3 * width),
            pl.BlockSpec((keys, 3 * width), lambda p, i: (p, 0)),
        ],
        out_specs=[tile(width), tile(width), tile(WIDE)],
        out_shape=[
            jax.ShapeDtypeStruct((rows, width), jnp.bfloat16),
            jax.ShapeDtypeStruct((rows, width), jnp.float32),
            jax.ShapeDtypeStruct((rows, WIDE), jnp.float32),
        ],
        scratch_shapes=[pltpu.VMEM((heads, keys, WIDE), jnp.bfloat16)] * 2,
        name="attend",
    )(lengths, qkv, qkv)


def attend_back(qkv, dcontext, exact, totals, lengths, passages):
    rows, width = qkv.shape[0], qkv.shape[1] // 3
    keys, heads = rows // passages, width // HEAD_DIM
    block = 512
    steps = keys // block
    factor = HEAD_DIM ** (-0.5)

    def kernel(
        len_ref, query_ref, dout_ref, exact_ref, total_ref, kv_ref, out_ref, key_side, value_side, key_turned, sums
    ):
        passage, step = pl.program_id(0), pl.program_id(1)

        @pl.when(step == 0)
        def _():
            fill = key_fill(len_ref[passage], keys)
            for h in range(heads):
                at = width + h * HEAD_DIM
                key = kv_ref[:, at : at + HEAD_DIM]
                key_side[h, :, :HEAD_DIM] = key
                key_side[h, :, HEAD_DIM:] = beside(keys, [fill, 1.0, 1.0, 1.0])
                key_turned[h] = (key * jnp.bfloat16(factor)).T
                value_side[h, :, :HEAD_DIM] = kv_ref[:, at + width : at + width + HEAD_DIM]
                value_side[h, :, HEAD_DIM:] = beside(keys, [1.0, 1.0, 1.0])
            sums[...] = jnp.zeros_like(sums)

        first = pl.multiple_of(step * block, block)
        blank = jnp.zeros((block, HEAD_DIM), jnp.bfloat16)
        for h in range(heads):
            lanes = slice(h * HEAD_DIM, (h + 1) * HEAD_DIM)
            dout = dout_ref[:, lanes]
            delta = jnp.sum(dout.astype(jnp.float32) * exact_ref[:, lanes], axis=-1, keepdims=True)
            query = query_ref[:, lanes] * jnp.bfloat16(factor)
            query_wide = jnp.concatenate(
                [query, beside(block, [1.0, *thirds(-total_ref[:, h : h + 1])])], axis=1
            )
            dout_wide = jnp.concatenate([dout, beside(block, thirds(-delta))], axis=1)
            nt = (((1,), (1,)), ((), ()))
            soft = jnp.exp(
                lax.dot_general(key_side[h], query_wide, nt, preferred_element_type=jnp.float32)
            )
            dsoft = lax.dot_general(value_side[h], dout_wide, nt, preferred_element_type=jnp.float32)
            dscore = (soft * dsoft).astype(jnp.bfloat16)
            soft = soft.astype(jnp.bfloat16)
            sums[h] += jnp.dot(
                soft, jnp.concatenate([dout, blank], axis=1), preferred_element_type=jnp.float32
            ) + jnp.dot(
                dscore, jnp.concatenate([blank, query], axis=1), preferred_element_type=jnp.float32
            )
            dquery = jnp.dot(key_turned[h], dscore, preferred_element_type=jnp.float32)
            out_ref[pl.ds(first, block), lanes] = dquery.T.astype(jnp.bfloat16)

        @pl.when(step == steps - 1)
        def _():
            for h in range(heads):
                both = sums[h].astype(jnp.bfloat16)
                at = width + h * HEAD_DIM
                out_ref[:, at : at + HEAD_DIM] = both[:, HEAD_DIM:]
                out_ref[:, at + width : at + width + HEAD_DIM] = both[:, :HEAD_DIM]

    def tile(columns):
        return pl.BlockSpec((block, columns), lambda p, i: (p * steps + i, 0))

    whole = pl.BlockSpec((keys, 3 * width), lambda p, i: (p, 0))
    return pl.pallas_call(
        kernel,
        grid=(passages, steps),
        in_specs=[
            pl.BlockSpec(memory_space=pltpu.SMEM),
            tile(3 * width),
            tile(width),
            tile(width),
            tile(WIDE),
            whole,
        ],
        out_specs=whole,
        out_shape=jax.ShapeDtypeStruct((rows, 3 * width), jnp.bfloat16),
        scratch_shapes=[
            pltpu.VMEM((heads, keys, WIDE), jnp.bfloat16),
            pltpu.VMEM((heads, keys, WIDE), jnp.bfloat16),
            pltpu.VMEM((heads, HEAD_DIM, keys), jnp.bfloat16),
            pltpu.VMEM((heads, keys, WIDE), jnp.float32),
        ],
        name="attend_back",
    )(lengths, qkv, dcontext, exact, totals, qkv)


RING_MAX = 8
ROW_PIECES = 4


def ring_place(position, size):
    far = position // (size // 2)
    return 2 * ((1 - far) * position + far * (size - 1 - position)) + far


def ring_position(index, size):
    row, far = index // 2, index % 2
    return (1 - far) * row + far * (size - 1 - row)


def ring_hops(index, size):
    longer, shorter = size // 2, size - 1 - size // 2
    return (longer, shorter) if index % 2 == 0 else (shorter, longer)


class Ring:
    def __init__(self, size):
        self.size = size
        self.me = lax.axis_index("dp")
        self.position = ring_position(self.me, size)
        self.targets = (self.at(1), self.at(-1))

    def at(self, offset):
        return ring_place(lax.rem(self.position + (offset + self.size), self.size), self.size)


class Chip:
    def __init__(self):
        self.me = lax.axis_index("tensor")
        chip, core = self.me // 2, self.me % 2
        self.mate = 2 * chip + (1 - core)
        self.peer = 2 * (1 - chip) + core
        self.across = 2 * (1 - chip) + (1 - core)


def greet(devices):
    barrier = pltpu.get_barrier_semaphore()
    for device in devices:
        pl.semaphore_signal(barrier, inc=1, device_id=device, device_id_type=MESH)
    pl.semaphore_wait(barrier, len(devices))


def remote(source, target, send, recv, device):
    return pltpu.make_async_remote_copy(
        src_ref=source,
        dst_ref=target,
        send_sem=send,
        recv_sem=recv,
        device_id=device,
        device_id_type=MESH,
    )


class RingGather:
    def __init__(self, ring, shards, outs, send, recv):
        self.ring, self.shards, self.outs, self.send, self.recv = ring, shards, outs, send, recv

    def copy(self, i, way, hop):
        owner = self.ring.at(-hop if way == 0 else hop)
        target = self.outs[i].at[owner]
        return remote(
            self.shards[i] if hop == 0 else target,
            target,
            self.send.at[i, way, hop],
            self.recv.at[i, way, hop],
            {"dp": self.ring.targets[way]},
        )

    def each(self, hop):
        for i in range(len(self.shards)):
            for way in (0, 1):
                if hop < ring_hops(i, self.ring.size)[way]:
                    yield i, way

    def start(self):
        for i, way in self.each(0):
            self.copy(i, way, 0).start()
        for shard, out in zip(self.shards, self.outs):
            out[self.ring.me] = shard[...]

    def relay(self, hop):
        for i, way in self.each(hop - 1):
            self.copy(i, way, hop - 1).wait_recv()
            if hop < ring_hops(i, self.ring.size)[way]:
                self.copy(i, way, hop).start()

    def finish(self):
        for hop in range(self.ring.size // 2):
            for i, way in self.each(hop):
                self.copy(i, way, hop).wait_send()


class RingScatter:
    def __init__(self, ring, parts, landing, send, recv):
        self.ring, self.parts, self.landing, self.send, self.recv = ring, parts, landing, send, recv

    def slot(self, i, way, hop):
        return self.landing[i].at[hop + (0 if way == 0 else ring_hops(i, self.ring.size)[0])]

    def owner(self, i, way, hop):
        left = ring_hops(i, self.ring.size)[way] - hop
        return self.ring.at(left if way == 0 else -left)

    def copy(self, i, way, hop):
        source = self.parts[i].at[self.owner(i, way, 0)] if hop == 0 else self.slot(i, way, hop - 1)
        return remote(
            source,
            self.slot(i, way, hop),
            self.send.at[i, way, hop],
            self.recv.at[i, way, hop],
            {"dp": self.ring.targets[way]},
        )

    def each(self, hop):
        for i in range(len(self.parts)):
            for way in (0, 1):
                if hop < ring_hops(i, self.ring.size)[way]:
                    yield i, way

    def start(self):
        for i, way in self.each(0):
            self.copy(i, way, 0).start()

    def relay(self, hop):
        for i, way in self.each(hop - 1):
            self.copy(i, way, hop - 1).wait_recv()
            if hop < ring_hops(i, self.ring.size)[way]:
                slot = self.slot(i, way, hop - 1)
                own = self.parts[i][self.owner(i, way, hop)]
                slot[...] = (slot[...].astype(jnp.float32) + own.astype(jnp.float32)).astype(slot.dtype)
                self.copy(i, way, hop).start()

    def total(self, i):
        up, down = ring_hops(i, self.ring.size)
        return (
            self.parts[i][self.ring.me].astype(jnp.float32)
            + self.slot(i, 0, up - 1)[...].astype(jnp.float32)
            + self.slot(i, 1, down - 1)[...].astype(jnp.float32)
        )

    def finish(self):
        for hop in range(self.ring.size // 2):
            for i, way in self.each(hop):
                self.copy(i, way, hop).wait_send()


class RowGather:
    def __init__(self, chip, own, out, send, recv):
        self.chip, self.own, self.out, self.send, self.recv = chip, own, out, send, recv
        self.step = own.shape[0] // ROW_PIECES

    def copy(self, kind, piece):
        rows = pl.ds(piece * self.step, self.step)
        chip = self.chip
        owner = chip.peer if kind == 2 else chip.me
        target = self.out.at[owner, rows]
        device = chip.peer if kind == 0 else chip.mate
        return remote(
            target if kind == 2 else self.own.at[rows],
            target,
            self.send.at[kind, piece],
            self.recv.at[kind, piece],
            {"tensor": device},
        )

    def start(self):
        for kind in (0, 1):
            for piece in range(ROW_PIECES):
                self.copy(kind, piece).start()
        self.out[self.chip.me] = self.own[...]

    def relay(self, piece):
        self.copy(0, piece).wait_recv()
        self.copy(2, piece).start()

    def finish(self):
        for kind in (1, 2):
            for piece in range(ROW_PIECES):
                self.copy(kind, piece).wait_recv()
        for kind in (0, 1, 2):
            for piece in range(ROW_PIECES):
                self.copy(kind, piece).wait_send()


class RowScatter:
    def __init__(self, chip, parts, landing, send, recv):
        self.chip, self.parts, self.landing, self.send, self.recv = chip, parts, landing, send, recv
        self.step = parts.shape[1] // ROW_PIECES

    def rows(self, piece):
        return pl.ds(piece * self.step, self.step)

    def copy(self, kind, piece):
        chip, rows = self.chip, self.rows(piece)
        source = (
            self.parts.at[chip.across, rows],
            self.landing.at[0, rows],
            self.parts.at[chip.mate, rows],
        )[kind]
        return remote(
            source,
            self.landing.at[kind, rows],
            self.send.at[kind, piece],
            self.recv.at[kind, piece],
            {"tensor": chip.peer if kind == 1 else chip.mate},
        )

    def start(self):
        for kind in (0, 2):
            for piece in range(ROW_PIECES):
                self.copy(kind, piece).start()

    def relay(self, piece):
        rows = self.rows(piece)
        self.copy(0, piece).wait_recv()
        total = self.landing[0, rows].astype(jnp.float32) + self.parts[self.chip.peer, rows].astype(
            jnp.float32
        )
        self.landing[0, rows] = total.astype(self.landing.dtype)
        self.copy(1, piece).start()

    def total(self, piece):
        rows = self.rows(piece)
        self.copy(2, piece).wait_recv()
        self.copy(1, piece).wait_recv()
        return (
            self.parts[self.chip.me, rows].astype(jnp.float32)
            + self.landing[1, rows].astype(jnp.float32)
            + self.landing[2, rows].astype(jnp.float32)
        )

    def finish(self):
        for kind in (0, 1, 2):
            for piece in range(ROW_PIECES):
                self.copy(kind, piece).wait_send()


def row_sems():
    return [pltpu.SemaphoreType.DMA((3, ROW_PIECES))] * 2


def ring_sems(count, size):
    return [pltpu.SemaphoreType.DMA((count, 2, size // 2))] * 2


def comm_params(collective_id):
    return pltpu.CompilerParams(collective_id=collective_id, has_side_effects=True)


def gather_rows(own, collective_id):
    def kernel(own_ref, out_ref, send, recv):
        chip = Chip()
        greet(({"tensor": chip.mate}, {"tensor": chip.peer}))
        rows = RowGather(chip, own_ref, out_ref, send, recv)
        rows.start()
        for piece in range(ROW_PIECES):
            rows.relay(piece)
        rows.finish()

    out = pl.pallas_call(
        kernel,
        out_shape=jax.ShapeDtypeStruct((4, *own.shape), own.dtype),
        in_specs=[VMEM],
        out_specs=VMEM,
        scratch_shapes=row_sems(),
        compiler_params=comm_params(collective_id),
        name="gather_rows",
    )(own)
    return out.reshape(4 * own.shape[0], own.shape[1])


def scatter_rows(parts, collective_id):
    parts = parts.reshape(4, parts.shape[0] // 4, parts.shape[1])

    def kernel(parts_ref, out_ref, landing, send, recv):
        chip = Chip()
        greet(({"tensor": chip.mate}, {"tensor": chip.peer}))
        rows = RowScatter(chip, parts_ref, landing, send, recv)
        rows.start()
        for piece in range(ROW_PIECES):
            rows.relay(piece)
        for piece in range(ROW_PIECES):
            out_ref[rows.rows(piece)] = rows.total(piece)
        rows.finish()

    return pl.pallas_call(
        kernel,
        out_shape=jax.ShapeDtypeStruct(parts.shape[1:], jnp.float32),
        in_specs=[VMEM],
        out_specs=VMEM,
        scratch_shapes=[pltpu.VMEM((3, *parts.shape[1:]), parts.dtype)] + row_sems(),
        compiler_params=comm_params(collective_id),
        name="scatter_rows",
    )(parts)


def gather_all(shards, own, size, collective_id):
    if size > RING_MAX:
        return [lax.all_gather(shard, "dp") for shard in shards], gather_rows(own, collective_id)
    count = len(shards)

    def kernel(*refs):
        shard_refs, own_ref = refs[:count], refs[count]
        out_refs, rows_ref = refs[count + 1 : 2 * count + 1], refs[2 * count + 1]
        ring_send, ring_recv, row_send, row_recv = refs[2 * count + 2 :]
        ring, chip = Ring(size), Chip()
        greet(
            (
                {"dp": ring.targets[0]},
                {"dp": ring.targets[1]},
                {"tensor": chip.mate},
                {"tensor": chip.peer},
            )
        )
        rows = RowGather(chip, own_ref, rows_ref, row_send, row_recv)
        weights = RingGather(ring, shard_refs, out_refs, ring_send, ring_recv)
        rows.start()
        weights.start()
        for hop in range(1, size // 2 + 1):
            for piece in range(ROW_PIECES):
                if piece * (size // 2) // ROW_PIECES == hop - 1:
                    rows.relay(piece)
            weights.relay(hop)
        rows.finish()
        weights.finish()

    *gathered, arrived = pl.pallas_call(
        kernel,
        out_shape=[jax.ShapeDtypeStruct((size, *s.shape), s.dtype) for s in shards]
        + [jax.ShapeDtypeStruct((4, *own.shape), own.dtype)],
        in_specs=[VMEM] * (count + 1),
        out_specs=[VMEM] * (count + 1),
        scratch_shapes=ring_sems(count, size) + row_sems(),
        compiler_params=comm_params(collective_id),
        name="gather_all",
    )(*shards, own)
    return gathered, arrived.reshape(4 * own.shape[0], own.shape[1])


def scatter_all(parts, shared, rows_part, size, collective_id):
    if size > RING_MAX:
        summed = [lax.psum_scatter(p.astype(jnp.float32), "dp", scatter_dimension=0) for p in parts]
        summed[-shared:] = [lax.psum(s, "tensor") for s in summed[-shared:]]
        return summed, scatter_rows(rows_part, collective_id)
    count = len(parts)
    rows_part = rows_part.reshape(4, rows_part.shape[0] // 4, rows_part.shape[1])

    def kernel(*refs):
        part_refs, rows_ref = refs[:count], refs[count]
        out_refs, own_ref = refs[count + 1 : 2 * count + 1], refs[2 * count + 1]
        scratch = refs[2 * count + 2 :]
        landing, row_landing = scratch[:count], scratch[count]
        meets = scratch[count + 1 : count + 1 + shared]
        ring_send, ring_recv, row_send, row_recv, meet_send, meet_recv = scratch[count + 1 + shared :]
        ring, chip = Ring(size), Chip()
        others = (chip.mate, chip.peer, chip.across)
        greet(
            ({"dp": ring.targets[0]}, {"dp": ring.targets[1]})
            + tuple({"tensor": other} for other in others)
        )
        rows = RowScatter(chip, rows_ref, row_landing, row_send, row_recv)
        grads = RingScatter(ring, part_refs, landing, ring_send, ring_recv)
        rows.start()
        grads.start()
        for hop in range(1, size // 2 + 1):
            for piece in range(ROW_PIECES):
                if piece * (size // 2) // ROW_PIECES == hop - 1:
                    rows.relay(piece)
            grads.relay(hop)
        copies = []
        for j in range(shared):
            meets[j][chip.me] = grads.total(count - shared + j)
            for k, other in enumerate(others):
                copy = remote(
                    meets[j].at[chip.me],
                    meets[j].at[chip.me],
                    meet_send.at[j, k],
                    meet_recv.at[j, k],
                    {"tensor": other},
                )
                copy.start()
                copies.append(copy)
        for i in range(count - shared):
            out_refs[i][...] = grads.total(i)
        for piece in range(ROW_PIECES):
            own_ref[rows.rows(piece)] = rows.total(piece)
        for copy in copies:
            copy.wait_recv()
        for j in range(shared):
            out_refs[count - shared + j][...] = (meets[j][0] + meets[j][1]) + (meets[j][2] + meets[j][3])
        rows.finish()
        grads.finish()
        for copy in copies:
            copy.wait_send()

    f32 = jnp.float32
    *summed, own = pl.pallas_call(
        kernel,
        out_shape=[jax.ShapeDtypeStruct(p.shape[1:], f32) for p in parts]
        + [jax.ShapeDtypeStruct(rows_part.shape[1:], f32)],
        in_specs=[VMEM] * (count + 1),
        out_specs=[VMEM] * (count + 1),
        scratch_shapes=[pltpu.VMEM((size - 1, *p.shape[1:]), p.dtype) for p in parts]
        + [pltpu.VMEM((3, *rows_part.shape[1:]), rows_part.dtype)]
        + [pltpu.VMEM((4, *p.shape[1:]), f32) for p in parts[-shared:]]
        + ring_sems(count, size)
        + row_sems()
        + [pltpu.SemaphoreType.DMA((shared, 3))] * 2,
        compiler_params=comm_params(collective_id),
        name="scatter_all",
    )(*parts, rows_part)
    return summed, own


def enter_slots(slots, arrived, weight, shift):
    group, width = arrived.shape
    block = 256

    def kernel(slots_ref, arrived_ref, weight_ref, shift_ref, rows_ref, out_ref):
        first = pl.program_id(0) * block
        wanted = first + lax.broadcasted_iota(jnp.int32, (block, group), 0)
        pick = jnp.where(slots_ref[...] == wanted, 1.0, 0.0).astype(jnp.bfloat16)
        rows = jnp.dot(pick, arrived_ref[...], preferred_element_type=jnp.float32).astype(jnp.bfloat16)
        rows_ref[...] = rows
        out = jnp.dot(rows, weight_ref[...], preferred_element_type=jnp.float32) + shift_ref[...]
        out_ref[...] = out.astype(jnp.bfloat16)

    return pl.pallas_call(
        kernel,
        grid=(group // block,),
        in_specs=[VMEM] * 4,
        out_specs=[
            pl.BlockSpec((block, width), lambda i: (i, 0)),
            pl.BlockSpec((block, weight.shape[1]), lambda i: (i, 0)),
        ],
        out_shape=[
            jax.ShapeDtypeStruct((group, width), jnp.bfloat16),
            jax.ShapeDtypeStruct((group, weight.shape[1]), jnp.bfloat16),
        ],
        name="enter_slots",
    )(slots.reshape(1, group), arrived, weight, shift.reshape(1, -1))


def leave_slots(slots, rows):
    group, width = rows.shape
    block = 256

    def kernel(slots_ref, rows_ref, out_ref):
        slot = lax.broadcasted_iota(jnp.int32, (block, group), 1)
        pick = jnp.where(slots_ref[...] == slot, 1.0, 0.0).astype(jnp.bfloat16)
        out_ref[...] = jnp.dot(pick, rows_ref[...], preferred_element_type=jnp.float32).astype(
            jnp.bfloat16
        )

    return pl.pallas_call(
        kernel,
        grid=(group // block,),
        in_specs=[pl.BlockSpec((block, 1), lambda i: (i, 0)), VMEM],
        out_specs=pl.BlockSpec((block, width), lambda i: (i, 0)),
        out_shape=jax.ShapeDtypeStruct((group, width), jnp.bfloat16),
        name="leave_slots",
    )(slots.reshape(group, 1), rows)


def body(
    tokens,
    lengths,
    arrival_slots,
    w_qkv,
    w_out,
    w_up,
    w_down,
    w_proj,
    norm_gains,
    biases,
    up_bias,
    cotangent,
):
    tensor_size = lax.axis_size("tensor")
    tensor_pos = lax.axis_index("tensor")
    own_rows = tokens.shape[0]
    group_rows = own_rows * tensor_size
    passages = group_rows // SLOT
    slot_order = arrival_slots[0]
    size = lax.axis_size("dp")
    part_rows, width_local = w_qkv.shape[1:]
    low = jnp.bfloat16
    shards = [
        w_qkv.astype(low).transpose(1, 0, 2).reshape(part_rows, 3 * width_local),
        w_up.astype(low),
        w_out.astype(low).T,
        w_down.astype(low).T,
        w_proj.astype(low),
        jnp.concatenate(
            [norm_gains.astype(low), biases.astype(low), up_bias.astype(low).reshape(-1, part_rows)]
        ),
    ]
    gathered, arrived = gather_all(shards, tokens, size, 0)
    width = size * part_rows
    qkv_weight, up_weight, out_weight, down_weight, proj_weight = (
        g.reshape(width, g.shape[2]) for g in gathered[:5]
    )
    small = gathered[5].astype(jnp.float32)
    side = small[:, :8].transpose(1, 0, 2).reshape(8, width)
    gain_full, bias_full = side[:2], side[2:]
    upbias_full = small[:, 8:].reshape(-1)
    hidden_local = up_weight.shape[1]
    heads_local = width_local // HEAD_DIM
    col_start = tensor_pos * width_local
    query_bias = lax.dynamic_slice_in_dim(bias_full[0], col_start, width_local)
    value_bias = lax.dynamic_slice_in_dim(bias_full[1], col_start, width_local)
    qkv_bias = jnp.concatenate([query_bias, jnp.zeros_like(query_bias), value_bias])
    slotted, qkv_all = enter_slots(slot_order, arrived, qkv_weight, qkv_bias)
    row_start = tensor_pos * own_rows
    resid_input = lax.dynamic_slice_in_dim(slotted, row_start, own_rows, 0).astype(jnp.float32)
    positions = row_start + jnp.arange(own_rows, dtype=jnp.int32)
    row_keep = (positions % SLOT < lengths[positions // SLOT]).astype(jnp.float32)
    context, exact, totals = attend(qkv_all, lengths, passages)
    attn_part = scatter_rows(times_transposed(context, out_weight).astype(low), 1)
    first_sum = resid_input + attn_part + bias_full[2]
    first_norm, back_first = jax.vjp(norm_rows, first_sum, gain_full[0], bias_full[3])
    first_low = first_norm.astype(jnp.bfloat16)
    mid_rows = gather_rows(first_low, 2)
    upbias_own = lax.dynamic_slice_in_dim(upbias_full, tensor_pos * hidden_local, hidden_local)
    ffn_pre = jnp.dot(mid_rows, up_weight, preferred_element_type=jnp.float32) + upbias_own
    hidden = gelu_exact(ffn_pre).astype(jnp.bfloat16)
    ffn_part = scatter_rows(times_transposed(hidden, down_weight).astype(low), 3)
    second_sum = first_norm + ffn_part + bias_full[4]
    second_norm, back_second = jax.vjp(norm_rows, second_sum, gain_full[1], bias_full[5])
    second_low = second_norm.astype(jnp.bfloat16)
    projected = jnp.dot(second_low, proj_weight, preferred_element_type=jnp.float32)

    def unit_rows(values):
        return (
            values
            * lax.rsqrt(jnp.sum(values * values, axis=-1, keepdims=True) + EPS_UNIT)
            * row_keep[:, None]
        )

    embeddings, back_unit = jax.vjp(unit_rows, projected)
    (dproj,) = back_unit(cotangent.astype(jnp.float32))
    dproj_low = dproj.astype(jnp.bfloat16)
    grad_proj = contract_rows(second_low, dproj_low)
    dsecond_norm = times_transposed(dproj_low, proj_weight)
    dsecond, grad_gain_two, grad_shift_two = back_second(dsecond_norm)
    dsecond_low = dsecond.astype(jnp.bfloat16)
    dsecond_rows = gather_rows(dsecond_low, 4)
    dhidden = jnp.dot(dsecond_rows, down_weight, preferred_element_type=jnp.float32)
    grad_down = contract_rows(dsecond_rows, hidden)
    (dpre,) = jax.vjp(gelu_exact, ffn_pre)[1](dhidden)
    dpre_low = dpre.astype(jnp.bfloat16)
    grad_upbias = lax.dynamic_update_slice_in_dim(
        jnp.zeros(upbias_full.shape, jnp.float32),
        jnp.sum(dpre_low.astype(jnp.float32), axis=0),
        tensor_pos * hidden_local,
        0,
    )
    grad_up = contract_rows(mid_rows, dpre_low)
    dfirst_norm = scatter_rows(times_transposed(dpre_low, up_weight).astype(low), 5)
    dfirst, grad_gain_one, grad_shift_one = back_first(dfirst_norm + dsecond)
    dfirst_low = dfirst.astype(jnp.bfloat16)
    dfirst_rows = gather_rows(dfirst_low, 6)
    dcontext = jnp.dot(dfirst_rows, out_weight, preferred_element_type=jnp.float32).astype(low)
    grad_out = contract_rows(dfirst_rows, context)
    dqkv = attend_back(qkv_all, dcontext, exact, totals, lengths, passages)
    grad_qkv = contract_rows(slotted, dqkv)
    column_sums = jnp.sum(dqkv.astype(jnp.float32), axis=0).reshape(3, width_local)
    through = times_transposed(dqkv, qkv_weight)
    own_through = lax.dynamic_slice_in_dim(through, row_start, own_rows, 0) + dfirst
    through = lax.dynamic_update_slice_in_dim(through, own_through, row_start, 0).astype(low)
    leaving = leave_slots(slot_order, through)
    zero_row = jnp.zeros((bias_full.shape[1],), jnp.float32)
    grad_biases = jnp.stack(
        [
            lax.dynamic_update_slice_in_dim(zero_row, column_sums[0], col_start, 0),
            lax.dynamic_update_slice_in_dim(zero_row, column_sums[2], col_start, 0),
            jnp.sum(dfirst, axis=0),
            grad_shift_one,
            jnp.sum(dsecond, axis=0),
            grad_shift_two,
        ]
    )
    grad_gains = jnp.stack([grad_gain_one, grad_gain_two])
    small_grad = jnp.concatenate([grad_gains, grad_biases]).reshape(8, size, part_rows).transpose(1, 0, 2)
    small_grad = jnp.concatenate([small_grad, grad_upbias.reshape(size, -1, part_rows)], axis=1)
    parts = [
        grad.astype(low).reshape(size, part_rows, grad.shape[1])
        for grad in (grad_qkv, grad_up, grad_out, grad_down, grad_proj)
    ]
    summed, grad_tokens = scatter_all([*parts, small_grad], 2, leaving, size, 7)
    sum_qkv, sum_up, sum_out, sum_down, sum_proj, sum_small = summed
    return (
        embeddings,
        grad_tokens,
        sum_qkv.reshape(part_rows, 3, width_local).transpose(1, 0, 2),
        sum_out.T,
        sum_up,
        sum_down.T,
        sum_proj,
        sum_small[:2],
        sum_small[2:8],
        sum_small[8:].reshape(-1),
    )


def solution(mesh):
    return jax.shard_map(
        body,
        mesh=mesh,
        in_specs=(
            P(("dp", "tensor"), None),
            P("dp"),
            P("dp", None),
            P(None, "dp", "tensor"),
            P("tensor", "dp"),
            P("dp", "tensor"),
            P("tensor", "dp"),
            P("dp", None),
            P(None, "dp"),
            P(None, "dp"),
            P("dp"),
            P(("dp", "tensor"), None),
        ),
        out_specs=(
            P(("dp", "tensor"), None),
            P(("dp", "tensor"), None),
            P(None, "dp", "tensor"),
            P("tensor", "dp"),
            P("dp", "tensor"),
            P("tensor", "dp"),
            P("dp", None),
            P(None, "dp"),
            P(None, "dp"),
            P("dp"),
        ),
        check_vma=False,
    )
```

```python
import jax
import jax.numpy as jnp
from jax import lax
from jax.experimental import pallas as pl
from jax.experimental.pallas import tpu as pltpu
from jax.sharding import PartitionSpec as P

HEAD_DIM = 64
SLOT = 2048


EPS_NORM = 1e-06
EPS_UNIT = 1e-06
NEG_FILL = -1e30


def norm_rows(values, gain, shift):
    center = values - jnp.mean(values, axis=-1, keepdims=True)
    spread = jnp.mean(center * center, axis=-1, keepdims=True)
    return center * lax.rsqrt(spread + EPS_NORM) * gain + shift


def contract_rows(left, right):
    return lax.dot_general(
        left, right, (((0,), (0,)), ((), ())), preferred_element_type=jnp.float32
    )


def times_transposed(left, right):
    return lax.dot_general(
        left, right, (((1,), (1,)), ((), ())), preferred_element_type=jnp.float32
    )


MESH = pl.DeviceIdType.MESH
VMEM = pl.BlockSpec(memory_space=pltpu.VMEM)
WIDE = 128


def lane_index(rows):
    return lax.broadcasted_iota(jnp.int32, (rows, WIDE - HEAD_DIM), 1)


def thirds(column):
    parts = []
    for _ in range(3):
        part = column.astype(jnp.bfloat16).astype(jnp.float32)
        parts.append(part)
        column = column - part
    return parts


def beside(rows, columns):
    lane = lane_index(rows)
    out = jnp.zeros(lane.shape, jnp.float32)
    for i, column in enumerate(columns):
        out = jnp.where(lane == i, column, out)
    return out.astype(jnp.bfloat16)


def key_fill(length, keys):
    position = lax.broadcasted_iota(jnp.int32, (keys, 1), 0)
    return jnp.where(position < length, 0.0, NEG_FILL)


def attend(qkv, lengths, passages):
    rows, width = qkv.shape[0], qkv.shape[1] // 3
    keys, heads = rows // passages, width // HEAD_DIM
    block = 512
    steps = keys // block
    factor = HEAD_DIM ** (-0.5)

    def kernel(len_ref, query_ref, kv_ref, out_ref, exact_ref, total_ref, key_side, value_side):
        passage, step = pl.program_id(0), pl.program_id(1)

        @pl.when(step == 0)
        def _():
            fill = key_fill(len_ref[passage], keys)
            for h in range(heads):
                at = width + h * HEAD_DIM
                key_side[h, :, :HEAD_DIM] = kv_ref[:, at : at + HEAD_DIM]
                key_side[h, :, HEAD_DIM:] = beside(keys, [fill])
                value_side[h, :, :HEAD_DIM] = kv_ref[:, at + width : at + width + HEAD_DIM]
                value_side[h, :, HEAD_DIM:] = beside(keys, [1.0])

        ones = beside(block, [1.0])
        totals = jnp.zeros((block, WIDE), jnp.float32)
        lane = lax.broadcasted_iota(jnp.int32, (block, WIDE), 1)
        for h in range(heads):
            query = query_ref[:, h * HEAD_DIM : (h + 1) * HEAD_DIM] * jnp.bfloat16(factor)
            query = jnp.concatenate([query, ones], axis=1)
            scores = lax.dot_general(
                query, key_side[h], (((1,), (1,)), ((), ())), preferred_element_type=jnp.float32
            )
            top = jnp.max(scores, axis=-1, keepdims=True)
            soft = jnp.exp(scores - top).astype(jnp.bfloat16)
            mixed = jnp.dot(soft, value_side[h], preferred_element_type=jnp.float32)
            total = mixed[:, HEAD_DIM : HEAD_DIM + 1]
            result = mixed[:, :HEAD_DIM] / total
            exact_ref[:, h * HEAD_DIM : (h + 1) * HEAD_DIM] = result
            out_ref[:, h * HEAD_DIM : (h + 1) * HEAD_DIM] = result.astype(jnp.bfloat16)
            totals = jnp.where(lane == h, top + jnp.log(total), totals)
        total_ref[...] = totals

    def tile(columns):
        return pl.BlockSpec((block, columns), lambda p, i: (p * steps + i, 0))

    return pl.pallas_call(
        kernel,
        grid=(passages, steps),
        in_specs=[
            pl.BlockSpec(memory_space=pltpu.SMEM),
            tile(3 * width),
            pl.BlockSpec((keys, 3 * width), lambda p, i: (p, 0)),
        ],
        out_specs=[tile(width), tile(width), tile(WIDE)],
        out_shape=[
            jax.ShapeDtypeStruct((rows, width), jnp.bfloat16),
            jax.ShapeDtypeStruct((rows, width), jnp.float32),
            jax.ShapeDtypeStruct((rows, WIDE), jnp.float32),
        ],
        scratch_shapes=[pltpu.VMEM((heads, keys, WIDE), jnp.bfloat16)] * 2,
        name="attend",
    )(lengths, qkv, qkv)


def attend_back(qkv, dcontext, exact, totals, lengths, passages):
    rows, width = qkv.shape[0], qkv.shape[1] // 3
    keys, heads = rows // passages, width // HEAD_DIM
    block = 512
    steps = keys // block
    factor = HEAD_DIM ** (-0.5)

    def kernel(
        len_ref, query_ref, dout_ref, exact_ref, total_ref, kv_ref, out_ref, key_side, value_side, key_turned, sums
    ):
        passage, step = pl.program_id(0), pl.program_id(1)

        @pl.when(step == 0)
        def _():
            fill = key_fill(len_ref[passage], keys)
            for h in range(heads):
                at = width + h * HEAD_DIM
                key = kv_ref[:, at : at + HEAD_DIM]
                key_side[h, :, :HEAD_DIM] = key
                key_side[h, :, HEAD_DIM:] = beside(keys, [fill, 1.0, 1.0, 1.0])
                key_turned[h] = (key * jnp.bfloat16(factor)).T
                value_side[h, :, :HEAD_DIM] = kv_ref[:, at + width : at + width + HEAD_DIM]
                value_side[h, :, HEAD_DIM:] = beside(keys, [1.0, 1.0, 1.0])
            sums[...] = jnp.zeros_like(sums)

        first = pl.multiple_of(step * block, block)
        blank = jnp.zeros((block, HEAD_DIM), jnp.bfloat16)
        for h in range(heads):
            lanes = slice(h * HEAD_DIM, (h + 1) * HEAD_DIM)
            dout = dout_ref[:, lanes]
            delta = jnp.sum(dout.astype(jnp.float32) * exact_ref[:, lanes], axis=-1, keepdims=True)
            query = query_ref[:, lanes] * jnp.bfloat16(factor)
            query_wide = jnp.concatenate(
                [query, beside(block, [1.0, *thirds(-total_ref[:, h : h + 1])])], axis=1
            )
            dout_wide = jnp.concatenate([dout, beside(block, thirds(-delta))], axis=1)
            nt = (((1,), (1,)), ((), ()))
            soft = jnp.exp(
                lax.dot_general(key_side[h], query_wide, nt, preferred_element_type=jnp.float32)
            )
            dsoft = lax.dot_general(value_side[h], dout_wide, nt, preferred_element_type=jnp.float32)
            dscore = (soft * dsoft).astype(jnp.bfloat16)
            soft = soft.astype(jnp.bfloat16)
            sums[h] += jnp.dot(
                soft, jnp.concatenate([dout, blank], axis=1), preferred_element_type=jnp.float32
            ) + jnp.dot(
                dscore, jnp.concatenate([blank, query], axis=1), preferred_element_type=jnp.float32
            )
            dquery = jnp.dot(key_turned[h], dscore, preferred_element_type=jnp.float32)
            out_ref[pl.ds(first, block), lanes] = dquery.T.astype(jnp.bfloat16)

        @pl.when(step == steps - 1)
        def _():
            for h in range(heads):
                both = sums[h].astype(jnp.bfloat16)
                at = width + h * HEAD_DIM
                out_ref[:, at : at + HEAD_DIM] = both[:, HEAD_DIM:]
                out_ref[:, at + width : at + width + HEAD_DIM] = both[:, :HEAD_DIM]

    def tile(columns):
        return pl.BlockSpec((block, columns), lambda p, i: (p * steps + i, 0))

    whole = pl.BlockSpec((keys, 3 * width), lambda p, i: (p, 0))
    return pl.pallas_call(
        kernel,
        grid=(passages, steps),
        in_specs=[
            pl.BlockSpec(memory_space=pltpu.SMEM),
            tile(3 * width),
            tile(width),
            tile(width),
            tile(WIDE),
            whole,
        ],
        out_specs=whole,
        out_shape=jax.ShapeDtypeStruct((rows, 3 * width), jnp.bfloat16),
        scratch_shapes=[
            pltpu.VMEM((heads, keys, WIDE), jnp.bfloat16),
            pltpu.VMEM((heads, keys, WIDE), jnp.bfloat16),
            pltpu.VMEM((heads, HEAD_DIM, keys), jnp.bfloat16),
            pltpu.VMEM((heads, keys, WIDE), jnp.float32),
        ],
        name="attend_back",
    )(lengths, qkv, dcontext, exact, totals, qkv)


RING_MAX = 8
ROW_PIECES = 4


def ring_place(position, size):
    far = position // (size // 2)
    return 2 * ((1 - far) * position + far * (size - 1 - position)) + far


def ring_position(index, size):
    row, far = index // 2, index % 2
    return (1 - far) * row + far * (size - 1 - row)


def ring_hops(index, size):
    longer, shorter = size // 2, size - 1 - size // 2
    return (longer, shorter) if index % 2 == 0 else (shorter, longer)


class Ring:
    def __init__(self, size):
        self.size = size
        self.me = lax.axis_index("dp")
        self.position = ring_position(self.me, size)
        self.targets = (self.at(1), self.at(-1))

    def at(self, offset):
        return ring_place(lax.rem(self.position + (offset + self.size), self.size), self.size)


class Chip:
    def __init__(self):
        self.me = lax.axis_index("tensor")
        chip, core = self.me // 2, self.me % 2
        self.mate = 2 * chip + (1 - core)
        self.peer = 2 * (1 - chip) + core
        self.across = 2 * (1 - chip) + (1 - core)


def greet(devices):
    barrier = pltpu.get_barrier_semaphore()
    for device in devices:
        pl.semaphore_signal(barrier, inc=1, device_id=device, device_id_type=MESH)
    pl.semaphore_wait(barrier, len(devices))


def remote(source, target, send, recv, device):
    return pltpu.make_async_remote_copy(
        src_ref=source,
        dst_ref=target,
        send_sem=send,
        recv_sem=recv,
        device_id=device,
        device_id_type=MESH,
    )


class RingGather:
    def __init__(self, ring, shards, outs, send, recv):
        self.ring, self.shards, self.outs, self.send, self.recv = ring, shards, outs, send, recv

    def copy(self, i, way, hop):
        owner = self.ring.at(-hop if way == 0 else hop)
        target = self.outs[i].at[owner]
        return remote(
            self.shards[i] if hop == 0 else target,
            target,
            self.send.at[i, way, hop],
            self.recv.at[i, way, hop],
            {"dp": self.ring.targets[way]},
        )

    def each(self, hop):
        for i in range(len(self.shards)):
            for way in (0, 1):
                if hop < ring_hops(i, self.ring.size)[way]:
                    yield i, way

    def start(self):
        for i, way in self.each(0):
            self.copy(i, way, 0).start()
        for shard, out in zip(self.shards, self.outs):
            out[self.ring.me] = shard[...]

    def relay(self, hop):
        for i, way in self.each(hop - 1):
            self.copy(i, way, hop - 1).wait_recv()
            if hop < ring_hops(i, self.ring.size)[way]:
                self.copy(i, way, hop).start()

    def finish(self):
        for hop in range(self.ring.size // 2):
            for i, way in self.each(hop):
                self.copy(i, way, hop).wait_send()


class RingScatter:
    def __init__(self, ring, parts, landing, send, recv):
        self.ring, self.parts, self.landing, self.send, self.recv = ring, parts, landing, send, recv

    def slot(self, i, way, hop):
        return self.landing[i].at[hop + (0 if way == 0 else ring_hops(i, self.ring.size)[0])]

    def owner(self, i, way, hop):
        left = ring_hops(i, self.ring.size)[way] - hop
        return self.ring.at(left if way == 0 else -left)

    def copy(self, i, way, hop):
        source = self.parts[i].at[self.owner(i, way, 0)] if hop == 0 else self.slot(i, way, hop - 1)
        return remote(
            source,
            self.slot(i, way, hop),
            self.send.at[i, way, hop],
            self.recv.at[i, way, hop],
            {"dp": self.ring.targets[way]},
        )

    def each(self, hop):
        for i in range(len(self.parts)):
            for way in (0, 1):
                if hop < ring_hops(i, self.ring.size)[way]:
                    yield i, way

    def start(self):
        for i, way in self.each(0):
            self.copy(i, way, 0).start()

    def relay(self, hop):
        for i, way in self.each(hop - 1):
            self.copy(i, way, hop - 1).wait_recv()
            if hop < ring_hops(i, self.ring.size)[way]:
                slot = self.slot(i, way, hop - 1)
                own = self.parts[i][self.owner(i, way, hop)]
                slot[...] = (slot[...].astype(jnp.float32) + own.astype(jnp.float32)).astype(slot.dtype)
                self.copy(i, way, hop).start()

    def total(self, i):
        up, down = ring_hops(i, self.ring.size)
        return (
            self.parts[i][self.ring.me].astype(jnp.float32)
            + self.slot(i, 0, up - 1)[...].astype(jnp.float32)
            + self.slot(i, 1, down - 1)[...].astype(jnp.float32)
        )

    def finish(self):
        for hop in range(self.ring.size // 2):
            for i, way in self.each(hop):
                self.copy(i, way, hop).wait_send()


def piece_rows(piece, step):
    return pl.ds(piece * step if isinstance(piece, int) else pl.multiple_of(piece * step, step), step)


class RowGather:
    def __init__(self, chip, own, out, send, recv):
        self.chip, self.own, self.out, self.send, self.recv = chip, own, out, send, recv
        self.step = own.shape[0] // ROW_PIECES

    def copy(self, kind, piece):
        rows = piece_rows(piece, self.step)
        chip = self.chip
        owner = chip.peer if kind == 2 else chip.me
        target = self.out.at[owner, rows]
        device = chip.peer if kind == 0 else chip.mate
        return remote(
            target if kind == 2 else self.own.at[rows],
            target,
            self.send.at[kind, piece],
            self.recv.at[kind, piece],
            {"tensor": device},
        )

    def start(self):
        for kind in (0, 1):
            for piece in range(ROW_PIECES):
                self.copy(kind, piece).start()
        self.out[self.chip.me] = self.own[...]

    def relay(self, piece):
        self.copy(0, piece).wait_recv()
        self.copy(2, piece).start()

    def finish(self):
        for kind in (1, 2):
            for piece in range(ROW_PIECES):
                self.copy(kind, piece).wait_recv()
        for kind in (0, 1, 2):
            for piece in range(ROW_PIECES):
                self.copy(kind, piece).wait_send()


class RowScatter:
    def __init__(self, chip, parts, landing, send, recv):
        self.chip, self.parts, self.landing, self.send, self.recv = chip, parts, landing, send, recv
        self.step = parts.shape[1] // ROW_PIECES

    def rows(self, piece):
        return piece_rows(piece, self.step)

    def copy(self, kind, piece):
        chip, rows = self.chip, self.rows(piece)
        source = (
            self.parts.at[chip.across, rows],
            self.landing.at[0, rows],
            self.parts.at[chip.mate, rows],
        )[kind]
        return remote(
            source,
            self.landing.at[kind, rows],
            self.send.at[kind, piece],
            self.recv.at[kind, piece],
            {"tensor": chip.peer if kind == 1 else chip.mate},
        )

    def start(self):
        for kind in (0, 2):
            for piece in range(ROW_PIECES):
                self.copy(kind, piece).start()

    def relay(self, piece):
        rows = self.rows(piece)
        self.copy(0, piece).wait_recv()
        total = self.landing[0, rows].astype(jnp.float32) + self.parts[self.chip.peer, rows].astype(
            jnp.float32
        )
        self.landing[0, rows] = total.astype(self.landing.dtype)
        self.copy(1, piece).start()

    def total(self, piece):
        rows = self.rows(piece)
        self.copy(2, piece).wait_recv()
        self.copy(1, piece).wait_recv()
        return (
            self.parts[self.chip.me, rows].astype(jnp.float32)
            + self.landing[1, rows].astype(jnp.float32)
            + self.landing[2, rows].astype(jnp.float32)
        )

    def finish(self):
        for kind in (0, 1, 2):
            for piece in range(ROW_PIECES):
                self.copy(kind, piece).wait_send()


def row_sems():
    return [pltpu.SemaphoreType.DMA((3, ROW_PIECES))] * 2


def ring_sems(count, size):
    return [pltpu.SemaphoreType.DMA((count, 2, size // 2))] * 2


def comm_params(collective_id):
    return pltpu.CompilerParams(collective_id=collective_id, has_side_effects=True)


def gather_rows(own, collective_id):
    def kernel(own_ref, out_ref, send, recv):
        chip = Chip()
        greet(({"tensor": chip.mate}, {"tensor": chip.peer}))
        rows = RowGather(chip, own_ref, out_ref, send, recv)
        rows.start()
        for piece in range(ROW_PIECES):
            rows.relay(piece)
        rows.finish()

    out = pl.pallas_call(
        kernel,
        out_shape=jax.ShapeDtypeStruct((4, *own.shape), own.dtype),
        in_specs=[VMEM],
        out_specs=VMEM,
        scratch_shapes=row_sems(),
        compiler_params=comm_params(collective_id),
        name="gather_rows",
    )(own)
    return out.reshape(4 * own.shape[0], own.shape[1])


def scatter_rows(parts, collective_id):
    parts = parts.reshape(4, parts.shape[0] // 4, parts.shape[1])

    def kernel(parts_ref, out_ref, landing, send, recv):
        chip = Chip()
        greet(({"tensor": chip.mate}, {"tensor": chip.peer}))
        rows = RowScatter(chip, parts_ref, landing, send, recv)
        rows.start()
        for piece in range(ROW_PIECES):
            rows.relay(piece)
        for piece in range(ROW_PIECES):
            out_ref[rows.rows(piece)] = rows.total(piece)
        rows.finish()

    return pl.pallas_call(
        kernel,
        out_shape=jax.ShapeDtypeStruct(parts.shape[1:], jnp.float32),
        in_specs=[VMEM],
        out_specs=VMEM,
        scratch_shapes=[pltpu.VMEM((3, *parts.shape[1:]), parts.dtype)] + row_sems(),
        compiler_params=comm_params(collective_id),
        name="scatter_rows",
    )(parts)


def gather_all(shards, own, size, collective_id):
    if size > RING_MAX:
        return [lax.all_gather(shard, "dp") for shard in shards], gather_rows(own, collective_id)
    count = len(shards)

    def kernel(*refs):
        shard_refs, own_ref = refs[:count], refs[count]
        out_refs, rows_ref = refs[count + 1 : 2 * count + 1], refs[2 * count + 1]
        ring_send, ring_recv, row_send, row_recv = refs[2 * count + 2 :]
        ring, chip = Ring(size), Chip()
        greet(
            (
                {"dp": ring.targets[0]},
                {"dp": ring.targets[1]},
                {"tensor": chip.mate},
                {"tensor": chip.peer},
            )
        )
        rows = RowGather(chip, own_ref, rows_ref, row_send, row_recv)
        weights = RingGather(ring, shard_refs, out_refs, ring_send, ring_recv)
        rows.start()
        weights.start()
        for hop in range(1, size // 2 + 1):
            for piece in range(ROW_PIECES):
                if piece * (size // 2) // ROW_PIECES == hop - 1:
                    rows.relay(piece)
            weights.relay(hop)
        rows.finish()
        weights.finish()

    *gathered, arrived = pl.pallas_call(
        kernel,
        out_shape=[jax.ShapeDtypeStruct((size, *s.shape), s.dtype) for s in shards]
        + [jax.ShapeDtypeStruct((4, *own.shape), own.dtype)],
        in_specs=[VMEM] * (count + 1),
        out_specs=[VMEM] * (count + 1),
        scratch_shapes=ring_sems(count, size) + row_sems(),
        compiler_params=comm_params(collective_id),
        name="gather_all",
    )(*shards, own)
    return gathered, arrived.reshape(4 * own.shape[0], own.shape[1])


def scatter_all(parts, shared, rows_part, size, collective_id):
    if size > RING_MAX:
        summed = [lax.psum_scatter(p.astype(jnp.float32), "dp", scatter_dimension=0) for p in parts]
        summed[-shared:] = [lax.psum(s, "tensor") for s in summed[-shared:]]
        return summed, scatter_rows(rows_part, collective_id)
    count = len(parts)
    rows_part = rows_part.reshape(4, rows_part.shape[0] // 4, rows_part.shape[1])

    def kernel(*refs):
        part_refs, rows_ref = refs[:count], refs[count]
        out_refs, own_ref = refs[count + 1 : 2 * count + 1], refs[2 * count + 1]
        scratch = refs[2 * count + 2 :]
        landing, row_landing = scratch[:count], scratch[count]
        meets = scratch[count + 1 : count + 1 + shared]
        ring_send, ring_recv, row_send, row_recv, meet_send, meet_recv = scratch[count + 1 + shared :]
        ring, chip = Ring(size), Chip()
        others = (chip.mate, chip.peer, chip.across)
        greet(
            ({"dp": ring.targets[0]}, {"dp": ring.targets[1]})
            + tuple({"tensor": other} for other in others)
        )
        rows = RowScatter(chip, rows_ref, row_landing, row_send, row_recv)
        grads = RingScatter(ring, part_refs, landing, ring_send, ring_recv)
        rows.start()
        grads.start()
        for hop in range(1, size // 2 + 1):
            for piece in range(ROW_PIECES):
                if piece * (size // 2) // ROW_PIECES == hop - 1:
                    rows.relay(piece)
            grads.relay(hop)
        copies = []
        for j in range(shared):
            meets[j][chip.me] = grads.total(count - shared + j)
            for k, other in enumerate(others):
                copy = remote(
                    meets[j].at[chip.me],
                    meets[j].at[chip.me],
                    meet_send.at[j, k],
                    meet_recv.at[j, k],
                    {"tensor": other},
                )
                copy.start()
                copies.append(copy)
        for i in range(count - shared):
            out_refs[i][...] = grads.total(i)
        for piece in range(ROW_PIECES):
            own_ref[rows.rows(piece)] = rows.total(piece)
        for copy in copies:
            copy.wait_recv()
        for j in range(shared):
            out_refs[count - shared + j][...] = (meets[j][0] + meets[j][1]) + (meets[j][2] + meets[j][3])
        rows.finish()
        grads.finish()
        for copy in copies:
            copy.wait_send()

    f32 = jnp.float32
    *summed, own = pl.pallas_call(
        kernel,
        out_shape=[jax.ShapeDtypeStruct(p.shape[1:], f32) for p in parts]
        + [jax.ShapeDtypeStruct(rows_part.shape[1:], f32)],
        in_specs=[VMEM] * (count + 1),
        out_specs=[VMEM] * (count + 1),
        scratch_shapes=[pltpu.VMEM((size - 1, *p.shape[1:]), p.dtype) for p in parts]
        + [pltpu.VMEM((3, *rows_part.shape[1:]), rows_part.dtype)]
        + [pltpu.VMEM((4, *p.shape[1:]), f32) for p in parts[-shared:]]
        + ring_sems(count, size)
        + row_sems()
        + [pltpu.SemaphoreType.DMA((shared, 3))] * 2,
        compiler_params=comm_params(collective_id),
        name="scatter_all",
    )(*parts, rows_part)
    return summed, own


def turned(left, right):
    return lax.dot_general(
        left, right, (((0,), (0,)), ((), ())), preferred_element_type=jnp.float32
    )


def around_rows(chip, gather, scatter, work, keep, middle=None, end=None):
    parts = scatter.parts

    def own(piece, carry):
        rows = scatter.rows(piece)
        keep[rows] = work(chip.me, rows)
        return carry

    def near(piece, carry):
        rows = scatter.rows(piece)
        gather.copy(1, piece).wait_recv()
        parts[chip.mate, rows] = work(chip.mate, rows).astype(parts.dtype)
        scatter.copy(2, piece).start()
        return carry

    def far(piece, carry):
        rows = scatter.rows(piece)
        gather.relay(piece)
        parts[chip.peer, rows] = work(chip.peer, rows).astype(parts.dtype)

        @pl.when(piece > 0)
        def _():
            scatter.relay(piece - 1)

        gather.copy(2, piece).wait_recv()
        parts[chip.across, rows] = work(chip.across, rows).astype(parts.dtype)
        scatter.copy(0, piece).start()
        return carry

    def last(piece, carry):
        rows = scatter.rows(piece)
        scatter.copy(2, piece).wait_recv()
        scatter.copy(1, piece).wait_recv()
        keep[rows] += scatter.landing[1, rows].astype(jnp.float32) + scatter.landing[2, rows].astype(
            jnp.float32
        )
        return carry

    gather.start()
    lax.fori_loop(0, ROW_PIECES, own, 0)
    lax.fori_loop(0, ROW_PIECES, near, 0)
    if middle is not None:
        middle()
    lax.fori_loop(0, ROW_PIECES, far, 0)
    scatter.relay(ROW_PIECES - 1)
    if end is not None:
        end()
    lax.fori_loop(0, ROW_PIECES, last, 0)
    for copies in (gather, scatter):
        for kind in (0, 1, 2):
            for piece in range(ROW_PIECES):
                copies.copy(kind, piece).wait_send()


def feed_forward(own, up_weight, shift, down_weight, collective_id):
    rows, width = own.shape
    hidden_width = up_weight.shape[1]
    low, f32 = jnp.bfloat16, jnp.float32

    def kernel(
        own_ref, up_ref, shift_ref, down_ref, rows_ref, hidden_ref, slope_ref, out_ref, parts, landing, *sems
    ):
        chip = Chip()
        greet(({"tensor": chip.mate}, {"tensor": chip.peer}))
        gather = RowGather(chip, own_ref, rows_ref, *sems[:2])
        scatter = RowScatter(chip, parts, landing, *sems[2:])

        def work(owner, rows):
            pre = jnp.dot(rows_ref[owner, rows], up_ref[...], preferred_element_type=f32) + shift_ref[...]
            cdf = 0.5 * (1.0 + lax.erf(pre * 0.7071067811865476))
            hidden = (pre * cdf).astype(low)
            hidden_ref[owner, rows] = hidden
            slope = cdf + pre * (jnp.exp(-0.5 * pre * pre) * 0.3989422804014327)
            slope_ref[owner, rows] = slope.astype(low)
            return times_transposed(hidden, down_ref[...])

        around_rows(chip, gather, scatter, work, out_ref)

    return pl.pallas_call(
        kernel,
        out_shape=[
            jax.ShapeDtypeStruct((4, rows, width), low),
            jax.ShapeDtypeStruct((4, rows, hidden_width), low),
            jax.ShapeDtypeStruct((4, rows, hidden_width), low),
            jax.ShapeDtypeStruct((rows, width), f32),
        ],
        in_specs=[VMEM] * 4,
        out_specs=[VMEM] * 4,
        scratch_shapes=[pltpu.VMEM((4, rows, width), low), pltpu.VMEM((3, rows, width), low)]
        + row_sems() * 2,
        compiler_params=comm_params(collective_id),
        name="feed_forward",
    )(own, up_weight, shift.reshape(1, -1), down_weight)


def feed_back(own, slope, mid_rows, hidden, up_weight, down_weight, collective_id):
    rows, width = own.shape
    hidden_width = up_weight.shape[1]
    low, f32 = jnp.bfloat16, jnp.float32
    band = 256

    def kernel(
        own_ref,
        slope_ref,
        mid_ref,
        hidden_ref,
        up_ref,
        down_ref,
        out_ref,
        grad_up_ref,
        grad_down_ref,
        shift_ref,
        rows_ref,
        dpre_ref,
        up_sum,
        down_sum,
        parts,
        landing,
        *sems,
    ):
        chip = Chip()
        greet(({"tensor": chip.mate}, {"tensor": chip.peer}))
        gather = RowGather(chip, own_ref, rows_ref, *sems[:2])
        scatter = RowScatter(chip, parts, landing, *sems[2:])
        shift_ref[...] = jnp.zeros_like(shift_ref)

        def work(owner, rows):
            dhidden = jnp.dot(rows_ref[owner, rows], down_ref[...], preferred_element_type=f32)
            dpre = (dhidden * slope_ref[owner, rows].astype(f32)).astype(low)
            dpre_ref[owner, rows] = dpre
            shift_ref[...] += jnp.sum(dpre.astype(f32), axis=0, keepdims=True)
            return times_transposed(dpre, up_ref[...])

        def grads(owners, first):
            def one(tile, carry):
                columns = pl.ds(pl.multiple_of(tile * band, band), band)
                for left, right, total in (
                    (mid_ref, dpre_ref, up_sum),
                    (rows_ref, hidden_ref, down_sum),
                ):
                    term = turned(left[owners[0], :, columns], right[owners[0]])
                    term += turned(left[owners[1], :, columns], right[owners[1]])
                    total[columns] = term if first else total[columns] + term
                return carry

            return lambda: lax.fori_loop(0, width // band, one, 0)

        around_rows(
            chip,
            gather,
            scatter,
            work,
            out_ref,
            grads((chip.me, chip.mate), True),
            grads((chip.peer, chip.across), False),
        )
        grad_up_ref[...] = up_sum[...].astype(low)
        grad_down_ref[...] = down_sum[...].astype(low)

    return pl.pallas_call(
        kernel,
        out_shape=[
            jax.ShapeDtypeStruct((rows, width), f32),
            jax.ShapeDtypeStruct((width, hidden_width), low),
            jax.ShapeDtypeStruct((width, hidden_width), low),
            jax.ShapeDtypeStruct((1, hidden_width), f32),
        ],
        in_specs=[VMEM] * 6,
        out_specs=[VMEM] * 4,
        scratch_shapes=[
            pltpu.VMEM((4, rows, width), low),
            pltpu.VMEM((4, rows, hidden_width), low),
            pltpu.VMEM((width, hidden_width), f32),
            pltpu.VMEM((width, hidden_width), f32),
            pltpu.VMEM((4, rows, width), low),
            pltpu.VMEM((3, rows, width), low),
        ]
        + row_sems() * 2,
        compiler_params=comm_params(collective_id),
        name="feed_back",
    )(own, slope, mid_rows, hidden, up_weight, down_weight)


def enter_slots(slots, arrived, weight, shift):
    group, width = arrived.shape
    block = 256

    def kernel(slots_ref, arrived_ref, weight_ref, shift_ref, rows_ref, out_ref):
        first = pl.program_id(0) * block
        wanted = first + lax.broadcasted_iota(jnp.int32, (block, group), 0)
        pick = jnp.where(slots_ref[...] == wanted, 1.0, 0.0).astype(jnp.bfloat16)
        rows = jnp.dot(pick, arrived_ref[...], preferred_element_type=jnp.float32).astype(jnp.bfloat16)
        rows_ref[...] = rows
        out = jnp.dot(rows, weight_ref[...], preferred_element_type=jnp.float32) + shift_ref[...]
        out_ref[...] = out.astype(jnp.bfloat16)

    return pl.pallas_call(
        kernel,
        grid=(group // block,),
        in_specs=[VMEM] * 4,
        out_specs=[
            pl.BlockSpec((block, width), lambda i: (i, 0)),
            pl.BlockSpec((block, weight.shape[1]), lambda i: (i, 0)),
        ],
        out_shape=[
            jax.ShapeDtypeStruct((group, width), jnp.bfloat16),
            jax.ShapeDtypeStruct((group, weight.shape[1]), jnp.bfloat16),
        ],
        name="enter_slots",
    )(slots.reshape(1, group), arrived, weight, shift.reshape(1, -1))


def leave_slots(slots, rows):
    group, width = rows.shape
    block = 256

    def kernel(slots_ref, rows_ref, out_ref):
        slot = lax.broadcasted_iota(jnp.int32, (block, group), 1)
        pick = jnp.where(slots_ref[...] == slot, 1.0, 0.0).astype(jnp.bfloat16)
        out_ref[...] = jnp.dot(pick, rows_ref[...], preferred_element_type=jnp.float32).astype(
            jnp.bfloat16
        )

    return pl.pallas_call(
        kernel,
        grid=(group // block,),
        in_specs=[pl.BlockSpec((block, 1), lambda i: (i, 0)), VMEM],
        out_specs=pl.BlockSpec((block, width), lambda i: (i, 0)),
        out_shape=jax.ShapeDtypeStruct((group, width), jnp.bfloat16),
        name="leave_slots",
    )(slots.reshape(group, 1), rows)


def body(
    tokens,
    lengths,
    arrival_slots,
    w_qkv,
    w_out,
    w_up,
    w_down,
    w_proj,
    norm_gains,
    biases,
    up_bias,
    cotangent,
):
    tensor_size = lax.axis_size("tensor")
    tensor_pos = lax.axis_index("tensor")
    own_rows = tokens.shape[0]
    group_rows = own_rows * tensor_size
    passages = group_rows // SLOT
    slot_order = arrival_slots[0]
    size = lax.axis_size("dp")
    part_rows, width_local = w_qkv.shape[1:]
    low = jnp.bfloat16
    shards = [
        w_qkv.astype(low).transpose(1, 0, 2).reshape(part_rows, 3 * width_local),
        w_up.astype(low),
        w_out.astype(low).T,
        w_down.astype(low).T,
        w_proj.astype(low),
        jnp.concatenate(
            [norm_gains.astype(low), biases.astype(low), up_bias.astype(low).reshape(-1, part_rows)]
        ),
    ]
    gathered, arrived = gather_all(shards, tokens, size, 0)
    width = size * part_rows
    qkv_weight, up_weight, out_weight, down_weight, proj_weight = (
        g.reshape(width, g.shape[2]) for g in gathered[:5]
    )
    small = gathered[5].astype(jnp.float32)
    side = small[:, :8].transpose(1, 0, 2).reshape(8, width)
    gain_full, bias_full = side[:2], side[2:]
    upbias_full = small[:, 8:].reshape(-1)
    hidden_local = up_weight.shape[1]
    col_start = tensor_pos * width_local
    query_bias = lax.dynamic_slice_in_dim(bias_full[0], col_start, width_local)
    value_bias = lax.dynamic_slice_in_dim(bias_full[1], col_start, width_local)
    qkv_bias = jnp.concatenate([query_bias, jnp.zeros_like(query_bias), value_bias])
    slotted, qkv_all = enter_slots(slot_order, arrived, qkv_weight, qkv_bias)
    row_start = tensor_pos * own_rows
    resid_input = lax.dynamic_slice_in_dim(slotted, row_start, own_rows, 0).astype(jnp.float32)
    positions = row_start + jnp.arange(own_rows, dtype=jnp.int32)
    row_keep = (positions % SLOT < lengths[positions // SLOT]).astype(jnp.float32)
    context, exact, totals = attend(qkv_all, lengths, passages)
    attn_part = scatter_rows(times_transposed(context, out_weight).astype(low), 1)
    first_sum = resid_input + attn_part + bias_full[2]
    first_norm, back_first = jax.vjp(norm_rows, first_sum, gain_full[0], bias_full[3])
    first_low = first_norm.astype(jnp.bfloat16)
    upbias_own = lax.dynamic_slice_in_dim(upbias_full, tensor_pos * hidden_local, hidden_local)
    mid_rows, hidden, slope, ffn_part = feed_forward(first_low, up_weight, upbias_own, down_weight, 2)
    second_sum = first_norm + ffn_part + bias_full[4]
    second_norm, back_second = jax.vjp(norm_rows, second_sum, gain_full[1], bias_full[5])
    second_low = second_norm.astype(jnp.bfloat16)
    projected = jnp.dot(second_low, proj_weight, preferred_element_type=jnp.float32)

    def unit_rows(values):
        return (
            values
            * lax.rsqrt(jnp.sum(values * values, axis=-1, keepdims=True) + EPS_UNIT)
            * row_keep[:, None]
        )

    embeddings, back_unit = jax.vjp(unit_rows, projected)
    (dproj,) = back_unit(cotangent.astype(jnp.float32))
    dproj_low = dproj.astype(jnp.bfloat16)
    grad_proj = contract_rows(second_low, dproj_low)
    dsecond_norm = times_transposed(dproj_low, proj_weight)
    dsecond, grad_gain_two, grad_shift_two = back_second(dsecond_norm)
    dsecond_low = dsecond.astype(jnp.bfloat16)
    dfirst_norm, grad_up, grad_down, dshift = feed_back(
        dsecond_low, slope, mid_rows, hidden, up_weight, down_weight, 4
    )
    grad_upbias = lax.dynamic_update_slice_in_dim(
        jnp.zeros(upbias_full.shape, jnp.float32), dshift[0], tensor_pos * hidden_local, 0
    )
    dfirst, grad_gain_one, grad_shift_one = back_first(dfirst_norm + dsecond)
    dfirst_low = dfirst.astype(jnp.bfloat16)
    dfirst_rows = gather_rows(dfirst_low, 6)
    dcontext = jnp.dot(dfirst_rows, out_weight, preferred_element_type=jnp.float32).astype(low)
    grad_out = contract_rows(dfirst_rows, context)
    dqkv = attend_back(qkv_all, dcontext, exact, totals, lengths, passages)
    grad_qkv = contract_rows(slotted, dqkv)
    column_sums = jnp.sum(dqkv.astype(jnp.float32), axis=0).reshape(3, width_local)
    through = times_transposed(dqkv, qkv_weight)
    own_through = lax.dynamic_slice_in_dim(through, row_start, own_rows, 0) + dfirst
    through = lax.dynamic_update_slice_in_dim(through, own_through, row_start, 0).astype(low)
    leaving = leave_slots(slot_order, through)
    zero_row = jnp.zeros((bias_full.shape[1],), jnp.float32)
    grad_biases = jnp.stack(
        [
            lax.dynamic_update_slice_in_dim(zero_row, column_sums[0], col_start, 0),
            lax.dynamic_update_slice_in_dim(zero_row, column_sums[2], col_start, 0),
            jnp.sum(dfirst, axis=0),
            grad_shift_one,
            jnp.sum(dsecond, axis=0),
            grad_shift_two,
        ]
    )
    grad_gains = jnp.stack([grad_gain_one, grad_gain_two])
    small_grad = jnp.concatenate([grad_gains, grad_biases]).reshape(8, size, part_rows).transpose(1, 0, 2)
    small_grad = jnp.concatenate([small_grad, grad_upbias.reshape(size, -1, part_rows)], axis=1)
    parts = [
        grad.astype(low).reshape(size, part_rows, grad.shape[1])
        for grad in (grad_qkv, grad_up, grad_out, grad_down, grad_proj)
    ]
    summed, grad_tokens = scatter_all([*parts, small_grad], 2, leaving, size, 7)
    sum_qkv, sum_up, sum_out, sum_down, sum_proj, sum_small = summed
    return (
        embeddings,
        grad_tokens,
        sum_qkv.reshape(part_rows, 3, width_local).transpose(1, 0, 2),
        sum_out.T,
        sum_up,
        sum_down.T,
        sum_proj,
        sum_small[:2],
        sum_small[2:8],
        sum_small[8:].reshape(-1),
    )


def solution(mesh):
    return jax.shard_map(
        body,
        mesh=mesh,
        in_specs=(
            P(("dp", "tensor"), None),
            P("dp"),
            P("dp", None),
            P(None, "dp", "tensor"),
            P("tensor", "dp"),
            P("dp", "tensor"),
            P("tensor", "dp"),
            P("dp", None),
            P(None, "dp"),
            P(None, "dp"),
            P("dp"),
            P(("dp", "tensor"), None),
        ),
        out_specs=(
            P(("dp", "tensor"), None),
            P(("dp", "tensor"), None),
            P(None, "dp", "tensor"),
            P("tensor", "dp"),
            P("dp", "tensor"),
            P("tensor", "dp"),
            P("dp", None),
            P(None, "dp"),
            P(None, "dp"),
            P("dp"),
        ),
        check_vma=False,
    )
```

```python
import jax
import jax.numpy as jnp
from jax import lax
from jax.experimental import pallas as pl
from jax.experimental.pallas import tpu as pltpu
from jax.sharding import PartitionSpec as P

HEAD_DIM = 64
SLOT = 2048


EPS_NORM = 1e-06
EPS_UNIT = 1e-06
NEG_FILL = -1e30


def norm_rows(values, gain, shift):
    center = values - jnp.mean(values, axis=-1, keepdims=True)
    spread = jnp.mean(center * center, axis=-1, keepdims=True)
    return center * lax.rsqrt(spread + EPS_NORM) * gain + shift


def contract_rows(left, right):
    return lax.dot_general(
        left, right, (((0,), (0,)), ((), ())), preferred_element_type=jnp.float32
    )


def times_transposed(left, right):
    return lax.dot_general(
        left, right, (((1,), (1,)), ((), ())), preferred_element_type=jnp.float32
    )


MESH = pl.DeviceIdType.MESH
VMEM = pl.BlockSpec(memory_space=pltpu.VMEM)
WIDE = 128


def lane_index(rows):
    return lax.broadcasted_iota(jnp.int32, (rows, WIDE - HEAD_DIM), 1)


def thirds(column):
    parts = []
    for _ in range(3):
        part = column.astype(jnp.bfloat16).astype(jnp.float32)
        parts.append(part)
        column = column - part
    return parts


def beside(rows, columns):
    lane = lane_index(rows)
    out = jnp.zeros(lane.shape, jnp.float32)
    for i, column in enumerate(columns):
        out = jnp.where(lane == i, column, out)
    return out.astype(jnp.bfloat16)


def key_fill(length, keys):
    position = lax.broadcasted_iota(jnp.int32, (keys, 1), 0)
    return jnp.where(position < length, 0.0, NEG_FILL)


def attend(qkv, lengths, passages):
    rows, width = qkv.shape[0], qkv.shape[1] // 3
    keys, heads = rows // passages, width // HEAD_DIM
    block = 512
    steps = keys // block
    factor = HEAD_DIM ** (-0.5)

    def kernel(len_ref, query_ref, kv_ref, out_ref, exact_ref, total_ref, key_side, value_side):
        passage, step = pl.program_id(0), pl.program_id(1)

        @pl.when(step == 0)
        def _():
            fill = key_fill(len_ref[passage], keys)
            for h in range(heads):
                at = width + h * HEAD_DIM
                key_side[h, :, :HEAD_DIM] = kv_ref[:, at : at + HEAD_DIM]
                key_side[h, :, HEAD_DIM:] = beside(keys, [fill])
                value_side[h, :, :HEAD_DIM] = kv_ref[:, at + width : at + width + HEAD_DIM]
                value_side[h, :, HEAD_DIM:] = beside(keys, [1.0])

        ones = beside(block, [1.0])
        totals = jnp.zeros((block, WIDE), jnp.float32)
        lane = lax.broadcasted_iota(jnp.int32, (block, WIDE), 1)
        for h in range(heads):
            query = query_ref[:, h * HEAD_DIM : (h + 1) * HEAD_DIM] * jnp.bfloat16(factor)
            query = jnp.concatenate([query, ones], axis=1)
            scores = lax.dot_general(
                query, key_side[h], (((1,), (1,)), ((), ())), preferred_element_type=jnp.float32
            )
            top = jnp.max(scores, axis=-1, keepdims=True)
            soft = jnp.exp(scores - top).astype(jnp.bfloat16)
            mixed = jnp.dot(soft, value_side[h], preferred_element_type=jnp.float32)
            total = mixed[:, HEAD_DIM : HEAD_DIM + 1]
            result = mixed[:, :HEAD_DIM] / total
            exact_ref[:, h * HEAD_DIM : (h + 1) * HEAD_DIM] = result
            out_ref[:, h * HEAD_DIM : (h + 1) * HEAD_DIM] = result.astype(jnp.bfloat16)
            totals = jnp.where(lane == h, top + jnp.log(total), totals)
        total_ref[...] = totals

    def tile(columns):
        return pl.BlockSpec((block, columns), lambda p, i: (p * steps + i, 0))

    return pl.pallas_call(
        kernel,
        grid=(passages, steps),
        in_specs=[
            pl.BlockSpec(memory_space=pltpu.SMEM),
            tile(3 * width),
            pl.BlockSpec((keys, 3 * width), lambda p, i: (p, 0)),
        ],
        out_specs=[tile(width), tile(width), tile(WIDE)],
        out_shape=[
            jax.ShapeDtypeStruct((rows, width), jnp.bfloat16),
            jax.ShapeDtypeStruct((rows, width), jnp.float32),
            jax.ShapeDtypeStruct((rows, WIDE), jnp.float32),
        ],
        scratch_shapes=[pltpu.VMEM((heads, keys, WIDE), jnp.bfloat16)] * 2,
        name="attend",
    )(lengths, qkv, qkv)


RING_MAX = 8
ROW_PIECES = 4


def ring_place(position, size):
    far = position // (size // 2)
    return 2 * ((1 - far) * position + far * (size - 1 - position)) + far


def ring_position(index, size):
    row, far = index // 2, index % 2
    return (1 - far) * row + far * (size - 1 - row)


def ring_hops(index, size):
    longer, shorter = size // 2, size - 1 - size // 2
    return (longer, shorter) if index % 2 == 0 else (shorter, longer)


class Ring:
    def __init__(self, size):
        self.size = size
        self.me = lax.axis_index("dp")
        self.position = ring_position(self.me, size)
        self.targets = (self.at(1), self.at(-1))

    def at(self, offset):
        return ring_place(lax.rem(self.position + (offset + self.size), self.size), self.size)


class Chip:
    def __init__(self):
        self.me = lax.axis_index("tensor")
        chip, core = self.me // 2, self.me % 2
        self.mate = 2 * chip + (1 - core)
        self.peer = 2 * (1 - chip) + core
        self.across = 2 * (1 - chip) + (1 - core)


def greet(devices):
    barrier = pltpu.get_barrier_semaphore()
    for device in devices:
        pl.semaphore_signal(barrier, inc=1, device_id=device, device_id_type=MESH)
    pl.semaphore_wait(barrier, len(devices))


def remote(source, target, send, recv, device):
    return pltpu.make_async_remote_copy(
        src_ref=source,
        dst_ref=target,
        send_sem=send,
        recv_sem=recv,
        device_id=device,
        device_id_type=MESH,
    )


class RingGather:
    def __init__(self, ring, shards, outs, send, recv):
        self.ring, self.shards, self.outs, self.send, self.recv = ring, shards, outs, send, recv

    def copy(self, i, way, hop):
        owner = self.ring.at(-hop if way == 0 else hop)
        target = self.outs[i].at[owner]
        return remote(
            self.shards[i] if hop == 0 else target,
            target,
            self.send.at[i, way, hop],
            self.recv.at[i, way, hop],
            {"dp": self.ring.targets[way]},
        )

    def each(self, hop):
        for i in range(len(self.shards)):
            for way in (0, 1):
                if hop < ring_hops(i, self.ring.size)[way]:
                    yield i, way

    def start(self):
        for i, way in self.each(0):
            self.copy(i, way, 0).start()
        for shard, out in zip(self.shards, self.outs):
            out[self.ring.me] = shard[...]

    def relay(self, hop):
        for i, way in self.each(hop - 1):
            self.copy(i, way, hop - 1).wait_recv()
            if hop < ring_hops(i, self.ring.size)[way]:
                self.copy(i, way, hop).start()

    def finish(self):
        for hop in range(self.ring.size // 2):
            for i, way in self.each(hop):
                self.copy(i, way, hop).wait_send()


class RingScatter:
    def __init__(self, ring, parts, landing, send, recv):
        self.ring, self.parts, self.landing, self.send, self.recv = ring, parts, landing, send, recv

    def slot(self, i, way, hop):
        return self.landing[i].at[hop + (0 if way == 0 else ring_hops(i, self.ring.size)[0])]

    def owner(self, i, way, hop):
        left = ring_hops(i, self.ring.size)[way] - hop
        return self.ring.at(left if way == 0 else -left)

    def copy(self, i, way, hop):
        source = self.parts[i].at[self.owner(i, way, 0)] if hop == 0 else self.slot(i, way, hop - 1)
        return remote(
            source,
            self.slot(i, way, hop),
            self.send.at[i, way, hop],
            self.recv.at[i, way, hop],
            {"dp": self.ring.targets[way]},
        )

    def each(self, hop):
        for i in range(len(self.parts)):
            for way in (0, 1):
                if hop < ring_hops(i, self.ring.size)[way]:
                    yield i, way

    def start(self):
        for i, way in self.each(0):
            self.copy(i, way, 0).start()

    def relay(self, hop):
        for i, way in self.each(hop - 1):
            self.copy(i, way, hop - 1).wait_recv()
            if hop < ring_hops(i, self.ring.size)[way]:
                slot = self.slot(i, way, hop - 1)
                own = self.parts[i][self.owner(i, way, hop)]
                slot[...] = (slot[...].astype(jnp.float32) + own.astype(jnp.float32)).astype(slot.dtype)
                self.copy(i, way, hop).start()

    def total(self, i):
        up, down = ring_hops(i, self.ring.size)
        return (
            self.parts[i][self.ring.me].astype(jnp.float32)
            + self.slot(i, 0, up - 1)[...].astype(jnp.float32)
            + self.slot(i, 1, down - 1)[...].astype(jnp.float32)
        )

    def finish(self):
        for hop in range(self.ring.size // 2):
            for i, way in self.each(hop):
                self.copy(i, way, hop).wait_send()


def piece_rows(piece, step):
    return pl.ds(piece * step if isinstance(piece, int) else pl.multiple_of(piece * step, step), step)


class RowGather:
    def __init__(self, chip, own, out, send, recv):
        self.chip, self.own, self.out, self.send, self.recv = chip, own, out, send, recv
        self.step = own.shape[0] // ROW_PIECES

    def copy(self, kind, piece):
        rows = piece_rows(piece, self.step)
        chip = self.chip
        owner = chip.peer if kind == 2 else chip.me
        target = self.out.at[owner, rows]
        device = chip.peer if kind == 0 else chip.mate
        return remote(
            target if kind == 2 else self.own.at[rows],
            target,
            self.send.at[kind, piece],
            self.recv.at[kind, piece],
            {"tensor": device},
        )

    def start(self):
        for kind in (0, 1):
            for piece in range(ROW_PIECES):
                self.copy(kind, piece).start()
        self.out[self.chip.me] = self.own[...]

    def relay(self, piece):
        self.copy(0, piece).wait_recv()
        self.copy(2, piece).start()

    def finish(self):
        for kind in (1, 2):
            for piece in range(ROW_PIECES):
                self.copy(kind, piece).wait_recv()
        for kind in (0, 1, 2):
            for piece in range(ROW_PIECES):
                self.copy(kind, piece).wait_send()


class RowScatter:
    def __init__(self, chip, parts, landing, send, recv):
        self.chip, self.parts, self.landing, self.send, self.recv = chip, parts, landing, send, recv
        self.pieces = send.shape[1]
        self.step = parts.shape[1] // self.pieces

    def rows(self, piece):
        return piece_rows(piece, self.step)

    def copy(self, kind, piece):
        chip, rows = self.chip, self.rows(piece)
        source = (
            self.parts.at[chip.across, rows],
            self.landing.at[0, rows],
            self.parts.at[chip.mate, rows],
        )[kind]
        return remote(
            source,
            self.landing.at[kind, rows],
            self.send.at[kind, piece],
            self.recv.at[kind, piece],
            {"tensor": chip.peer if kind == 1 else chip.mate},
        )

    def start(self):
        for kind in (0, 2):
            for piece in range(ROW_PIECES):
                self.copy(kind, piece).start()

    def relay(self, piece):
        rows = self.rows(piece)
        self.copy(0, piece).wait_recv()
        total = self.landing[0, rows].astype(jnp.float32) + self.parts[self.chip.peer, rows].astype(
            jnp.float32
        )
        self.landing[0, rows] = total.astype(self.landing.dtype)
        self.copy(1, piece).start()

    def total(self, piece):
        rows = self.rows(piece)
        self.copy(2, piece).wait_recv()
        self.copy(1, piece).wait_recv()
        return (
            self.parts[self.chip.me, rows].astype(jnp.float32)
            + self.landing[1, rows].astype(jnp.float32)
            + self.landing[2, rows].astype(jnp.float32)
        )

    def finish(self):
        for kind in (0, 1, 2):
            for piece in range(self.pieces):
                self.copy(kind, piece).wait_send()


class Meet:
    def __init__(self, chip, held, send, recv):
        self.chip, self.held, self.send, self.recv = chip, held, send, recv
        self.others = (chip.mate, chip.peer, chip.across)

    def copies(self):
        own = self.held.at[self.chip.me]
        for k, other in enumerate(self.others):
            yield remote(own, own, self.send.at[k], self.recv.at[k], {"tensor": other})

    def start(self, value):
        self.held[self.chip.me] = value
        for copy in self.copies():
            copy.start()

    def total(self):
        for copy in self.copies():
            copy.wait_recv()
        return (self.held[0] + self.held[1]) + (self.held[2] + self.held[3])

    def finish(self):
        for copy in self.copies():
            copy.wait_send()


def meet_sems():
    return [pltpu.SemaphoreType.DMA((3,))] * 2


def row_sems(pieces=ROW_PIECES):
    return [pltpu.SemaphoreType.DMA((3, pieces))] * 2


def ring_sems(count, size):
    return [pltpu.SemaphoreType.DMA((count, 2, size // 2))] * 2


def comm_params(collective_id):
    return pltpu.CompilerParams(collective_id=collective_id, has_side_effects=True)


def gather_rows(own, collective_id):
    def kernel(own_ref, out_ref, send, recv):
        chip = Chip()
        greet(({"tensor": chip.mate}, {"tensor": chip.peer}))
        rows = RowGather(chip, own_ref, out_ref, send, recv)
        rows.start()
        for piece in range(ROW_PIECES):
            rows.relay(piece)
        rows.finish()

    out = pl.pallas_call(
        kernel,
        out_shape=jax.ShapeDtypeStruct((4, *own.shape), own.dtype),
        in_specs=[VMEM],
        out_specs=VMEM,
        scratch_shapes=row_sems(),
        compiler_params=comm_params(collective_id),
        name="gather_rows",
    )(own)
    return out.reshape(4 * own.shape[0], own.shape[1])


def scatter_rows(parts, collective_id):
    parts = parts.reshape(4, parts.shape[0] // 4, parts.shape[1])

    def kernel(parts_ref, out_ref, landing, send, recv):
        chip = Chip()
        greet(({"tensor": chip.mate}, {"tensor": chip.peer}))
        rows = RowScatter(chip, parts_ref, landing, send, recv)
        rows.start()
        for piece in range(ROW_PIECES):
            rows.relay(piece)
        for piece in range(ROW_PIECES):
            out_ref[rows.rows(piece)] = rows.total(piece)
        rows.finish()

    return pl.pallas_call(
        kernel,
        out_shape=jax.ShapeDtypeStruct(parts.shape[1:], jnp.float32),
        in_specs=[VMEM],
        out_specs=VMEM,
        scratch_shapes=[pltpu.VMEM((3, *parts.shape[1:]), parts.dtype)] + row_sems(),
        compiler_params=comm_params(collective_id),
        name="scatter_rows",
    )(parts)


def gather_all(shards, own, size, collective_id):
    if size > RING_MAX:
        return [lax.all_gather(shard, "dp") for shard in shards], gather_rows(own, collective_id)
    count = len(shards)

    def kernel(*refs):
        shard_refs, own_ref = refs[:count], refs[count]
        out_refs, rows_ref = refs[count + 1 : 2 * count + 1], refs[2 * count + 1]
        ring_send, ring_recv, row_send, row_recv = refs[2 * count + 2 :]
        ring, chip = Ring(size), Chip()
        greet(
            (
                {"dp": ring.targets[0]},
                {"dp": ring.targets[1]},
                {"tensor": chip.mate},
                {"tensor": chip.peer},
            )
        )
        rows = RowGather(chip, own_ref, rows_ref, row_send, row_recv)
        weights = RingGather(ring, shard_refs, out_refs, ring_send, ring_recv)
        rows.start()
        weights.start()
        for hop in range(1, size // 2 + 1):
            for piece in range(ROW_PIECES):
                if piece * (size // 2) // ROW_PIECES == hop - 1:
                    rows.relay(piece)
            weights.relay(hop)
        rows.finish()
        weights.finish()

    *gathered, arrived = pl.pallas_call(
        kernel,
        out_shape=[jax.ShapeDtypeStruct((size, *s.shape), s.dtype) for s in shards]
        + [jax.ShapeDtypeStruct((4, *own.shape), own.dtype)],
        in_specs=[VMEM] * (count + 1),
        out_specs=[VMEM] * (count + 1),
        scratch_shapes=ring_sems(count, size) + row_sems(),
        compiler_params=comm_params(collective_id),
        name="gather_all",
    )(*shards, own)
    return gathered, arrived.reshape(4 * own.shape[0], own.shape[1])


def turned(left, right):
    return lax.dot_general(
        left, right, (((0,), (0,)), ((), ())), preferred_element_type=jnp.float32
    )


def around_rows(chip, gather, scatter, work, keep, middle=None, end=None):
    parts = scatter.parts

    def own(piece, carry):
        rows = scatter.rows(piece)
        keep[rows] = work(chip.me, rows)
        return carry

    def near(piece, carry):
        rows = scatter.rows(piece)
        gather.copy(1, piece).wait_recv()
        parts[chip.mate, rows] = work(chip.mate, rows).astype(parts.dtype)
        scatter.copy(2, piece).start()
        return carry

    def far(piece, carry):
        rows = scatter.rows(piece)
        gather.relay(piece)
        parts[chip.peer, rows] = work(chip.peer, rows).astype(parts.dtype)

        @pl.when(piece > 0)
        def _():
            scatter.relay(piece - 1)

        gather.copy(2, piece).wait_recv()
        parts[chip.across, rows] = work(chip.across, rows).astype(parts.dtype)
        scatter.copy(0, piece).start()
        return carry

    def last(piece, carry):
        rows = scatter.rows(piece)
        scatter.copy(2, piece).wait_recv()
        scatter.copy(1, piece).wait_recv()
        keep[rows] += scatter.landing[1, rows].astype(jnp.float32) + scatter.landing[2, rows].astype(
            jnp.float32
        )
        return carry

    gather.start()
    lax.fori_loop(0, ROW_PIECES, own, 0)
    lax.fori_loop(0, ROW_PIECES, near, 0)
    if middle is not None:
        middle()
    lax.fori_loop(0, ROW_PIECES, far, 0)
    scatter.relay(ROW_PIECES - 1)
    if end is not None:
        end()
    lax.fori_loop(0, ROW_PIECES, last, 0)
    for copies in (gather, scatter):
        for kind in (0, 1, 2):
            for piece in range(ROW_PIECES):
                copies.copy(kind, piece).wait_send()


def feed_forward(own, up_weight, shift, down_weight, collective_id):
    rows, width = own.shape
    hidden_width = up_weight.shape[1]
    low, f32 = jnp.bfloat16, jnp.float32

    def kernel(
        own_ref, up_ref, shift_ref, down_ref, rows_ref, hidden_ref, slope_ref, out_ref, parts, landing, *sems
    ):
        chip = Chip()
        greet(({"tensor": chip.mate}, {"tensor": chip.peer}))
        gather = RowGather(chip, own_ref, rows_ref, *sems[:2])
        scatter = RowScatter(chip, parts, landing, *sems[2:])

        def work(owner, rows):
            pre = jnp.dot(rows_ref[owner, rows], up_ref[...], preferred_element_type=f32) + shift_ref[...]
            cdf = 0.5 * (1.0 + lax.erf(pre * 0.7071067811865476))
            hidden = (pre * cdf).astype(low)
            hidden_ref[owner, rows] = hidden
            slope = cdf + pre * (jnp.exp(-0.5 * pre * pre) * 0.3989422804014327)
            slope_ref[owner, rows] = slope.astype(low)
            return times_transposed(hidden, down_ref[...])

        around_rows(chip, gather, scatter, work, out_ref)

    return pl.pallas_call(
        kernel,
        out_shape=[
            jax.ShapeDtypeStruct((4, rows, width), low),
            jax.ShapeDtypeStruct((4, rows, hidden_width), low),
            jax.ShapeDtypeStruct((4, rows, hidden_width), low),
            jax.ShapeDtypeStruct((rows, width), f32),
        ],
        in_specs=[VMEM] * 4,
        out_specs=[VMEM] * 4,
        scratch_shapes=[pltpu.VMEM((4, rows, width), low), pltpu.VMEM((3, rows, width), low)]
        + row_sems() * 2,
        compiler_params=comm_params(collective_id),
        name="feed_forward",
    )(own, up_weight, shift.reshape(1, -1), down_weight)


def feed_back(own, slope, mid_rows, hidden, up_weight, down_weight, collective_id):
    rows, width = own.shape
    hidden_width = up_weight.shape[1]
    low, f32 = jnp.bfloat16, jnp.float32
    band = 256

    def kernel(
        own_ref,
        slope_ref,
        mid_ref,
        hidden_ref,
        up_ref,
        down_ref,
        out_ref,
        grad_up_ref,
        grad_down_ref,
        shift_ref,
        rows_ref,
        dpre_ref,
        up_sum,
        down_sum,
        parts,
        landing,
        *sems,
    ):
        chip = Chip()
        greet(({"tensor": chip.mate}, {"tensor": chip.peer}))
        gather = RowGather(chip, own_ref, rows_ref, *sems[:2])
        scatter = RowScatter(chip, parts, landing, *sems[2:])
        shift_ref[...] = jnp.zeros_like(shift_ref)

        def work(owner, rows):
            dhidden = jnp.dot(rows_ref[owner, rows], down_ref[...], preferred_element_type=f32)
            dpre = (dhidden * slope_ref[owner, rows].astype(f32)).astype(low)
            dpre_ref[owner, rows] = dpre
            shift_ref[...] += jnp.sum(dpre.astype(f32), axis=0, keepdims=True)
            return times_transposed(dpre, up_ref[...])

        def grads(owners, first):
            def one(tile, carry):
                columns = pl.ds(pl.multiple_of(tile * band, band), band)
                for left, right, total in (
                    (mid_ref, dpre_ref, up_sum),
                    (rows_ref, hidden_ref, down_sum),
                ):
                    term = turned(left[owners[0], :, columns], right[owners[0]])
                    term += turned(left[owners[1], :, columns], right[owners[1]])
                    total[columns] = term if first else total[columns] + term
                return carry

            return lambda: lax.fori_loop(0, width // band, one, 0)

        around_rows(
            chip,
            gather,
            scatter,
            work,
            out_ref,
            grads((chip.me, chip.mate), True),
            grads((chip.peer, chip.across), False),
        )
        grad_up_ref[...] = up_sum[...].astype(low)
        grad_down_ref[...] = down_sum[...].astype(low)

    return pl.pallas_call(
        kernel,
        out_shape=[
            jax.ShapeDtypeStruct((rows, width), f32),
            jax.ShapeDtypeStruct((width, hidden_width), low),
            jax.ShapeDtypeStruct((width, hidden_width), low),
            jax.ShapeDtypeStruct((1, hidden_width), f32),
        ],
        in_specs=[VMEM] * 6,
        out_specs=[VMEM] * 4,
        scratch_shapes=[
            pltpu.VMEM((4, rows, width), low),
            pltpu.VMEM((4, rows, hidden_width), low),
            pltpu.VMEM((width, hidden_width), f32),
            pltpu.VMEM((width, hidden_width), f32),
            pltpu.VMEM((4, rows, width), low),
            pltpu.VMEM((3, rows, width), low),
        ]
        + row_sems() * 2,
        compiler_params=comm_params(collective_id),
        name="feed_back",
    )(own, slope, mid_rows, hidden, up_weight, down_weight)


def enter_slots(slots, arrived, weight, shift):
    group, width = arrived.shape
    block = 256

    def kernel(slots_ref, arrived_ref, weight_ref, shift_ref, rows_ref, out_ref):
        first = pl.program_id(0) * block
        wanted = first + lax.broadcasted_iota(jnp.int32, (block, group), 0)
        pick = jnp.where(slots_ref[...] == wanted, 1.0, 0.0).astype(jnp.bfloat16)
        rows = jnp.dot(pick, arrived_ref[...], preferred_element_type=jnp.float32).astype(jnp.bfloat16)
        rows_ref[...] = rows
        out = jnp.dot(rows, weight_ref[...], preferred_element_type=jnp.float32) + shift_ref[...]
        out_ref[...] = out.astype(jnp.bfloat16)

    return pl.pallas_call(
        kernel,
        grid=(group // block,),
        in_specs=[VMEM] * 4,
        out_specs=[
            pl.BlockSpec((block, width), lambda i: (i, 0)),
            pl.BlockSpec((block, weight.shape[1]), lambda i: (i, 0)),
        ],
        out_shape=[
            jax.ShapeDtypeStruct((group, width), jnp.bfloat16),
            jax.ShapeDtypeStruct((group, weight.shape[1]), jnp.bfloat16),
        ],
        name="enter_slots",
    )(slots.reshape(1, group), arrived, weight, shift.reshape(1, -1))


def attend_back(own, out_weight, context, qkv, exact, totals, lengths, parts, size, collective_id):
    ringed = size <= RING_MAX
    given = parts if ringed else []
    count = len(given)
    block, model = own.shape
    keys, width = qkv.shape[0], qkv.shape[1] // 3
    heads = width // HEAD_DIM
    factor = HEAD_DIM ** (-0.5)
    low, f32 = jnp.bfloat16, jnp.float32

    def kernel(*refs):
        len_ref, own_ref, weight_ref, context_ref, qkv_ref, exact_ref, total_ref = refs[:7]
        part_refs, refs = refs[7 : 7 + count], refs[7 + count :]
        out_ref, column_ref, grad_ref = refs[:3]
        sum_refs, refs = refs[3 : 3 + count], refs[3 + count :]
        rows_ref, key_side, value_side, key_turned, sums, grad_sum, row_send, row_recv = refs[:8]
        refs = refs[8:]
        chip = Chip()
        neighbours = ({"tensor": chip.mate}, {"tensor": chip.peer})
        if ringed:
            landing, (held, ring_send, ring_recv, meet_send, meet_recv) = refs[:count], refs[count:]
            ring = Ring(size)
            meet = Meet(chip, held, meet_send, meet_recv)
            grads = RingScatter(ring, part_refs, landing, ring_send, ring_recv)
            neighbours += ({"tensor": chip.across},)
            neighbours += ({"dp": ring.targets[0]}, {"dp": ring.targets[1]})
        greet(neighbours)
        rows = RowGather(chip, own_ref, rows_ref, row_send, row_recv)
        rows.start()
        if ringed:
            grads.start()
        fill = key_fill(len_ref[0], keys)
        for h in range(heads):
            at = width + h * HEAD_DIM
            key = qkv_ref[:, at : at + HEAD_DIM]
            key_side[h, :, :HEAD_DIM] = key
            key_side[h, :, HEAD_DIM:] = beside(keys, [fill, 1.0, 1.0, 1.0])
            key_turned[h] = (key * low(factor)).T
            value_side[h, :, :HEAD_DIM] = qkv_ref[:, at + width : at + width + HEAD_DIM]
            value_side[h, :, HEAD_DIM:] = beside(keys, [1.0, 1.0, 1.0])
        sums[...] = jnp.zeros_like(sums)
        grad_sum[...] = jnp.zeros_like(grad_sum)

        def one(step, carry):
            owner = 2 * lax.rem(chip.me // 2 + step // 2, 2) + lax.rem(lax.rem(chip.me, 2) + step, 2)

            @pl.when(step == 1)
            def _():
                for piece in range(ROW_PIECES):
                    rows.copy(1, piece).wait_recv()

            @pl.when(step == 3)
            def _():
                for piece in range(ROW_PIECES):
                    rows.copy(2, piece).wait_recv()

            first = pl.multiple_of(owner * block, block)
            here = pl.ds(first, block)
            drows = rows_ref[owner]
            dcontext = jnp.dot(drows, weight_ref[...], preferred_element_type=f32).astype(low)
            grad_sum[...] += turned(drows, context_ref[here])
            blank = jnp.zeros((block, HEAD_DIM), low)
            for h in range(heads):
                lanes = slice(h * HEAD_DIM, (h + 1) * HEAD_DIM)
                dout = dcontext[:, lanes]
                delta = jnp.sum(dout.astype(f32) * exact_ref[here, lanes], axis=-1, keepdims=True)
                query = qkv_ref[here, lanes] * low(factor)
                query_wide = jnp.concatenate(
                    [query, beside(block, [1.0, *thirds(-total_ref[here, h : h + 1])])], axis=1
                )
                dout_wide = jnp.concatenate([dout, beside(block, thirds(-delta))], axis=1)
                soft = jnp.exp(times_transposed(key_side[h], query_wide))
                dsoft = times_transposed(value_side[h], dout_wide)
                dscore = (soft * dsoft).astype(low)
                soft = soft.astype(low)
                sums[h] += jnp.dot(
                    soft, jnp.concatenate([dout, blank], axis=1), preferred_element_type=f32
                ) + jnp.dot(
                    dscore, jnp.concatenate([blank, query], axis=1), preferred_element_type=f32
                )
                dquery = jnp.dot(key_turned[h], dscore, preferred_element_type=f32)
                out_ref[here, lanes] = dquery.T.astype(low)
                if ringed and h == 0:

                    @pl.when(step == 3)
                    def _():
                        grads.relay(size // 2)
                        meet.start(grads.total(count - 1))

                if ringed and h == heads - 1:
                    for hop in range(1, size // 2):

                        @pl.when(step == hop - 1)
                        def _():
                            grads.relay(hop)

            @pl.when(step < 2)
            def _():
                rows.relay(2 * step)
                rows.relay(2 * step + 1)

            return carry

        lax.fori_loop(0, 4, one, 0)
        for h in range(heads):
            both = sums[h].astype(low)
            at = width + h * HEAD_DIM
            out_ref[:, at : at + HEAD_DIM] = both[:, HEAD_DIM:]
            out_ref[:, at + width : at + width + HEAD_DIM] = both[:, :HEAD_DIM]
        column_ref[...] = jnp.sum(out_ref[...].astype(f32), axis=0, keepdims=True)
        grad_ref[...] = grad_sum[...].astype(low)
        for i in range(count - 1):
            sum_refs[i][...] = grads.total(i)
        if ringed:
            sum_refs[count - 1][...] = meet.total()
            meet.finish()
            grads.finish()
        for kind in (0, 1, 2):
            for piece in range(ROW_PIECES):
                rows.copy(kind, piece).wait_send()

    scratch = [
        pltpu.VMEM((4, block, model), low),
        pltpu.VMEM((heads, keys, WIDE), low),
        pltpu.VMEM((heads, keys, WIDE), low),
        pltpu.VMEM((heads, HEAD_DIM, keys), low),
        pltpu.VMEM((heads, keys, WIDE), f32),
        pltpu.VMEM((model, width), f32),
        *row_sems(),
    ]
    if ringed:
        scratch += [pltpu.VMEM((size - 1, *p.shape[1:]), p.dtype) for p in parts]
        scratch += [pltpu.VMEM((4, *parts[-1].shape[1:]), f32)]
        scratch += ring_sems(count, size) + meet_sems()
    dqkv, columns, grad_out, *summed = pl.pallas_call(
        kernel,
        out_shape=[
            jax.ShapeDtypeStruct((keys, 3 * width), low),
            jax.ShapeDtypeStruct((1, 3 * width), f32),
            jax.ShapeDtypeStruct((model, width), low),
        ]
        + [jax.ShapeDtypeStruct(p.shape[1:], f32) for p in given],
        in_specs=[pl.BlockSpec(memory_space=pltpu.SMEM)] + [VMEM] * (6 + count),
        out_specs=[VMEM] * (3 + count),
        scratch_shapes=scratch,
        compiler_params=comm_params(collective_id),
        name="attend_back",
    )(lengths, own, out_weight, context, qkv, exact, totals, *given)
    if not ringed:
        summed = [lax.psum_scatter(p.astype(f32), "dp", scatter_dimension=0) for p in parts]
        summed[-1] = lax.psum(summed[-1], "tensor")
    return dqkv, columns[0], grad_out, summed


def finish(rows, dqkv, weight, resid, slots, parts, size, collective_id):
    ringed = size <= RING_MAX
    given = parts if ringed else []
    count = len(given) + 1
    group, model = rows.shape
    columns = dqkv.shape[1]
    own_rows = group // 4
    pieces, band = 2, model // 2
    low, f32 = jnp.bfloat16, jnp.float32

    def kernel(*refs):
        rows_ref, dqkv_ref, weight_ref, resid_ref, slots_ref = refs[:5]
        part_refs, refs = refs[5 : 4 + count], refs[4 + count :]
        own_ref, grad_ref, *sum_refs = refs[: 1 + count]
        through, leaving, row_landing, row_send, row_recv, *refs = refs[1 + count :]
        chip = Chip()
        neighbours = ({"tensor": chip.mate}, {"tensor": chip.peer})
        if ringed:
            local, landing, (held, ring_send, ring_recv, meet_send, meet_recv) = (
                refs[0],
                refs[1 : 1 + count],
                refs[1 + count :],
            )
            ring = Ring(size)
            meet = Meet(chip, held, meet_send, meet_recv)
            grads = RingScatter(ring, (*part_refs, local), landing, ring_send, ring_recv)
            neighbours += ({"tensor": chip.across},)
            neighbours += ({"dp": ring.targets[0]}, {"dp": ring.targets[1]})
        greet(neighbours)
        scatter = RowScatter(chip, leaving, row_landing, row_send, row_recv)
        half = group // 2

        def spread(part, carry):
            here = pl.ds(pl.multiple_of(part * half, half), half)
            through[here] = times_transposed(dqkv_ref[here], weight_ref[...]).astype(low)
            return carry

        lax.fori_loop(0, 2, spread, 0)
        mine = pl.ds(pl.multiple_of(chip.me * own_rows, own_rows), own_rows)
        through[mine] = (
            times_transposed(dqkv_ref[mine], weight_ref[...]) + resid_ref[...]
        ).astype(low)
        step = own_rows // pieces
        slot = lax.broadcasted_iota(jnp.int32, (step, group), 1)

        def leave(owner, piece):
            first = pl.multiple_of(owner * own_rows + piece * step, step)
            pick = jnp.where(slots_ref[pl.ds(first, step)] == slot, 1.0, 0.0).astype(low)
            moved = jnp.dot(pick, through[...], preferred_element_type=f32).astype(low)
            leaving[owner, scatter.rows(piece)] = moved

        def outward(piece, carry):
            leave(chip.across, piece)
            scatter.copy(0, piece).start()
            leave(chip.peer, piece)
            scatter.relay(piece)
            return carry

        def inward(piece, carry):
            leave(chip.mate, piece)
            scatter.copy(2, piece).start()
            leave(chip.me, piece)
            return carry

        lax.fori_loop(0, 1, outward, 0)
        for tile in range(2):
            grad = turned(rows_ref[:, tile * band : (tile + 1) * band], dqkv_ref[...]).astype(low)
            if ringed:
                half_ring = size // 2
                local[tile * half_ring : (tile + 1) * half_ring] = grad.reshape(
                    half_ring, band // half_ring, columns
                )
            else:
                grad_ref[tile * band : (tile + 1) * band] = grad
        if ringed:
            grads.start()
        lax.fori_loop(1, pieces, outward, 0)
        if ringed:
            grads.relay(1)
        lax.fori_loop(0, pieces, inward, 0)
        if ringed:
            for hop in range(2, size // 2 + 1):
                grads.relay(hop)
            meet.start(grads.total(count - 2))
        for piece in range(pieces):
            own_ref[scatter.rows(piece)] = scatter.total(piece)
        if ringed:
            grad_ref[...] = grads.total(count - 1)
            for i in range(count - 2):
                sum_refs[i][...] = grads.total(i)
            sum_refs[count - 2][...] = meet.total()
            meet.finish()
            grads.finish()
        scatter.finish()

    scratch = [
        pltpu.VMEM((group, model), low),
        pltpu.VMEM((4, own_rows, model), low),
        pltpu.VMEM((3, own_rows, model), low),
        *row_sems(pieces),
    ]
    if ringed:
        local = jax.ShapeDtypeStruct((size, model // size, columns), low)
        scratch += [pltpu.VMEM(local.shape, low)]
        scratch += [pltpu.VMEM((size - 1, *p.shape[1:]), p.dtype) for p in (*parts, local)]
        scratch += [pltpu.VMEM((4, *parts[-1].shape[1:]), f32)]
        scratch += ring_sems(count, size) + meet_sems()
        first = jax.ShapeDtypeStruct(local.shape[1:], f32)
    else:
        first = jax.ShapeDtypeStruct((model, columns), low)
    own, grad, *summed = pl.pallas_call(
        kernel,
        out_shape=[jax.ShapeDtypeStruct((own_rows, model), f32), first]
        + [jax.ShapeDtypeStruct(p.shape[1:], f32) for p in given],
        in_specs=[VMEM] * (4 + count),
        out_specs=[VMEM] * (1 + count),
        scratch_shapes=scratch,
        compiler_params=comm_params(collective_id),
        name="finish",
    )(rows, dqkv, weight, resid, slots.reshape(group, 1), *given)
    if not ringed:
        grad = grad.astype(f32).reshape(size, model // size, columns)
        grad, *summed = [lax.psum_scatter(p.astype(f32), "dp", scatter_dimension=0) for p in (grad, *parts)]
        summed[-1] = lax.psum(summed[-1], "tensor")
    return own, grad, summed


def body(
    tokens,
    lengths,
    arrival_slots,
    w_qkv,
    w_out,
    w_up,
    w_down,
    w_proj,
    norm_gains,
    biases,
    up_bias,
    cotangent,
):
    tensor_size = lax.axis_size("tensor")
    tensor_pos = lax.axis_index("tensor")
    own_rows = tokens.shape[0]
    group_rows = own_rows * tensor_size
    passages = group_rows // SLOT
    slot_order = arrival_slots[0]
    size = lax.axis_size("dp")
    part_rows, width_local = w_qkv.shape[1:]
    low = jnp.bfloat16
    shards = [
        w_qkv.astype(low).transpose(1, 0, 2).reshape(part_rows, 3 * width_local),
        w_up.astype(low),
        w_out.astype(low).T,
        w_down.astype(low).T,
        w_proj.astype(low),
        jnp.concatenate(
            [norm_gains.astype(low), biases.astype(low), up_bias.astype(low).reshape(-1, part_rows)]
        ),
    ]
    gathered, arrived = gather_all(shards, tokens, size, 0)
    width = size * part_rows
    qkv_weight, up_weight, out_weight, down_weight, proj_weight = (
        g.reshape(width, g.shape[2]) for g in gathered[:5]
    )
    small = gathered[5].astype(jnp.float32)
    side = small[:, :8].transpose(1, 0, 2).reshape(8, width)
    gain_full, bias_full = side[:2], side[2:]
    upbias_full = small[:, 8:].reshape(-1)
    hidden_local = up_weight.shape[1]
    col_start = tensor_pos * width_local
    query_bias = lax.dynamic_slice_in_dim(bias_full[0], col_start, width_local)
    value_bias = lax.dynamic_slice_in_dim(bias_full[1], col_start, width_local)
    qkv_bias = jnp.concatenate([query_bias, jnp.zeros_like(query_bias), value_bias])
    slotted, qkv_all = enter_slots(slot_order, arrived, qkv_weight, qkv_bias)
    row_start = tensor_pos * own_rows
    resid_input = lax.dynamic_slice_in_dim(slotted, row_start, own_rows, 0).astype(jnp.float32)
    positions = row_start + jnp.arange(own_rows, dtype=jnp.int32)
    row_keep = (positions % SLOT < lengths[positions // SLOT]).astype(jnp.float32)
    context, exact, totals = attend(qkv_all, lengths, passages)
    attn_part = scatter_rows(times_transposed(context, out_weight).astype(low), 1)
    first_sum = resid_input + attn_part + bias_full[2]
    first_norm, back_first = jax.vjp(norm_rows, first_sum, gain_full[0], bias_full[3])
    first_low = first_norm.astype(jnp.bfloat16)
    upbias_own = lax.dynamic_slice_in_dim(upbias_full, tensor_pos * hidden_local, hidden_local)
    mid_rows, hidden, slope, ffn_part = feed_forward(first_low, up_weight, upbias_own, down_weight, 2)
    second_sum = first_norm + ffn_part + bias_full[4]
    second_norm, back_second = jax.vjp(norm_rows, second_sum, gain_full[1], bias_full[5])
    second_low = second_norm.astype(jnp.bfloat16)
    projected = jnp.dot(second_low, proj_weight, preferred_element_type=jnp.float32)

    def unit_rows(values):
        return (
            values
            * lax.rsqrt(jnp.sum(values * values, axis=-1, keepdims=True) + EPS_UNIT)
            * row_keep[:, None]
        )

    embeddings, back_unit = jax.vjp(unit_rows, projected)
    (dproj,) = back_unit(cotangent.astype(jnp.float32))
    dproj_low = dproj.astype(jnp.bfloat16)
    grad_proj = contract_rows(second_low, dproj_low)
    dsecond_norm = times_transposed(dproj_low, proj_weight)
    dsecond, grad_gain_two, grad_shift_two = back_second(dsecond_norm)
    dsecond_low = dsecond.astype(jnp.bfloat16)
    dfirst_norm, grad_up, grad_down, dshift = feed_back(
        dsecond_low, slope, mid_rows, hidden, up_weight, down_weight, 4
    )
    grad_upbias = lax.dynamic_update_slice_in_dim(
        jnp.zeros(upbias_full.shape, jnp.float32), dshift[0], tensor_pos * hidden_local, 0
    )
    dfirst, grad_gain_one, grad_shift_one = back_first(dfirst_norm + dsecond)
    dfirst_low = dfirst.astype(jnp.bfloat16)
    cut = lambda grad: grad.astype(low).reshape(size, part_rows, grad.shape[1])
    dqkv, column_sums, grad_out, (sum_up, sum_down, sum_proj) = attend_back(
        dfirst_low,
        out_weight,
        context,
        qkv_all,
        exact,
        totals,
        lengths,
        [cut(grad_up), cut(grad_down), cut(grad_proj)],
        size,
        6,
    )
    column_sums = column_sums.reshape(3, width_local)
    zero_row = jnp.zeros((bias_full.shape[1],), jnp.float32)
    grad_biases = jnp.stack(
        [
            lax.dynamic_update_slice_in_dim(zero_row, column_sums[0], col_start, 0),
            lax.dynamic_update_slice_in_dim(zero_row, column_sums[2], col_start, 0),
            jnp.sum(dfirst, axis=0),
            grad_shift_one,
            jnp.sum(dsecond, axis=0),
            grad_shift_two,
        ]
    )
    grad_gains = jnp.stack([grad_gain_one, grad_gain_two])
    small_grad = jnp.concatenate([grad_gains, grad_biases]).reshape(8, size, part_rows).transpose(1, 0, 2)
    small_grad = jnp.concatenate([small_grad, grad_upbias.reshape(size, -1, part_rows)], axis=1)
    grad_tokens, sum_qkv, (sum_out, sum_small) = finish(
        slotted, dqkv, qkv_weight, dfirst, slot_order, [cut(grad_out), small_grad], size, 7
    )
    return (
        embeddings,
        grad_tokens,
        sum_qkv.reshape(part_rows, 3, width_local).transpose(1, 0, 2),
        sum_out.T,
        sum_up,
        sum_down.T,
        sum_proj,
        sum_small[:2],
        sum_small[2:8],
        sum_small[8:].reshape(-1),
    )


def solution(mesh):
    return jax.shard_map(
        body,
        mesh=mesh,
        in_specs=(
            P(("dp", "tensor"), None),
            P("dp"),
            P("dp", None),
            P(None, "dp", "tensor"),
            P("tensor", "dp"),
            P("dp", "tensor"),
            P("tensor", "dp"),
            P("dp", None),
            P(None, "dp"),
            P(None, "dp"),
            P("dp"),
            P(("dp", "tensor"), None),
        ),
        out_specs=(
            P(("dp", "tensor"), None),
            P(("dp", "tensor"), None),
            P(None, "dp", "tensor"),
            P("tensor", "dp"),
            P("dp", "tensor"),
            P("tensor", "dp"),
            P("dp", None),
            P(None, "dp"),
            P(None, "dp"),
            P("dp"),
        ),
        check_vma=False,
    )
```

```python
import jax
import jax.numpy as jnp
from jax import lax
from jax.experimental import pallas as pl
from jax.experimental.pallas import tpu as pltpu
from jax.sharding import PartitionSpec as P

HEAD_DIM = 64
SLOT = 2048


EPS_NORM = 1e-06
EPS_UNIT = 1e-06
NEG_FILL = -1e30


def norm_rows(values, gain, shift):
    center = values - jnp.mean(values, axis=-1, keepdims=True)
    spread = jnp.mean(center * center, axis=-1, keepdims=True)
    return center * lax.rsqrt(spread + EPS_NORM) * gain + shift


def contract_rows(left, right):
    return lax.dot_general(
        left, right, (((0,), (0,)), ((), ())), preferred_element_type=jnp.float32
    )


def times_transposed(left, right):
    return lax.dot_general(
        left, right, (((1,), (1,)), ((), ())), preferred_element_type=jnp.float32
    )


MESH = pl.DeviceIdType.MESH
VMEM = pl.BlockSpec(memory_space=pltpu.VMEM)
WIDE = 128


def lane_index(rows):
    return lax.broadcasted_iota(jnp.int32, (rows, WIDE - HEAD_DIM), 1)


def thirds(column):
    parts = []
    for _ in range(3):
        part = column.astype(jnp.bfloat16).astype(jnp.float32)
        parts.append(part)
        column = column - part
    return parts


def beside(rows, columns):
    lane = lane_index(rows)
    out = jnp.zeros(lane.shape, jnp.float32)
    for i, column in enumerate(columns):
        out = jnp.where(lane == i, column, out)
    return out.astype(jnp.bfloat16)


def key_fill(length, keys):
    position = lax.broadcasted_iota(jnp.int32, (keys, 1), 0)
    return jnp.where(position < length, 0.0, NEG_FILL)


RING_MAX = 8
ROW_PIECES = 4


def ring_place(position, size):
    far = position // (size // 2)
    return 2 * ((1 - far) * position + far * (size - 1 - position)) + far


def ring_position(index, size):
    row, far = index // 2, index % 2
    return (1 - far) * row + far * (size - 1 - row)


def ring_hops(index, size):
    longer, shorter = size // 2, size - 1 - size // 2
    return (longer, shorter) if index % 2 == 0 else (shorter, longer)


class Ring:
    def __init__(self, size):
        self.size = size
        self.me = lax.axis_index("dp")
        self.position = ring_position(self.me, size)
        self.targets = (self.at(1), self.at(-1))

    def at(self, offset):
        return ring_place(lax.rem(self.position + (offset + self.size), self.size), self.size)


class Chip:
    def __init__(self):
        self.me = lax.axis_index("tensor")
        chip, core = self.me // 2, self.me % 2
        self.mate = 2 * chip + (1 - core)
        self.peer = 2 * (1 - chip) + core
        self.across = 2 * (1 - chip) + (1 - core)


def greet(devices):
    barrier = pltpu.get_barrier_semaphore()
    for device in devices:
        pl.semaphore_signal(barrier, inc=1, device_id=device, device_id_type=MESH)
    pl.semaphore_wait(barrier, len(devices))


def remote(source, target, send, recv, device):
    return pltpu.make_async_remote_copy(
        src_ref=source,
        dst_ref=target,
        send_sem=send,
        recv_sem=recv,
        device_id=device,
        device_id_type=MESH,
    )


class RingGather:
    def __init__(self, ring, shards, outs, send, recv):
        self.ring, self.shards, self.outs, self.send, self.recv = ring, shards, outs, send, recv

    def copy(self, i, way, hop):
        owner = self.ring.at(-hop if way == 0 else hop)
        target = self.outs[i].at[owner]
        return remote(
            self.shards[i] if hop == 0 else target,
            target,
            self.send.at[i, way, hop],
            self.recv.at[i, way, hop],
            {"dp": self.ring.targets[way]},
        )

    def each(self, hop):
        for i in range(len(self.shards)):
            for way in (0, 1):
                if hop < ring_hops(i, self.ring.size)[way]:
                    yield i, way

    def start(self):
        for i, way in self.each(0):
            self.copy(i, way, 0).start()
        for shard, out in zip(self.shards, self.outs):
            out[self.ring.me] = shard[...]

    def relay(self, hop):
        for i, way in self.each(hop - 1):
            self.copy(i, way, hop - 1).wait_recv()
            if hop < ring_hops(i, self.ring.size)[way]:
                self.copy(i, way, hop).start()

    def finish(self):
        for hop in range(self.ring.size // 2):
            for i, way in self.each(hop):
                self.copy(i, way, hop).wait_send()


class RingScatter:
    def __init__(self, ring, parts, landing, send, recv):
        self.ring, self.parts, self.landing, self.send, self.recv = ring, parts, landing, send, recv

    def slot(self, i, way, hop):
        return self.landing[i].at[hop + (0 if way == 0 else ring_hops(i, self.ring.size)[0])]

    def owner(self, i, way, hop):
        left = ring_hops(i, self.ring.size)[way] - hop
        return self.ring.at(left if way == 0 else -left)

    def copy(self, i, way, hop):
        source = self.parts[i].at[self.owner(i, way, 0)] if hop == 0 else self.slot(i, way, hop - 1)
        return remote(
            source,
            self.slot(i, way, hop),
            self.send.at[i, way, hop],
            self.recv.at[i, way, hop],
            {"dp": self.ring.targets[way]},
        )

    def each(self, hop):
        for i in range(len(self.parts)):
            for way in (0, 1):
                if hop < ring_hops(i, self.ring.size)[way]:
                    yield i, way

    def start(self):
        for i, way in self.each(0):
            self.copy(i, way, 0).start()

    def relay(self, hop):
        for i, way in self.each(hop - 1):
            self.copy(i, way, hop - 1).wait_recv()
            if hop < ring_hops(i, self.ring.size)[way]:
                slot = self.slot(i, way, hop - 1)
                own = self.parts[i][self.owner(i, way, hop)]
                slot[...] = (slot[...].astype(jnp.float32) + own.astype(jnp.float32)).astype(slot.dtype)
                self.copy(i, way, hop).start()

    def total(self, i):
        up, down = ring_hops(i, self.ring.size)
        return (
            self.parts[i][self.ring.me].astype(jnp.float32)
            + self.slot(i, 0, up - 1)[...].astype(jnp.float32)
            + self.slot(i, 1, down - 1)[...].astype(jnp.float32)
        )

    def finish(self):
        for hop in range(self.ring.size // 2):
            for i, way in self.each(hop):
                self.copy(i, way, hop).wait_send()


def piece_rows(piece, step):
    return pl.ds(piece * step if isinstance(piece, int) else pl.multiple_of(piece * step, step), step)


class RowGather:
    def __init__(self, chip, own, out, send, recv):
        self.chip, self.own, self.out, self.send, self.recv = chip, own, out, send, recv
        self.step = own.shape[0] // ROW_PIECES

    def copy(self, kind, piece):
        rows = piece_rows(piece, self.step)
        chip = self.chip
        owner = chip.peer if kind == 2 else chip.me
        target = self.out.at[owner, rows]
        device = chip.peer if kind == 0 else chip.mate
        return remote(
            target if kind == 2 else self.own.at[rows],
            target,
            self.send.at[kind, piece],
            self.recv.at[kind, piece],
            {"tensor": device},
        )

    def start(self):
        for kind in (0, 1):
            for piece in range(ROW_PIECES):
                self.copy(kind, piece).start()
        self.out[self.chip.me] = self.own[...]

    def relay(self, piece):
        self.copy(0, piece).wait_recv()
        self.copy(2, piece).start()

    def finish(self):
        for kind in (1, 2):
            for piece in range(ROW_PIECES):
                self.copy(kind, piece).wait_recv()
        for kind in (0, 1, 2):
            for piece in range(ROW_PIECES):
                self.copy(kind, piece).wait_send()


class RowScatter:
    def __init__(self, chip, parts, landing, send, recv):
        self.chip, self.parts, self.landing, self.send, self.recv = chip, parts, landing, send, recv
        self.pieces = send.shape[1]
        self.step = parts.shape[1] // self.pieces

    def rows(self, piece):
        return piece_rows(piece, self.step)

    def copy(self, kind, piece):
        chip, rows = self.chip, self.rows(piece)
        source = (
            self.parts.at[chip.across, rows],
            self.landing.at[0, rows],
            self.parts.at[chip.mate, rows],
        )[kind]
        return remote(
            source,
            self.landing.at[kind, rows],
            self.send.at[kind, piece],
            self.recv.at[kind, piece],
            {"tensor": chip.peer if kind == 1 else chip.mate},
        )

    def start(self):
        for kind in (0, 2):
            for piece in range(ROW_PIECES):
                self.copy(kind, piece).start()

    def relay(self, piece):
        rows = self.rows(piece)
        self.copy(0, piece).wait_recv()
        total = self.landing[0, rows].astype(jnp.float32) + self.parts[self.chip.peer, rows].astype(
            jnp.float32
        )
        self.landing[0, rows] = total.astype(self.landing.dtype)
        self.copy(1, piece).start()

    def total(self, piece):
        rows = self.rows(piece)
        self.copy(2, piece).wait_recv()
        self.copy(1, piece).wait_recv()
        return (
            self.parts[self.chip.me, rows].astype(jnp.float32)
            + self.landing[1, rows].astype(jnp.float32)
            + self.landing[2, rows].astype(jnp.float32)
        )

    def finish(self):
        for kind in (0, 1, 2):
            for piece in range(self.pieces):
                self.copy(kind, piece).wait_send()


class Meet:
    def __init__(self, chip, held, send, recv):
        self.chip, self.held, self.send, self.recv = chip, held, send, recv
        self.others = (chip.mate, chip.peer, chip.across)

    def copies(self):
        own = self.held.at[self.chip.me]
        for k, other in enumerate(self.others):
            yield remote(own, own, self.send.at[k], self.recv.at[k], {"tensor": other})

    def start(self, value):
        self.held[self.chip.me] = value
        for copy in self.copies():
            copy.start()

    def total(self):
        for copy in self.copies():
            copy.wait_recv()
        return (self.held[0] + self.held[1]) + (self.held[2] + self.held[3])

    def finish(self):
        for copy in self.copies():
            copy.wait_send()


def meet_sems():
    return [pltpu.SemaphoreType.DMA((3,))] * 2


def row_sems(pieces=ROW_PIECES):
    return [pltpu.SemaphoreType.DMA((3, pieces))] * 2


def ring_sems(count, size):
    return [pltpu.SemaphoreType.DMA((count, 2, size // 2))] * 2


def comm_params(collective_id):
    return pltpu.CompilerParams(collective_id=collective_id, has_side_effects=True)


def gather_rows(own, collective_id):
    def kernel(own_ref, out_ref, send, recv):
        chip = Chip()
        greet(({"tensor": chip.mate}, {"tensor": chip.peer}))
        rows = RowGather(chip, own_ref, out_ref, send, recv)
        rows.start()
        for piece in range(ROW_PIECES):
            rows.relay(piece)
        rows.finish()

    out = pl.pallas_call(
        kernel,
        out_shape=jax.ShapeDtypeStruct((4, *own.shape), own.dtype),
        in_specs=[VMEM],
        out_specs=VMEM,
        scratch_shapes=row_sems(),
        compiler_params=comm_params(collective_id),
        name="gather_rows",
    )(own)
    return out.reshape(4 * own.shape[0], own.shape[1])


def enter(slots, own, shards, shift_rows, size, collective_id):
    count = len(shards)
    block, model = own.shape
    group = 4 * block
    width = shards[0].shape[1] // 3
    tile = 256
    tiles = group // tile
    low, f32 = jnp.bfloat16, jnp.float32

    def kernel(*refs):
        slots_ref, own_ref, shard_refs = refs[0], refs[1], refs[2 : 2 + count]
        refs = refs[2 + count :]
        out_refs, (slotted_ref, qkv_ref) = refs[:count], refs[count : count + 2]
        rows_ref, total, shift, ring_send, ring_recv, row_send, row_recv = refs[count + 2 :]
        ring, chip = Ring(size), Chip()
        greet(
            (
                {"dp": ring.targets[0]},
                {"dp": ring.targets[1]},
                {"tensor": chip.mate},
                {"tensor": chip.peer},
            )
        )
        rows = RowGather(chip, own_ref, rows_ref, row_send, row_recv)
        weights = RingGather(ring, shard_refs, out_refs, ring_send, ring_recv)
        rows.start()
        weights.start()

        def pick(here, owner):
            first = pl.multiple_of(owner * block, block)
            wanted = here * tile + lax.broadcasted_iota(jnp.int32, (tile, block), 0)
            chosen = jnp.where(slots_ref[:, pl.ds(first, block)] == wanted, 1.0, 0.0).astype(low)
            return jnp.dot(chosen, rows_ref[owner], preferred_element_type=f32)

        def near(here, carry):
            @pl.when(here == tiles // 2)
            def _():
                rows.relay(0)

            total[piece_rows(here, tile)] = pick(here, chip.me) + pick(here, chip.mate)
            return carry

        def far(here, carry):
            @pl.when(here == tiles // 4)
            def _():
                weights.relay(3)

            at = piece_rows(here, tile)
            moved = total[at] + (pick(here, chip.peer) + pick(here, chip.across))
            slotted_ref[at] = moved.astype(low)
            return carry

        for piece in range(ROW_PIECES):
            rows.copy(1, piece).wait_recv()
        lax.fori_loop(0, tiles, near, 0)
        rows.relay(1)
        weights.relay(1)
        rows.relay(2)
        weights.relay(2)
        rows.relay(3)
        for piece in range(ROW_PIECES):
            rows.copy(2, piece).wait_recv()
        lax.fori_loop(0, tiles, far, 0)
        for hop in range(4, size // 2 + 1):
            weights.relay(hop)
        side, span = out_refs[-1], shards[-1].shape[1]
        shift[...] = jnp.zeros_like(shift)
        for j in range(width // span):
            owner = chip.me * (width // span) + j
            for part, row in shift_rows:
                at = part * width + j * span
                shift[:, at : at + span] = side[owner, row : row + 1].astype(f32)

        def project(here, carry):
            at = piece_rows(here, block)
            weight = out_refs[0][...].reshape(model, 3 * width)
            out = jnp.dot(slotted_ref[at], weight, preferred_element_type=f32) + shift[...]
            qkv_ref[at] = out.astype(low)
            return carry

        lax.fori_loop(0, 4, project, 0)
        for kind in (0, 1, 2):
            for piece in range(ROW_PIECES):
                rows.copy(kind, piece).wait_send()
        weights.finish()

    *gathered, slotted, qkv = pl.pallas_call(
        kernel,
        out_shape=[jax.ShapeDtypeStruct((size, *s.shape), s.dtype) for s in shards]
        + [jax.ShapeDtypeStruct((group, model), low), jax.ShapeDtypeStruct((group, 3 * width), low)],
        in_specs=[VMEM] * (count + 2),
        out_specs=[VMEM] * (count + 2),
        scratch_shapes=[
            pltpu.VMEM((4, block, model), low),
            pltpu.VMEM((group, model), f32),
            pltpu.VMEM((1, 3 * width), f32),
        ]
        + ring_sems(count, size)
        + row_sems(),
        compiler_params=comm_params(collective_id),
        name="enter",
    )(slots.reshape(1, group), own, *shards)
    return gathered, slotted, qkv


def attend(qkv, lengths, out_weight, shards, size, collective_id):
    ringed = size <= RING_MAX
    given = shards if ringed else []
    count = len(given)
    keys, width = qkv.shape[0], qkv.shape[1] // 3
    heads, model = width // HEAD_DIM, out_weight.shape[0]
    own_rows, pieces = keys // 4, 2
    block = own_rows // pieces
    factor = HEAD_DIM ** (-0.5)
    low, f32 = jnp.bfloat16, jnp.float32

    def kernel(*refs):
        len_ref, qkv_ref, weight_ref = refs[:3]
        shard_refs, refs = refs[3 : 3 + count], refs[3 + count :]
        out_ref, exact_ref, total_ref, sum_ref = refs[:4]
        full_refs, refs = refs[4 : 4 + count], refs[4 + count :]
        key_side, value_side, parts, landing, row_send, row_recv, *refs = refs
        chip = Chip()
        neighbours = ({"tensor": chip.mate}, {"tensor": chip.peer})
        if ringed:
            ring = Ring(size)
            weights = RingGather(ring, shard_refs, full_refs, *refs)
            neighbours += ({"dp": ring.targets[0]}, {"dp": ring.targets[1]})
        greet(neighbours)
        scatter = RowScatter(chip, parts, landing, row_send, row_recv)
        if ringed:
            weights.start()
        fill = key_fill(len_ref[0], keys)
        for h in range(heads):
            at = width + h * HEAD_DIM
            key_side[h, :, :HEAD_DIM] = qkv_ref[:, at : at + HEAD_DIM]
            key_side[h, :, HEAD_DIM:] = beside(keys, [fill])
            value_side[h, :, :HEAD_DIM] = qkv_ref[:, at + width : at + width + HEAD_DIM]
            value_side[h, :, HEAD_DIM:] = beside(keys, [1.0])
        ones = beside(block, [1.0])
        lane = lax.broadcasted_iota(jnp.int32, (block, WIDE), 1)

        def one(step, carry):
            near, odd = step // 4, lax.rem(step, 2)
            piece = lax.rem(step, 4) // 2
            owner = 2 * lax.rem(chip.me // 2 + 1 - near, 2) + lax.rem(lax.rem(chip.me, 2) + 1 - odd, 2)
            here = pl.ds(pl.multiple_of(owner * own_rows + piece * block, block), block)
            totals = jnp.zeros((block, WIDE), f32)
            for h in range(heads):
                lanes = slice(h * HEAD_DIM, (h + 1) * HEAD_DIM)
                query = jnp.concatenate([qkv_ref[here, lanes] * low(factor), ones], axis=1)
                scores = times_transposed(query, key_side[h])
                top = jnp.max(scores, axis=-1, keepdims=True)
                soft = jnp.exp(scores - top).astype(low)
                mixed = jnp.dot(soft, value_side[h], preferred_element_type=f32)
                total = mixed[:, HEAD_DIM : HEAD_DIM + 1]
                result = mixed[:, :HEAD_DIM] / total
                exact_ref[here, lanes] = result
                out_ref[here, lanes] = result.astype(low)
                totals = jnp.where(lane == h, top + jnp.log(total), totals)
            total_ref[here] = totals
            parts[owner, scatter.rows(piece)] = times_transposed(out_ref[here], weight_ref[...]).astype(low)

            @pl.when((near == 0) & (odd == 0))
            def _():
                scatter.copy(0, piece).start()

            @pl.when((near == 0) & (odd == 1))
            def _():
                scatter.relay(piece)

            @pl.when((near == 1) & (odd == 0))
            def _():
                scatter.copy(2, piece).start()

            if ringed:
                for hop in range(1, size // 2 + 1):

                    @pl.when(step == 2 * hop - 1)
                    def _():
                        weights.relay(hop)

            return carry

        lax.fori_loop(0, 4 * pieces, one, 0)
        for piece in range(pieces):
            sum_ref[scatter.rows(piece)] = scatter.total(piece)
        scatter.finish()
        if ringed:
            weights.finish()

    context, exact, totals, summed, *gathered = pl.pallas_call(
        kernel,
        out_shape=[
            jax.ShapeDtypeStruct((keys, width), low),
            jax.ShapeDtypeStruct((keys, width), f32),
            jax.ShapeDtypeStruct((keys, WIDE), f32),
            jax.ShapeDtypeStruct((own_rows, model), f32),
        ]
        + [jax.ShapeDtypeStruct((size, *s.shape), s.dtype) for s in given],
        in_specs=[pl.BlockSpec(memory_space=pltpu.SMEM)] + [VMEM] * (2 + count),
        out_specs=[VMEM] * (4 + count),
        scratch_shapes=[
            pltpu.VMEM((heads, keys, WIDE), low),
            pltpu.VMEM((heads, keys, WIDE), low),
            pltpu.VMEM((4, own_rows, model), low),
            pltpu.VMEM((3, own_rows, model), low),
        ]
        + row_sems(pieces)
        + (ring_sems(count, size) if ringed else []),
        compiler_params=comm_params(collective_id),
        name="attend",
    )(lengths, qkv, out_weight, *given)
    if not ringed:
        gathered = [lax.all_gather(shard, "dp") for shard in shards]
    return context, exact, totals, summed, gathered


def turned(left, right):
    return lax.dot_general(
        left, right, (((0,), (0,)), ((), ())), preferred_element_type=jnp.float32
    )


def around_rows(chip, gather, scatter, work, keep, middle=None, end=None):
    parts = scatter.parts

    def own(piece, carry):
        rows = scatter.rows(piece)
        keep[rows] = work(chip.me, rows)
        return carry

    def near(piece, carry):
        rows = scatter.rows(piece)
        gather.copy(1, piece).wait_recv()
        parts[chip.mate, rows] = work(chip.mate, rows).astype(parts.dtype)
        scatter.copy(2, piece).start()
        return carry

    def far(piece, carry):
        rows = scatter.rows(piece)
        gather.relay(piece)
        parts[chip.peer, rows] = work(chip.peer, rows).astype(parts.dtype)

        @pl.when(piece > 0)
        def _():
            scatter.relay(piece - 1)

        gather.copy(2, piece).wait_recv()
        parts[chip.across, rows] = work(chip.across, rows).astype(parts.dtype)
        scatter.copy(0, piece).start()
        return carry

    def last(piece, carry):
        rows = scatter.rows(piece)
        scatter.copy(2, piece).wait_recv()
        scatter.copy(1, piece).wait_recv()
        keep[rows] += scatter.landing[1, rows].astype(jnp.float32) + scatter.landing[2, rows].astype(
            jnp.float32
        )
        return carry

    gather.start()
    lax.fori_loop(0, ROW_PIECES, own, 0)
    lax.fori_loop(0, ROW_PIECES, near, 0)
    if middle is not None:
        middle()
    lax.fori_loop(0, ROW_PIECES, far, 0)
    scatter.relay(ROW_PIECES - 1)
    if end is not None:
        end()
    lax.fori_loop(0, ROW_PIECES, last, 0)
    for copies in (gather, scatter):
        for kind in (0, 1, 2):
            for piece in range(ROW_PIECES):
                copies.copy(kind, piece).wait_send()


def feed_forward(own, up_weight, shift, down_weight, collective_id):
    rows, width = own.shape
    hidden_width = up_weight.shape[1]
    low, f32 = jnp.bfloat16, jnp.float32

    def kernel(
        own_ref, up_ref, shift_ref, down_ref, rows_ref, hidden_ref, slope_ref, out_ref, parts, landing, *sems
    ):
        chip = Chip()
        greet(({"tensor": chip.mate}, {"tensor": chip.peer}))
        gather = RowGather(chip, own_ref, rows_ref, *sems[:2])
        scatter = RowScatter(chip, parts, landing, *sems[2:])

        def work(owner, rows):
            pre = jnp.dot(rows_ref[owner, rows], up_ref[...], preferred_element_type=f32) + shift_ref[...]
            cdf = 0.5 * (1.0 + lax.erf(pre * 0.7071067811865476))
            hidden = (pre * cdf).astype(low)
            hidden_ref[owner, rows] = hidden
            slope = cdf + pre * (jnp.exp(-0.5 * pre * pre) * 0.3989422804014327)
            slope_ref[owner, rows] = slope.astype(low)
            return times_transposed(hidden, down_ref[...])

        around_rows(chip, gather, scatter, work, out_ref)

    return pl.pallas_call(
        kernel,
        out_shape=[
            jax.ShapeDtypeStruct((4, rows, width), low),
            jax.ShapeDtypeStruct((4, rows, hidden_width), low),
            jax.ShapeDtypeStruct((4, rows, hidden_width), low),
            jax.ShapeDtypeStruct((rows, width), f32),
        ],
        in_specs=[VMEM] * 4,
        out_specs=[VMEM] * 4,
        scratch_shapes=[pltpu.VMEM((4, rows, width), low), pltpu.VMEM((3, rows, width), low)]
        + row_sems() * 2,
        compiler_params=comm_params(collective_id),
        name="feed_forward",
    )(own, up_weight, shift.reshape(1, -1), down_weight)


def feed_back(own, slope, mid_rows, hidden, up_weight, down_weight, collective_id):
    rows, width = own.shape
    hidden_width = up_weight.shape[1]
    low, f32 = jnp.bfloat16, jnp.float32
    band = 256

    def kernel(
        own_ref,
        slope_ref,
        mid_ref,
        hidden_ref,
        up_ref,
        down_ref,
        out_ref,
        grad_up_ref,
        grad_down_ref,
        shift_ref,
        rows_ref,
        dpre_ref,
        up_sum,
        down_sum,
        parts,
        landing,
        *sems,
    ):
        chip = Chip()
        greet(({"tensor": chip.mate}, {"tensor": chip.peer}))
        gather = RowGather(chip, own_ref, rows_ref, *sems[:2])
        scatter = RowScatter(chip, parts, landing, *sems[2:])
        shift_ref[...] = jnp.zeros_like(shift_ref)

        def work(owner, rows):
            dhidden = jnp.dot(rows_ref[owner, rows], down_ref[...], preferred_element_type=f32)
            dpre = (dhidden * slope_ref[owner, rows].astype(f32)).astype(low)
            dpre_ref[owner, rows] = dpre
            shift_ref[...] += jnp.sum(dpre.astype(f32), axis=0, keepdims=True)
            return times_transposed(dpre, up_ref[...])

        def grads(owners, first):
            def one(tile, carry):
                columns = pl.ds(pl.multiple_of(tile * band, band), band)
                for left, right, total in (
                    (mid_ref, dpre_ref, up_sum),
                    (rows_ref, hidden_ref, down_sum),
                ):
                    term = turned(left[owners[0], :, columns], right[owners[0]])
                    term += turned(left[owners[1], :, columns], right[owners[1]])
                    total[columns] = term if first else total[columns] + term
                return carry

            return lambda: lax.fori_loop(0, width // band, one, 0)

        around_rows(
            chip,
            gather,
            scatter,
            work,
            out_ref,
            grads((chip.me, chip.mate), True),
            grads((chip.peer, chip.across), False),
        )
        grad_up_ref[...] = up_sum[...].astype(low)
        grad_down_ref[...] = down_sum[...].astype(low)

    return pl.pallas_call(
        kernel,
        out_shape=[
            jax.ShapeDtypeStruct((rows, width), f32),
            jax.ShapeDtypeStruct((width, hidden_width), low),
            jax.ShapeDtypeStruct((width, hidden_width), low),
            jax.ShapeDtypeStruct((1, hidden_width), f32),
        ],
        in_specs=[VMEM] * 6,
        out_specs=[VMEM] * 4,
        scratch_shapes=[
            pltpu.VMEM((4, rows, width), low),
            pltpu.VMEM((4, rows, hidden_width), low),
            pltpu.VMEM((width, hidden_width), f32),
            pltpu.VMEM((width, hidden_width), f32),
            pltpu.VMEM((4, rows, width), low),
            pltpu.VMEM((3, rows, width), low),
        ]
        + row_sems() * 2,
        compiler_params=comm_params(collective_id),
        name="feed_back",
    )(own, slope, mid_rows, hidden, up_weight, down_weight)


def enter_slots(slots, arrived, weight, shift):
    group, width = arrived.shape
    block = 256

    def kernel(slots_ref, arrived_ref, weight_ref, shift_ref, rows_ref, out_ref):
        first = pl.program_id(0) * block
        wanted = first + lax.broadcasted_iota(jnp.int32, (block, group), 0)
        pick = jnp.where(slots_ref[...] == wanted, 1.0, 0.0).astype(jnp.bfloat16)
        rows = jnp.dot(pick, arrived_ref[...], preferred_element_type=jnp.float32).astype(jnp.bfloat16)
        rows_ref[...] = rows
        out = jnp.dot(rows, weight_ref[...], preferred_element_type=jnp.float32) + shift_ref[...]
        out_ref[...] = out.astype(jnp.bfloat16)

    return pl.pallas_call(
        kernel,
        grid=(group // block,),
        in_specs=[VMEM] * 4,
        out_specs=[
            pl.BlockSpec((block, width), lambda i: (i, 0)),
            pl.BlockSpec((block, weight.shape[1]), lambda i: (i, 0)),
        ],
        out_shape=[
            jax.ShapeDtypeStruct((group, width), jnp.bfloat16),
            jax.ShapeDtypeStruct((group, weight.shape[1]), jnp.bfloat16),
        ],
        name="enter_slots",
    )(slots.reshape(1, group), arrived, weight, shift.reshape(1, -1))


def attend_back(own, out_weight, context, qkv, exact, totals, lengths, parts, size, collective_id):
    ringed = size <= RING_MAX
    given = parts if ringed else []
    count = len(given)
    block, model = own.shape
    keys, width = qkv.shape[0], qkv.shape[1] // 3
    heads = width // HEAD_DIM
    factor = HEAD_DIM ** (-0.5)
    low, f32 = jnp.bfloat16, jnp.float32

    def kernel(*refs):
        len_ref, own_ref, weight_ref, context_ref, qkv_ref, exact_ref, total_ref = refs[:7]
        part_refs, refs = refs[7 : 7 + count], refs[7 + count :]
        out_ref, column_ref, grad_ref = refs[:3]
        sum_refs, refs = refs[3 : 3 + count], refs[3 + count :]
        rows_ref, key_side, value_side, key_turned, sums, grad_sum, row_send, row_recv = refs[:8]
        refs = refs[8:]
        chip = Chip()
        neighbours = ({"tensor": chip.mate}, {"tensor": chip.peer})
        if ringed:
            landing, (held, ring_send, ring_recv, meet_send, meet_recv) = refs[:count], refs[count:]
            ring = Ring(size)
            meet = Meet(chip, held, meet_send, meet_recv)
            grads = RingScatter(ring, part_refs, landing, ring_send, ring_recv)
            neighbours += ({"tensor": chip.across},)
            neighbours += ({"dp": ring.targets[0]}, {"dp": ring.targets[1]})
        greet(neighbours)
        rows = RowGather(chip, own_ref, rows_ref, row_send, row_recv)
        rows.start()
        if ringed:
            grads.start()
        fill = key_fill(len_ref[0], keys)
        for h in range(heads):
            at = width + h * HEAD_DIM
            key = qkv_ref[:, at : at + HEAD_DIM]
            key_side[h, :, :HEAD_DIM] = key
            key_side[h, :, HEAD_DIM:] = beside(keys, [fill, 1.0, 1.0, 1.0])
            key_turned[h] = (key * low(factor)).T
            value_side[h, :, :HEAD_DIM] = qkv_ref[:, at + width : at + width + HEAD_DIM]
            value_side[h, :, HEAD_DIM:] = beside(keys, [1.0, 1.0, 1.0])
        sums[...] = jnp.zeros_like(sums)
        grad_sum[...] = jnp.zeros_like(grad_sum)

        def one(step, carry):
            owner = 2 * lax.rem(chip.me // 2 + step // 2, 2) + lax.rem(lax.rem(chip.me, 2) + step, 2)

            @pl.when(step == 1)
            def _():
                for piece in range(ROW_PIECES):
                    rows.copy(1, piece).wait_recv()

            @pl.when(step == 3)
            def _():
                for piece in range(ROW_PIECES):
                    rows.copy(2, piece).wait_recv()

            first = pl.multiple_of(owner * block, block)
            here = pl.ds(first, block)
            drows = rows_ref[owner]
            dcontext = jnp.dot(drows, weight_ref[...], preferred_element_type=f32).astype(low)
            grad_sum[...] += turned(drows, context_ref[here])
            blank = jnp.zeros((block, HEAD_DIM), low)
            for h in range(heads):
                lanes = slice(h * HEAD_DIM, (h + 1) * HEAD_DIM)
                dout = dcontext[:, lanes]
                delta = jnp.sum(dout.astype(f32) * exact_ref[here, lanes], axis=-1, keepdims=True)
                query = qkv_ref[here, lanes] * low(factor)
                query_wide = jnp.concatenate(
                    [query, beside(block, [1.0, *thirds(-total_ref[here, h : h + 1])])], axis=1
                )
                dout_wide = jnp.concatenate([dout, beside(block, thirds(-delta))], axis=1)
                soft = jnp.exp(times_transposed(key_side[h], query_wide))
                dsoft = times_transposed(value_side[h], dout_wide)
                dscore = (soft * dsoft).astype(low)
                soft = soft.astype(low)
                sums[h] += jnp.dot(
                    soft, jnp.concatenate([dout, blank], axis=1), preferred_element_type=f32
                ) + jnp.dot(
                    dscore, jnp.concatenate([blank, query], axis=1), preferred_element_type=f32
                )
                dquery = jnp.dot(key_turned[h], dscore, preferred_element_type=f32)
                out_ref[here, lanes] = dquery.T.astype(low)
                if ringed and h == 0:

                    @pl.when(step == 3)
                    def _():
                        grads.relay(size // 2)
                        meet.start(grads.total(count - 1))

                if ringed and h == heads - 1:
                    for hop in range(1, size // 2):

                        @pl.when(step == hop - 1)
                        def _():
                            grads.relay(hop)

            @pl.when(step < 2)
            def _():
                rows.relay(2 * step)
                rows.relay(2 * step + 1)

            return carry

        lax.fori_loop(0, 4, one, 0)
        for h in range(heads):
            both = sums[h].astype(low)
            at = width + h * HEAD_DIM
            out_ref[:, at : at + HEAD_DIM] = both[:, HEAD_DIM:]
            out_ref[:, at + width : at + width + HEAD_DIM] = both[:, :HEAD_DIM]
        column_ref[...] = jnp.sum(out_ref[...].astype(f32), axis=0, keepdims=True)
        grad_ref[...] = grad_sum[...].astype(low)
        for i in range(count - 1):
            sum_refs[i][...] = grads.total(i)
        if ringed:
            sum_refs[count - 1][...] = meet.total()
            meet.finish()
            grads.finish()
        for kind in (0, 1, 2):
            for piece in range(ROW_PIECES):
                rows.copy(kind, piece).wait_send()

    scratch = [
        pltpu.VMEM((4, block, model), low),
        pltpu.VMEM((heads, keys, WIDE), low),
        pltpu.VMEM((heads, keys, WIDE), low),
        pltpu.VMEM((heads, HEAD_DIM, keys), low),
        pltpu.VMEM((heads, keys, WIDE), f32),
        pltpu.VMEM((model, width), f32),
        *row_sems(),
    ]
    if ringed:
        scratch += [pltpu.VMEM((size - 1, *p.shape[1:]), p.dtype) for p in parts]
        scratch += [pltpu.VMEM((4, *parts[-1].shape[1:]), f32)]
        scratch += ring_sems(count, size) + meet_sems()
    dqkv, columns, grad_out, *summed = pl.pallas_call(
        kernel,
        out_shape=[
            jax.ShapeDtypeStruct((keys, 3 * width), low),
            jax.ShapeDtypeStruct((1, 3 * width), f32),
            jax.ShapeDtypeStruct((model, width), low),
        ]
        + [jax.ShapeDtypeStruct(p.shape[1:], f32) for p in given],
        in_specs=[pl.BlockSpec(memory_space=pltpu.SMEM)] + [VMEM] * (6 + count),
        out_specs=[VMEM] * (3 + count),
        scratch_shapes=scratch,
        compiler_params=comm_params(collective_id),
        name="attend_back",
    )(lengths, own, out_weight, context, qkv, exact, totals, *given)
    if not ringed:
        summed = [lax.psum_scatter(p.astype(f32), "dp", scatter_dimension=0) for p in parts]
        summed[-1] = lax.psum(summed[-1], "tensor")
    return dqkv, columns[0], grad_out, summed


def finish(rows, dqkv, weight, resid, slots, parts, size, collective_id):
    ringed = size <= RING_MAX
    given = parts if ringed else []
    count = len(given) + 1
    group, model = rows.shape
    columns = dqkv.shape[1]
    own_rows = group // 4
    pieces, band = 2, model // 2
    low, f32 = jnp.bfloat16, jnp.float32

    def kernel(*refs):
        rows_ref, dqkv_ref, weight_ref, resid_ref, slots_ref = refs[:5]
        part_refs, refs = refs[5 : 4 + count], refs[4 + count :]
        own_ref, grad_ref, *sum_refs = refs[: 1 + count]
        through, leaving, row_landing, row_send, row_recv, *refs = refs[1 + count :]
        chip = Chip()
        neighbours = ({"tensor": chip.mate}, {"tensor": chip.peer})
        if ringed:
            local, landing, (held, ring_send, ring_recv, meet_send, meet_recv) = (
                refs[0],
                refs[1 : 1 + count],
                refs[1 + count :],
            )
            ring = Ring(size)
            meet = Meet(chip, held, meet_send, meet_recv)
            grads = RingScatter(ring, (*part_refs, local), landing, ring_send, ring_recv)
            neighbours += ({"tensor": chip.across},)
            neighbours += ({"dp": ring.targets[0]}, {"dp": ring.targets[1]})
        greet(neighbours)
        scatter = RowScatter(chip, leaving, row_landing, row_send, row_recv)
        half = group // 2

        def spread(part, carry):
            here = pl.ds(pl.multiple_of(part * half, half), half)
            through[here] = times_transposed(dqkv_ref[here], weight_ref[...]).astype(low)
            return carry

        lax.fori_loop(0, 2, spread, 0)
        mine = pl.ds(pl.multiple_of(chip.me * own_rows, own_rows), own_rows)
        through[mine] = (
            times_transposed(dqkv_ref[mine], weight_ref[...]) + resid_ref[...]
        ).astype(low)
        step = own_rows // pieces
        slot = lax.broadcasted_iota(jnp.int32, (step, group), 1)

        def leave(owner, piece):
            first = pl.multiple_of(owner * own_rows + piece * step, step)
            pick = jnp.where(slots_ref[pl.ds(first, step)] == slot, 1.0, 0.0).astype(low)
            moved = jnp.dot(pick, through[...], preferred_element_type=f32).astype(low)
            leaving[owner, scatter.rows(piece)] = moved

        def outward(piece, carry):
            leave(chip.across, piece)
            scatter.copy(0, piece).start()
            leave(chip.peer, piece)
            scatter.relay(piece)
            return carry

        def inward(piece, carry):
            leave(chip.mate, piece)
            scatter.copy(2, piece).start()
            leave(chip.me, piece)
            return carry

        lax.fori_loop(0, 1, outward, 0)
        for tile in range(2):
            grad = turned(rows_ref[:, tile * band : (tile + 1) * band], dqkv_ref[...]).astype(low)
            if ringed:
                half_ring = size // 2
                local[tile * half_ring : (tile + 1) * half_ring] = grad.reshape(
                    half_ring, band // half_ring, columns
                )
            else:
                grad_ref[tile * band : (tile + 1) * band] = grad
        if ringed:
            grads.start()
        lax.fori_loop(1, pieces, outward, 0)
        if ringed:
            grads.relay(1)
        lax.fori_loop(0, pieces, inward, 0)
        if ringed:
            for hop in range(2, size // 2 + 1):
                grads.relay(hop)
            meet.start(grads.total(count - 2))
        for piece in range(pieces):
            own_ref[scatter.rows(piece)] = scatter.total(piece)
        if ringed:
            grad_ref[...] = grads.total(count - 1)
            for i in range(count - 2):
                sum_refs[i][...] = grads.total(i)
            sum_refs[count - 2][...] = meet.total()
            meet.finish()
            grads.finish()
        scatter.finish()

    scratch = [
        pltpu.VMEM((group, model), low),
        pltpu.VMEM((4, own_rows, model), low),
        pltpu.VMEM((3, own_rows, model), low),
        *row_sems(pieces),
    ]
    if ringed:
        local = jax.ShapeDtypeStruct((size, model // size, columns), low)
        scratch += [pltpu.VMEM(local.shape, low)]
        scratch += [pltpu.VMEM((size - 1, *p.shape[1:]), p.dtype) for p in (*parts, local)]
        scratch += [pltpu.VMEM((4, *parts[-1].shape[1:]), f32)]
        scratch += ring_sems(count, size) + meet_sems()
        first = jax.ShapeDtypeStruct(local.shape[1:], f32)
    else:
        first = jax.ShapeDtypeStruct((model, columns), low)
    own, grad, *summed = pl.pallas_call(
        kernel,
        out_shape=[jax.ShapeDtypeStruct((own_rows, model), f32), first]
        + [jax.ShapeDtypeStruct(p.shape[1:], f32) for p in given],
        in_specs=[VMEM] * (4 + count),
        out_specs=[VMEM] * (1 + count),
        scratch_shapes=scratch,
        compiler_params=comm_params(collective_id),
        name="finish",
    )(rows, dqkv, weight, resid, slots.reshape(group, 1), *given)
    if not ringed:
        grad = grad.astype(f32).reshape(size, model // size, columns)
        grad, *summed = [lax.psum_scatter(p.astype(f32), "dp", scatter_dimension=0) for p in (grad, *parts)]
        summed[-1] = lax.psum(summed[-1], "tensor")
    return own, grad, summed


def body(
    tokens,
    lengths,
    arrival_slots,
    w_qkv,
    w_out,
    w_up,
    w_down,
    w_proj,
    norm_gains,
    biases,
    up_bias,
    cotangent,
):
    tensor_size = lax.axis_size("tensor")
    tensor_pos = lax.axis_index("tensor")
    own_rows = tokens.shape[0]
    group_rows = own_rows * tensor_size
    slot_order = arrival_slots[0]
    size = lax.axis_size("dp")
    part_rows, width_local = w_qkv.shape[1:]
    low = jnp.bfloat16
    width = size * part_rows
    flat = lambda full: full.reshape(width, full.shape[2])
    shards = [
        w_qkv.astype(low).transpose(1, 0, 2).reshape(part_rows, 3 * width_local),
        w_up.astype(low),
        w_out.astype(low).T,
        jnp.concatenate(
            [norm_gains.astype(low), biases.astype(low), up_bias.astype(low).reshape(-1, part_rows)]
        ),
    ]
    ringed = size <= RING_MAX
    if ringed:
        gathered, slotted, qkv_all = enter(slot_order, tokens, shards, ((0, 2), (2, 3)), size, 0)
    else:
        gathered = [lax.all_gather(shard, "dp") for shard in shards]
    qkv_weight, up_weight, out_weight = (flat(full) for full in gathered[:3])
    small = gathered[3].astype(jnp.float32)
    side = small[:, :8].transpose(1, 0, 2).reshape(8, width)
    gain_full, bias_full = side[:2], side[2:]
    upbias_full = small[:, 8:].reshape(-1)
    hidden_local = up_weight.shape[1]
    col_start = tensor_pos * width_local
    if not ringed:
        query_bias = lax.dynamic_slice_in_dim(bias_full[0], col_start, width_local)
        value_bias = lax.dynamic_slice_in_dim(bias_full[1], col_start, width_local)
        qkv_bias = jnp.concatenate([query_bias, jnp.zeros_like(query_bias), value_bias])
        arrived = gather_rows(tokens, 0)
        slotted, qkv_all = enter_slots(slot_order, arrived, qkv_weight, qkv_bias)
    row_start = tensor_pos * own_rows
    resid_input = lax.dynamic_slice_in_dim(slotted, row_start, own_rows, 0).astype(jnp.float32)
    positions = row_start + jnp.arange(own_rows, dtype=jnp.int32)
    row_keep = (positions % SLOT < lengths[positions // SLOT]).astype(jnp.float32)
    context, exact, totals, attn_part, gathered = attend(
        qkv_all, lengths, out_weight, [w_down.astype(low).T, w_proj.astype(low)], size, 1
    )
    down_weight, proj_weight = (flat(full) for full in gathered)
    first_sum = resid_input + attn_part + bias_full[2]
    first_norm, back_first = jax.vjp(norm_rows, first_sum, gain_full[0], bias_full[3])
    first_low = first_norm.astype(jnp.bfloat16)
    upbias_own = lax.dynamic_slice_in_dim(upbias_full, tensor_pos * hidden_local, hidden_local)
    mid_rows, hidden, slope, ffn_part = feed_forward(first_low, up_weight, upbias_own, down_weight, 2)
    second_sum = first_norm + ffn_part + bias_full[4]
    second_norm, back_second = jax.vjp(norm_rows, second_sum, gain_full[1], bias_full[5])
    second_low = second_norm.astype(jnp.bfloat16)
    projected = jnp.dot(second_low, proj_weight, preferred_element_type=jnp.float32)

    def unit_rows(values):
        return (
            values
            * lax.rsqrt(jnp.sum(values * values, axis=-1, keepdims=True) + EPS_UNIT)
            * row_keep[:, None]
        )

    embeddings, back_unit = jax.vjp(unit_rows, projected)
    (dproj,) = back_unit(cotangent.astype(jnp.float32))
    dproj_low = dproj.astype(jnp.bfloat16)
    grad_proj = contract_rows(second_low, dproj_low)
    dsecond_norm = times_transposed(dproj_low, proj_weight)
    dsecond, grad_gain_two, grad_shift_two = back_second(dsecond_norm)
    dsecond_low = dsecond.astype(jnp.bfloat16)
    dfirst_norm, grad_up, grad_down, dshift = feed_back(
        dsecond_low, slope, mid_rows, hidden, up_weight, down_weight, 4
    )
    grad_upbias = lax.dynamic_update_slice_in_dim(
        jnp.zeros(upbias_full.shape, jnp.float32), dshift[0], tensor_pos * hidden_local, 0
    )
    dfirst, grad_gain_one, grad_shift_one = back_first(dfirst_norm + dsecond)
    dfirst_low = dfirst.astype(jnp.bfloat16)
    cut = lambda grad: grad.astype(low).reshape(size, part_rows, grad.shape[1])
    dqkv, column_sums, grad_out, (sum_up, sum_down, sum_proj) = attend_back(
        dfirst_low,
        out_weight,
        context,
        qkv_all,
        exact,
        totals,
        lengths,
        [cut(grad_up), cut(grad_down), cut(grad_proj)],
        size,
        6,
    )
    column_sums = column_sums.reshape(3, width_local)
    zero_row = jnp.zeros((bias_full.shape[1],), jnp.float32)
    grad_biases = jnp.stack(
        [
            lax.dynamic_update_slice_in_dim(zero_row, column_sums[0], col_start, 0),
            lax.dynamic_update_slice_in_dim(zero_row, column_sums[2], col_start, 0),
            jnp.sum(dfirst, axis=0),
            grad_shift_one,
            jnp.sum(dsecond, axis=0),
            grad_shift_two,
        ]
    )
    grad_gains = jnp.stack([grad_gain_one, grad_gain_two])
    small_grad = jnp.concatenate([grad_gains, grad_biases]).reshape(8, size, part_rows).transpose(1, 0, 2)
    small_grad = jnp.concatenate([small_grad, grad_upbias.reshape(size, -1, part_rows)], axis=1)
    grad_tokens, sum_qkv, (sum_out, sum_small) = finish(
        slotted, dqkv, qkv_weight, dfirst, slot_order, [cut(grad_out), small_grad], size, 7
    )
    return (
        embeddings,
        grad_tokens,
        sum_qkv.reshape(part_rows, 3, width_local).transpose(1, 0, 2),
        sum_out.T,
        sum_up,
        sum_down.T,
        sum_proj,
        sum_small[:2],
        sum_small[2:8],
        sum_small[8:].reshape(-1),
    )


def solution(mesh):
    return jax.shard_map(
        body,
        mesh=mesh,
        in_specs=(
            P(("dp", "tensor"), None),
            P("dp"),
            P("dp", None),
            P(None, "dp", "tensor"),
            P("tensor", "dp"),
            P("dp", "tensor"),
            P("tensor", "dp"),
            P("dp", None),
            P(None, "dp"),
            P(None, "dp"),
            P("dp"),
            P(("dp", "tensor"), None),
        ),
        out_specs=(
            P(("dp", "tensor"), None),
            P(("dp", "tensor"), None),
            P(None, "dp", "tensor"),
            P("tensor", "dp"),
            P("dp", "tensor"),
            P("tensor", "dp"),
            P("dp", None),
            P(None, "dp"),
            P(None, "dp"),
            P("dp"),
        ),
        check_vma=False,
    )
```

```python
import jax
import jax.numpy as jnp
from jax import lax
from jax.experimental import pallas as pl
from jax.experimental.pallas import tpu as pltpu
from jax.sharding import PartitionSpec as P

HEAD_DIM = 64
SLOT = 2048


EPS_NORM = 1e-06
EPS_UNIT = 1e-06
NEG_FILL = -1e30


def norm_rows(values, gain, shift):
    center = values - jnp.mean(values, axis=-1, keepdims=True)
    spread = jnp.mean(center * center, axis=-1, keepdims=True)
    return center * lax.rsqrt(spread + EPS_NORM) * gain + shift


def contract_rows(left, right):
    return lax.dot_general(
        left, right, (((0,), (0,)), ((), ())), preferred_element_type=jnp.float32
    )


def times_transposed(left, right):
    return lax.dot_general(
        left, right, (((1,), (1,)), ((), ())), preferred_element_type=jnp.float32
    )


MESH = pl.DeviceIdType.MESH
VMEM = pl.BlockSpec(memory_space=pltpu.VMEM)
WIDE = 128


def lane_index(rows):
    return lax.broadcasted_iota(jnp.int32, (rows, WIDE - HEAD_DIM), 1)


def thirds(column):
    parts = []
    for _ in range(3):
        part = column.astype(jnp.bfloat16).astype(jnp.float32)
        parts.append(part)
        column = column - part
    return parts


def beside(rows, columns):
    lane = lane_index(rows)
    out = jnp.zeros(lane.shape, jnp.float32)
    for i, column in enumerate(columns):
        out = jnp.where(lane == i, column, out)
    return out.astype(jnp.bfloat16)


def key_fill(length, keys):
    position = lax.broadcasted_iota(jnp.int32, (keys, 1), 0)
    return jnp.where(position < length, 0.0, NEG_FILL)


RING_MAX = 8
VMEM_GRANT = 40 << 20
ROW_PIECES = 4


def ring_place(position, size):
    far = position // (size // 2)
    return 2 * ((1 - far) * position + far * (size - 1 - position)) + far


def ring_position(index, size):
    row, far = index // 2, index % 2
    return (1 - far) * row + far * (size - 1 - row)


def ring_hops(index, size):
    longer, shorter = size // 2, size - 1 - size // 2
    return (longer, shorter) if index % 2 == 0 else (shorter, longer)


class Ring:
    def __init__(self, size):
        self.size = size
        self.me = lax.axis_index("dp")
        self.position = ring_position(self.me, size)
        self.targets = (self.at(1), self.at(-1))

    def at(self, offset):
        return ring_place(lax.rem(self.position + (offset + self.size), self.size), self.size)


class Chip:
    def __init__(self):
        self.me = lax.axis_index("tensor")
        chip, core = self.me // 2, self.me % 2
        self.mate = 2 * chip + (1 - core)
        self.peer = 2 * (1 - chip) + core
        self.across = 2 * (1 - chip) + (1 - core)


def greet(devices):
    barrier = pltpu.get_barrier_semaphore()
    for device in devices:
        pl.semaphore_signal(barrier, inc=1, device_id=device, device_id_type=MESH)
    pl.semaphore_wait(barrier, len(devices))


def remote(source, target, send, recv, device):
    return pltpu.make_async_remote_copy(
        src_ref=source,
        dst_ref=target,
        send_sem=send,
        recv_sem=recv,
        device_id=device,
        device_id_type=MESH,
    )


class RingGather:
    def __init__(self, ring, shards, outs, send, recv):
        self.ring, self.shards, self.outs, self.send, self.recv = ring, shards, outs, send, recv

    def copy(self, i, way, hop):
        owner = self.ring.at(-hop if way == 0 else hop)
        target = self.outs[i].at[owner]
        return remote(
            self.shards[i] if hop == 0 else target,
            target,
            self.send.at[i, way, hop],
            self.recv.at[i, way, hop],
            {"dp": self.ring.targets[way]},
        )

    def each(self, hop):
        for i in range(len(self.shards)):
            for way in (0, 1):
                if hop < ring_hops(i, self.ring.size)[way]:
                    yield i, way

    def start(self):
        for i, way in self.each(0):
            self.copy(i, way, 0).start()
        for shard, out in zip(self.shards, self.outs):
            out[self.ring.me] = shard[...]

    def relay(self, hop, only=None):
        for i, way in self.each(hop - 1):
            if only is not None and i not in only:
                continue
            self.copy(i, way, hop - 1).wait_recv()
            if hop < ring_hops(i, self.ring.size)[way]:
                self.copy(i, way, hop).start()

    def finish(self):
        for hop in range(self.ring.size // 2):
            for i, way in self.each(hop):
                self.copy(i, way, hop).wait_send()


class RingScatter:
    def __init__(self, ring, parts, landing, send, recv):
        self.ring, self.parts, self.landing, self.send, self.recv = ring, parts, landing, send, recv

    def slot(self, i, way, hop):
        return self.landing[i].at[hop + (0 if way == 0 else ring_hops(i, self.ring.size)[0])]

    def owner(self, i, way, hop):
        left = ring_hops(i, self.ring.size)[way] - hop
        return self.ring.at(left if way == 0 else -left)

    def copy(self, i, way, hop):
        source = self.parts[i].at[self.owner(i, way, 0)] if hop == 0 else self.slot(i, way, hop - 1)
        return remote(
            source,
            self.slot(i, way, hop),
            self.send.at[i, way, hop],
            self.recv.at[i, way, hop],
            {"dp": self.ring.targets[way]},
        )

    def each(self, hop):
        for i in range(len(self.parts)):
            for way in (0, 1):
                if hop < ring_hops(i, self.ring.size)[way]:
                    yield i, way

    def start(self):
        for i, way in self.each(0):
            self.copy(i, way, 0).start()

    def relay(self, hop):
        for i, way in self.each(hop - 1):
            self.copy(i, way, hop - 1).wait_recv()
            if hop < ring_hops(i, self.ring.size)[way]:
                slot = self.slot(i, way, hop - 1)
                own = self.parts[i][self.owner(i, way, hop)]
                slot[...] = (slot[...].astype(jnp.float32) + own.astype(jnp.float32)).astype(slot.dtype)
                self.copy(i, way, hop).start()

    def total(self, i):
        up, down = ring_hops(i, self.ring.size)
        return (
            self.parts[i][self.ring.me].astype(jnp.float32)
            + self.slot(i, 0, up - 1)[...].astype(jnp.float32)
            + self.slot(i, 1, down - 1)[...].astype(jnp.float32)
        )

    def finish(self):
        for hop in range(self.ring.size // 2):
            for i, way in self.each(hop):
                self.copy(i, way, hop).wait_send()


def piece_rows(piece, step):
    return pl.ds(piece * step if isinstance(piece, int) else pl.multiple_of(piece * step, step), step)


class RowGather:
    def __init__(self, chip, own, out, send, recv):
        self.chip, self.own, self.out, self.send, self.recv = chip, own, out, send, recv
        self.step = own.shape[0] // ROW_PIECES

    def copy(self, kind, piece):
        rows = piece_rows(piece, self.step)
        chip = self.chip
        owner = chip.peer if kind == 2 else chip.me
        target = self.out.at[owner, rows]
        device = chip.peer if kind == 0 else chip.mate
        return remote(
            target if kind == 2 else self.own.at[rows],
            target,
            self.send.at[kind, piece],
            self.recv.at[kind, piece],
            {"tensor": device},
        )

    def start(self):
        for kind in (0, 1):
            for piece in range(ROW_PIECES):
                self.copy(kind, piece).start()
        self.out[self.chip.me] = self.own[...]

    def relay(self, piece):
        self.copy(0, piece).wait_recv()
        self.copy(2, piece).start()

    def finish(self):
        for kind in (1, 2):
            for piece in range(ROW_PIECES):
                self.copy(kind, piece).wait_recv()
        for kind in (0, 1, 2):
            for piece in range(ROW_PIECES):
                self.copy(kind, piece).wait_send()


class RowScatter:
    def __init__(self, chip, parts, landing, send, recv):
        self.chip, self.parts, self.landing, self.send, self.recv = chip, parts, landing, send, recv
        self.pieces = send.shape[1]
        self.step = parts.shape[1] // self.pieces

    def rows(self, piece):
        return piece_rows(piece, self.step)

    def copy(self, kind, piece):
        chip, rows = self.chip, self.rows(piece)
        source = (
            self.parts.at[chip.across, rows],
            self.landing.at[0, rows],
            self.parts.at[chip.mate, rows],
        )[kind]
        return remote(
            source,
            self.landing.at[kind, rows],
            self.send.at[kind, piece],
            self.recv.at[kind, piece],
            {"tensor": chip.peer if kind == 1 else chip.mate},
        )

    def start(self):
        for kind in (0, 2):
            for piece in range(ROW_PIECES):
                self.copy(kind, piece).start()

    def relay(self, piece):
        rows = self.rows(piece)
        self.copy(0, piece).wait_recv()
        total = self.landing[0, rows].astype(jnp.float32) + self.parts[self.chip.peer, rows].astype(
            jnp.float32
        )
        self.landing[0, rows] = total.astype(self.landing.dtype)
        self.copy(1, piece).start()

    def total(self, piece):
        rows = self.rows(piece)
        self.copy(2, piece).wait_recv()
        self.copy(1, piece).wait_recv()
        return (
            self.parts[self.chip.me, rows].astype(jnp.float32)
            + self.landing[1, rows].astype(jnp.float32)
            + self.landing[2, rows].astype(jnp.float32)
        )

    def finish(self):
        for kind in (0, 1, 2):
            for piece in range(self.pieces):
                self.copy(kind, piece).wait_send()


class Meet:
    def __init__(self, chip, held, send, recv):
        self.chip, self.held, self.send, self.recv = chip, held, send, recv
        self.others = (chip.mate, chip.peer, chip.across)

    def copies(self):
        own = self.held.at[self.chip.me]
        for k, other in enumerate(self.others):
            yield remote(own, own, self.send.at[k], self.recv.at[k], {"tensor": other})

    def start(self, value):
        self.held[self.chip.me] = value
        for copy in self.copies():
            copy.start()

    def total(self):
        for copy in self.copies():
            copy.wait_recv()
        return (self.held[0] + self.held[1]) + (self.held[2] + self.held[3])

    def finish(self):
        for copy in self.copies():
            copy.wait_send()


def meet_sems():
    return [pltpu.SemaphoreType.DMA((3,))] * 2


def row_sems(pieces=ROW_PIECES):
    return [pltpu.SemaphoreType.DMA((3, pieces))] * 2


def ring_sems(count, size):
    return [pltpu.SemaphoreType.DMA((count, 2, size // 2))] * 2


def comm_params(collective_id):
    return pltpu.CompilerParams(
        collective_id=collective_id, has_side_effects=True, vmem_limit_bytes=VMEM_GRANT
    )


def gather_rows(own, collective_id):
    def kernel(own_ref, out_ref, send, recv):
        chip = Chip()
        greet(({"tensor": chip.mate}, {"tensor": chip.peer}))
        rows = RowGather(chip, own_ref, out_ref, send, recv)
        rows.start()
        for piece in range(ROW_PIECES):
            rows.relay(piece)
        rows.finish()

    out = pl.pallas_call(
        kernel,
        out_shape=jax.ShapeDtypeStruct((4, *own.shape), own.dtype),
        in_specs=[VMEM],
        out_specs=VMEM,
        scratch_shapes=row_sems(),
        compiler_params=comm_params(collective_id),
        name="gather_rows",
    )(own)
    return out.reshape(4 * own.shape[0], own.shape[1])


def enter(slots, own, shards, shift_rows, size, collective_id):
    count = len(shards)
    block, model = own.shape
    group = 4 * block
    width = shards[0].shape[1] // 3
    tile = 256
    tiles = group // tile
    low, f32 = jnp.bfloat16, jnp.float32

    def kernel(*refs):
        slots_ref, own_ref, shard_refs = refs[0], refs[1], refs[2 : 2 + count]
        refs = refs[2 + count :]
        out_refs, (slotted_ref, qkv_ref) = refs[:count], refs[count : count + 2]
        rows_ref, total, shift, ring_send, ring_recv, row_send, row_recv = refs[count + 2 :]
        ring, chip = Ring(size), Chip()
        greet(
            (
                {"dp": ring.targets[0]},
                {"dp": ring.targets[1]},
                {"tensor": chip.mate},
                {"tensor": chip.peer},
            )
        )
        rows = RowGather(chip, own_ref, rows_ref, row_send, row_recv)
        weights = RingGather(ring, shard_refs, out_refs, ring_send, ring_recv)
        rows.start()
        weights.start()

        half = block // 2

        def pick(here, owner, start, length):
            first = pl.multiple_of(owner * block, block) + start
            wanted = here * tile + lax.broadcasted_iota(jnp.int32, (tile, length), 0)
            chosen = jnp.where(slots_ref[:, pl.ds(first, length)] == wanted, 1.0, 0.0).astype(low)
            return jnp.dot(chosen, rows_ref[owner, start : start + length], preferred_element_type=f32)

        def near(here, carry):
            @pl.when(here == tiles // 2)
            def _():
                rows.relay(0)

            total[piece_rows(here, tile)] = pick(here, chip.me, 0, block) + pick(here, chip.mate, 0, block)
            return carry

        def middle(here, carry):
            total[piece_rows(here, tile)] += pick(here, chip.peer, 0, half) + pick(here, chip.across, 0, half)
            return carry

        def far(here, carry):
            @pl.when(here == tiles // 2)
            def _():
                weights.relay(3)

            at = piece_rows(here, tile)
            moved = pick(here, chip.peer, half, half) + pick(here, chip.across, half, half)
            slotted_ref[at] = (total[at] + moved).astype(low)
            return carry

        for piece in range(ROW_PIECES):
            rows.copy(1, piece).wait_recv()
        lax.fori_loop(0, tiles, near, 0)
        rows.relay(1)
        weights.relay(1)
        for piece in range(ROW_PIECES // 2):
            rows.copy(2, piece).wait_recv()
        lax.fori_loop(0, tiles, middle, 0)
        rows.relay(2)
        weights.relay(2)
        rows.relay(3)
        for piece in range(ROW_PIECES // 2, ROW_PIECES):
            rows.copy(2, piece).wait_recv()
        lax.fori_loop(0, tiles, far, 0)
        weights.relay(4, (0, count - 1))
        side, span = out_refs[-1], shards[-1].shape[1]
        shift[...] = jnp.zeros_like(shift)
        for j in range(width // span):
            owner = chip.me * (width // span) + j
            for part, row in shift_rows:
                at = part * width + j * span
                shift[:, at : at + span] = side[owner, row : row + 1].astype(f32)

        def project(here, carry):
            at = piece_rows(here, block)
            weight = out_refs[0][...].reshape(model, 3 * width)
            out = jnp.dot(slotted_ref[at], weight, preferred_element_type=f32) + shift[...]
            qkv_ref[at] = out.astype(low)
            return carry

        lax.fori_loop(0, 4, project, 0)
        weights.relay(4, tuple(range(1, count - 1)))
        for kind in (0, 1, 2):
            for piece in range(ROW_PIECES):
                rows.copy(kind, piece).wait_send()
        weights.finish()

    *gathered, slotted, qkv = pl.pallas_call(
        kernel,
        out_shape=[jax.ShapeDtypeStruct((size, *s.shape), s.dtype) for s in shards]
        + [jax.ShapeDtypeStruct((group, model), low), jax.ShapeDtypeStruct((group, 3 * width), low)],
        in_specs=[VMEM] * (count + 2),
        out_specs=[VMEM] * (count + 2),
        scratch_shapes=[
            pltpu.VMEM((4, block, model), low),
            pltpu.VMEM((group, model), f32),
            pltpu.VMEM((1, 3 * width), f32),
        ]
        + ring_sems(count, size)
        + row_sems(),
        compiler_params=comm_params(collective_id),
        name="enter",
    )(slots.reshape(1, group), own, *shards)
    return gathered, slotted, qkv


def attend(qkv, lengths, out_weight, shards, size, collective_id):
    ringed = size <= RING_MAX
    given = shards if ringed else []
    count = len(given)
    keys, width = qkv.shape[0], qkv.shape[1] // 3
    heads, model = width // HEAD_DIM, out_weight.shape[0]
    own_rows, pieces = keys // 4, 2
    block = own_rows // pieces
    factor = HEAD_DIM ** (-0.5)
    low, f32 = jnp.bfloat16, jnp.float32

    def kernel(*refs):
        len_ref, qkv_ref, weight_ref = refs[:3]
        shard_refs, refs = refs[3 : 3 + count], refs[3 + count :]
        out_ref, exact_ref, total_ref, sum_ref = refs[:4]
        full_refs, refs = refs[4 : 4 + count], refs[4 + count :]
        key_side, value_side, parts, landing, row_send, row_recv, *refs = refs
        chip = Chip()
        neighbours = ({"tensor": chip.mate}, {"tensor": chip.peer})
        if ringed:
            ring = Ring(size)
            weights = RingGather(ring, shard_refs, full_refs, *refs)
            neighbours += ({"dp": ring.targets[0]}, {"dp": ring.targets[1]})
        greet(neighbours)
        scatter = RowScatter(chip, parts, landing, row_send, row_recv)
        if ringed:
            weights.start()
        fill = key_fill(len_ref[0], keys)
        for h in range(heads):
            at = width + h * HEAD_DIM
            key_side[h, :, :HEAD_DIM] = qkv_ref[:, at : at + HEAD_DIM]
            key_side[h, :, HEAD_DIM:] = beside(keys, [fill])
            value_side[h, :, :HEAD_DIM] = qkv_ref[:, at + width : at + width + HEAD_DIM]
            value_side[h, :, HEAD_DIM:] = beside(keys, [1.0])
        ones = beside(block, [1.0])
        lane = lax.broadcasted_iota(jnp.int32, (block, WIDE), 1)

        def one(step, carry):
            near, odd = step // 4, lax.rem(step, 2)
            piece = lax.rem(step, 4) // 2
            owner = 2 * lax.rem(chip.me // 2 + 1 - near, 2) + lax.rem(lax.rem(chip.me, 2) + 1 - odd, 2)
            here = pl.ds(pl.multiple_of(owner * own_rows + piece * block, block), block)
            totals = jnp.zeros((block, WIDE), f32)
            for h in range(heads):
                lanes = slice(h * HEAD_DIM, (h + 1) * HEAD_DIM)
                query = jnp.concatenate([qkv_ref[here, lanes] * low(factor), ones], axis=1)
                scores = times_transposed(query, key_side[h])
                top = jnp.max(scores, axis=-1, keepdims=True)
                soft = jnp.exp(scores - top).astype(low)
                mixed = jnp.dot(soft, value_side[h], preferred_element_type=f32)
                total = mixed[:, HEAD_DIM : HEAD_DIM + 1]
                result = mixed[:, :HEAD_DIM] / total
                exact_ref[here, lanes] = result
                out_ref[here, lanes] = result.astype(low)
                totals = jnp.where(lane == h, top + jnp.log(total), totals)
            total_ref[here] = totals
            parts[owner, scatter.rows(piece)] = times_transposed(out_ref[here], weight_ref[...]).astype(low)

            @pl.when((near == 0) & (odd == 0))
            def _():
                scatter.copy(0, piece).start()

            @pl.when((near == 0) & (odd == 1))
            def _():
                scatter.relay(piece)

            @pl.when((near == 1) & (odd == 0))
            def _():
                scatter.copy(2, piece).start()

            if ringed:
                for hop in range(1, size // 2 + 1):

                    @pl.when(step == 2 * hop - 1)
                    def _():
                        weights.relay(hop)

            return carry

        lax.fori_loop(0, 4 * pieces, one, 0)
        for piece in range(pieces):
            sum_ref[scatter.rows(piece)] = scatter.total(piece)
        scatter.finish()
        if ringed:
            weights.finish()

    context, exact, totals, summed, *gathered = pl.pallas_call(
        kernel,
        out_shape=[
            jax.ShapeDtypeStruct((keys, width), low),
            jax.ShapeDtypeStruct((keys, width), f32),
            jax.ShapeDtypeStruct((keys, WIDE), f32),
            jax.ShapeDtypeStruct((own_rows, model), f32),
        ]
        + [jax.ShapeDtypeStruct((size, *s.shape), s.dtype) for s in given],
        in_specs=[pl.BlockSpec(memory_space=pltpu.SMEM)] + [VMEM] * (2 + count),
        out_specs=[VMEM] * (4 + count),
        scratch_shapes=[
            pltpu.VMEM((heads, keys, WIDE), low),
            pltpu.VMEM((heads, keys, WIDE), low),
            pltpu.VMEM((4, own_rows, model), low),
            pltpu.VMEM((3, own_rows, model), low),
        ]
        + row_sems(pieces)
        + (ring_sems(count, size) if ringed else []),
        compiler_params=comm_params(collective_id),
        name="attend",
    )(lengths, qkv, out_weight, *given)
    if not ringed:
        gathered = [lax.all_gather(shard, "dp") for shard in shards]
    return context, exact, totals, summed, gathered


def turned(left, right):
    return lax.dot_general(
        left, right, (((0,), (0,)), ((), ())), preferred_element_type=jnp.float32
    )


def around_rows(chip, gather, scatter, work, keep, middle=None, end=None):
    parts = scatter.parts

    def own(piece, carry):
        rows = scatter.rows(piece)
        keep[rows] = work(chip.me, rows)
        return carry

    def near(piece, carry):
        rows = scatter.rows(piece)
        gather.copy(1, piece).wait_recv()
        parts[chip.mate, rows] = work(chip.mate, rows).astype(parts.dtype)
        scatter.copy(2, piece).start()
        return carry

    def far(piece, carry):
        rows = scatter.rows(piece)
        gather.relay(piece)
        parts[chip.peer, rows] = work(chip.peer, rows).astype(parts.dtype)

        @pl.when(piece > 0)
        def _():
            scatter.relay(piece - 1)

        gather.copy(2, piece).wait_recv()
        parts[chip.across, rows] = work(chip.across, rows).astype(parts.dtype)
        scatter.copy(0, piece).start()
        return carry

    def last(piece, carry):
        rows = scatter.rows(piece)
        scatter.copy(2, piece).wait_recv()
        scatter.copy(1, piece).wait_recv()
        keep[rows] += scatter.landing[1, rows].astype(jnp.float32) + scatter.landing[2, rows].astype(
            jnp.float32
        )
        return carry

    gather.start()
    lax.fori_loop(0, ROW_PIECES, own, 0)
    lax.fori_loop(0, ROW_PIECES, near, 0)
    if middle is not None:
        middle()
    lax.fori_loop(0, ROW_PIECES, far, 0)
    scatter.relay(ROW_PIECES - 1)
    if end is not None:
        end()
    lax.fori_loop(0, ROW_PIECES, last, 0)
    for copies in (gather, scatter):
        for kind in (0, 1, 2):
            for piece in range(ROW_PIECES):
                copies.copy(kind, piece).wait_send()


def feed_forward(own, up_weight, shift, down_weight, collective_id):
    rows, width = own.shape
    hidden_width = up_weight.shape[1]
    low, f32 = jnp.bfloat16, jnp.float32

    def kernel(
        own_ref, up_ref, shift_ref, down_ref, rows_ref, hidden_ref, slope_ref, out_ref, parts, landing, *sems
    ):
        chip = Chip()
        greet(({"tensor": chip.mate}, {"tensor": chip.peer}))
        gather = RowGather(chip, own_ref, rows_ref, *sems[:2])
        scatter = RowScatter(chip, parts, landing, *sems[2:])

        def work(owner, rows):
            pre = jnp.dot(rows_ref[owner, rows], up_ref[...], preferred_element_type=f32) + shift_ref[...]
            cdf = 0.5 * (1.0 + lax.erf(pre * 0.7071067811865476))
            hidden = (pre * cdf).astype(low)
            hidden_ref[owner, rows] = hidden
            slope = cdf + pre * (jnp.exp(-0.5 * pre * pre) * 0.3989422804014327)
            slope_ref[owner, rows] = slope.astype(low)
            return times_transposed(hidden, down_ref[...])

        around_rows(chip, gather, scatter, work, out_ref)

    return pl.pallas_call(
        kernel,
        out_shape=[
            jax.ShapeDtypeStruct((4, rows, width), low),
            jax.ShapeDtypeStruct((4, rows, hidden_width), low),
            jax.ShapeDtypeStruct((4, rows, hidden_width), low),
            jax.ShapeDtypeStruct((rows, width), f32),
        ],
        in_specs=[VMEM] * 4,
        out_specs=[VMEM] * 4,
        scratch_shapes=[pltpu.VMEM((4, rows, width), low), pltpu.VMEM((3, rows, width), low)]
        + row_sems() * 2,
        compiler_params=comm_params(collective_id),
        name="feed_forward",
    )(own, up_weight, shift.reshape(1, -1), down_weight)


def feed_back(own, slope, mid_rows, hidden, up_weight, down_weight, collective_id):
    rows, width = own.shape
    hidden_width = up_weight.shape[1]
    low, f32 = jnp.bfloat16, jnp.float32
    band = 256

    def kernel(
        own_ref,
        slope_ref,
        mid_ref,
        hidden_ref,
        up_ref,
        down_ref,
        out_ref,
        grad_up_ref,
        grad_down_ref,
        shift_ref,
        rows_ref,
        dpre_ref,
        up_sum,
        down_sum,
        parts,
        landing,
        *sems,
    ):
        chip = Chip()
        greet(({"tensor": chip.mate}, {"tensor": chip.peer}))
        gather = RowGather(chip, own_ref, rows_ref, *sems[:2])
        scatter = RowScatter(chip, parts, landing, *sems[2:])
        shift_ref[...] = jnp.zeros_like(shift_ref)

        def work(owner, rows):
            dhidden = jnp.dot(rows_ref[owner, rows], down_ref[...], preferred_element_type=f32)
            dpre = (dhidden * slope_ref[owner, rows].astype(f32)).astype(low)
            dpre_ref[owner, rows] = dpre
            shift_ref[...] += jnp.sum(dpre.astype(f32), axis=0, keepdims=True)
            return times_transposed(dpre, up_ref[...])

        def grads(owners, first):
            def one(tile, carry):
                columns = pl.ds(pl.multiple_of(tile * band, band), band)
                for left, right, total in (
                    (mid_ref, dpre_ref, up_sum),
                    (rows_ref, hidden_ref, down_sum),
                ):
                    term = turned(left[owners[0], :, columns], right[owners[0]])
                    term += turned(left[owners[1], :, columns], right[owners[1]])
                    total[columns] = term if first else total[columns] + term
                return carry

            return lambda: lax.fori_loop(0, width // band, one, 0)

        around_rows(
            chip,
            gather,
            scatter,
            work,
            out_ref,
            grads((chip.me, chip.mate), True),
            grads((chip.peer, chip.across), False),
        )
        grad_up_ref[...] = up_sum[...].astype(low)
        grad_down_ref[...] = down_sum[...].astype(low)

    return pl.pallas_call(
        kernel,
        out_shape=[
            jax.ShapeDtypeStruct((rows, width), f32),
            jax.ShapeDtypeStruct((width, hidden_width), low),
            jax.ShapeDtypeStruct((width, hidden_width), low),
            jax.ShapeDtypeStruct((1, hidden_width), f32),
        ],
        in_specs=[VMEM] * 6,
        out_specs=[VMEM] * 4,
        scratch_shapes=[
            pltpu.VMEM((4, rows, width), low),
            pltpu.VMEM((4, rows, hidden_width), low),
            pltpu.VMEM((width, hidden_width), f32),
            pltpu.VMEM((width, hidden_width), f32),
            pltpu.VMEM((4, rows, width), low),
            pltpu.VMEM((3, rows, width), low),
        ]
        + row_sems() * 2,
        compiler_params=comm_params(collective_id),
        name="feed_back",
    )(own, slope, mid_rows, hidden, up_weight, down_weight)


def enter_slots(slots, arrived, weight, shift):
    group, width = arrived.shape
    block = 256

    def kernel(slots_ref, arrived_ref, weight_ref, shift_ref, rows_ref, out_ref):
        first = pl.program_id(0) * block
        wanted = first + lax.broadcasted_iota(jnp.int32, (block, group), 0)
        pick = jnp.where(slots_ref[...] == wanted, 1.0, 0.0).astype(jnp.bfloat16)
        rows = jnp.dot(pick, arrived_ref[...], preferred_element_type=jnp.float32).astype(jnp.bfloat16)
        rows_ref[...] = rows
        out = jnp.dot(rows, weight_ref[...], preferred_element_type=jnp.float32) + shift_ref[...]
        out_ref[...] = out.astype(jnp.bfloat16)

    return pl.pallas_call(
        kernel,
        grid=(group // block,),
        in_specs=[VMEM] * 4,
        out_specs=[
            pl.BlockSpec((block, width), lambda i: (i, 0)),
            pl.BlockSpec((block, weight.shape[1]), lambda i: (i, 0)),
        ],
        out_shape=[
            jax.ShapeDtypeStruct((group, width), jnp.bfloat16),
            jax.ShapeDtypeStruct((group, weight.shape[1]), jnp.bfloat16),
        ],
        name="enter_slots",
    )(slots.reshape(1, group), arrived, weight, shift.reshape(1, -1))


def attend_back(own, out_weight, context, qkv, exact, totals, lengths, parts, size, collective_id):
    ringed = size <= RING_MAX
    given = parts if ringed else []
    count = len(given)
    block, model = own.shape
    keys, width = qkv.shape[0], qkv.shape[1] // 3
    heads = width // HEAD_DIM
    factor = HEAD_DIM ** (-0.5)
    low, f32 = jnp.bfloat16, jnp.float32

    def kernel(*refs):
        len_ref, own_ref, weight_ref, context_ref, qkv_ref, exact_ref, total_ref = refs[:7]
        part_refs, refs = refs[7 : 7 + count], refs[7 + count :]
        out_ref, column_ref, grad_ref = refs[:3]
        sum_refs, refs = refs[3 : 3 + count], refs[3 + count :]
        rows_ref, key_side, value_side, key_turned, sums, grad_sum, row_send, row_recv = refs[:8]
        refs = refs[8:]
        chip = Chip()
        neighbours = ({"tensor": chip.mate}, {"tensor": chip.peer})
        if ringed:
            landing, (held, ring_send, ring_recv, meet_send, meet_recv) = refs[:count], refs[count:]
            ring = Ring(size)
            meet = Meet(chip, held, meet_send, meet_recv)
            grads = RingScatter(ring, part_refs, landing, ring_send, ring_recv)
            neighbours += ({"tensor": chip.across},)
            neighbours += ({"dp": ring.targets[0]}, {"dp": ring.targets[1]})
        greet(neighbours)
        rows = RowGather(chip, own_ref, rows_ref, row_send, row_recv)
        rows.start()
        if ringed:
            grads.start()
        fill = key_fill(len_ref[0], keys)
        for h in range(heads):
            at = width + h * HEAD_DIM
            key = qkv_ref[:, at : at + HEAD_DIM]
            key_side[h, :, :HEAD_DIM] = key
            key_side[h, :, HEAD_DIM:] = beside(keys, [fill, 1.0, 1.0, 1.0])
            key_turned[h] = (key * low(factor)).T
            value_side[h, :, :HEAD_DIM] = qkv_ref[:, at + width : at + width + HEAD_DIM]
            value_side[h, :, HEAD_DIM:] = beside(keys, [1.0, 1.0, 1.0])
        sums[...] = jnp.zeros_like(sums)
        grad_sum[...] = jnp.zeros_like(grad_sum)

        def one(step, carry):
            owner = 2 * lax.rem(chip.me // 2 + step // 2, 2) + lax.rem(lax.rem(chip.me, 2) + step, 2)

            @pl.when(step == 1)
            def _():
                for piece in range(ROW_PIECES):
                    rows.copy(1, piece).wait_recv()

            @pl.when(step == 3)
            def _():
                for piece in range(ROW_PIECES):
                    rows.copy(2, piece).wait_recv()

            first = pl.multiple_of(owner * block, block)
            here = pl.ds(first, block)
            drows = rows_ref[owner]
            dcontext = jnp.dot(drows, weight_ref[...], preferred_element_type=f32).astype(low)
            grad_sum[...] += turned(drows, context_ref[here])
            blank = jnp.zeros((block, HEAD_DIM), low)
            for h in range(heads):
                lanes = slice(h * HEAD_DIM, (h + 1) * HEAD_DIM)
                dout = dcontext[:, lanes]
                delta = jnp.sum(dout.astype(f32) * exact_ref[here, lanes], axis=-1, keepdims=True)
                query = qkv_ref[here, lanes] * low(factor)
                query_wide = jnp.concatenate(
                    [query, beside(block, [1.0, *thirds(-total_ref[here, h : h + 1])])], axis=1
                )
                dout_wide = jnp.concatenate([dout, beside(block, thirds(-delta))], axis=1)
                soft = jnp.exp(times_transposed(key_side[h], query_wide))
                dsoft = times_transposed(value_side[h], dout_wide)
                dscore = (soft * dsoft).astype(low)
                soft = soft.astype(low)
                sums[h] += jnp.dot(
                    soft, jnp.concatenate([dout, blank], axis=1), preferred_element_type=f32
                ) + jnp.dot(
                    dscore, jnp.concatenate([blank, query], axis=1), preferred_element_type=f32
                )
                dquery = jnp.dot(key_turned[h], dscore, preferred_element_type=f32)
                out_ref[here, lanes] = dquery.T.astype(low)
                if ringed and h == 0:

                    @pl.when(step == 3)
                    def _():
                        grads.relay(size // 2)
                        meet.start(grads.total(count - 1))

                if ringed and h == heads - 1:
                    for hop in range(1, size // 2):

                        @pl.when(step == hop - 1)
                        def _():
                            grads.relay(hop)

            @pl.when(step < 2)
            def _():
                rows.relay(2 * step)
                rows.relay(2 * step + 1)

            return carry

        lax.fori_loop(0, 4, one, 0)
        for h in range(heads):
            both = sums[h].astype(low)
            at = width + h * HEAD_DIM
            out_ref[:, at : at + HEAD_DIM] = both[:, HEAD_DIM:]
            out_ref[:, at + width : at + width + HEAD_DIM] = both[:, :HEAD_DIM]
        column_ref[...] = jnp.sum(out_ref[...].astype(f32), axis=0, keepdims=True)
        grad_ref[...] = grad_sum[...].astype(low)
        if ringed:
            sum_refs[0][...] = grads.total(0)
            sum_refs[1][...] = grads.total(1).T
            sum_refs[2][...] = meet.total()
            meet.finish()
            grads.finish()
        for kind in (0, 1, 2):
            for piece in range(ROW_PIECES):
                rows.copy(kind, piece).wait_send()

    scratch = [
        pltpu.VMEM((4, block, model), low),
        pltpu.VMEM((heads, keys, WIDE), low),
        pltpu.VMEM((heads, keys, WIDE), low),
        pltpu.VMEM((heads, HEAD_DIM, keys), low),
        pltpu.VMEM((heads, keys, WIDE), f32),
        pltpu.VMEM((model, width), f32),
        *row_sems(),
    ]
    if ringed:
        scratch += [pltpu.VMEM((size - 1, *p.shape[1:]), p.dtype) for p in parts]
        scratch += [pltpu.VMEM((4, *parts[-1].shape[1:]), f32)]
        scratch += ring_sems(count, size) + meet_sems()
    dqkv, columns, grad_out, *summed = pl.pallas_call(
        kernel,
        out_shape=[
            jax.ShapeDtypeStruct((keys, 3 * width), low),
            jax.ShapeDtypeStruct((1, 3 * width), f32),
            jax.ShapeDtypeStruct((model, width), low),
        ]
        + [
            jax.ShapeDtypeStruct(p.shape[:0:-1] if i == 1 else p.shape[1:], f32)
            for i, p in enumerate(given)
        ],
        in_specs=[pl.BlockSpec(memory_space=pltpu.SMEM)] + [VMEM] * (6 + count),
        out_specs=[VMEM] * (3 + count),
        scratch_shapes=scratch,
        compiler_params=comm_params(collective_id),
        name="attend_back",
    )(lengths, own, out_weight, context, qkv, exact, totals, *given)
    if not ringed:
        summed = [lax.psum_scatter(p.astype(f32), "dp", scatter_dimension=0) for p in parts]
        summed = [summed[0], summed[1].T, lax.psum(summed[2], "tensor")]
    return dqkv, columns[0], grad_out, summed


def finish(rows, dqkv, weight, resid, slots, parts, size, collective_id):
    ringed = size <= RING_MAX
    given = parts if ringed else []
    count = len(given) + 1
    group, model = rows.shape
    columns = dqkv.shape[1]
    own_rows = group // 4
    pieces, band = 2, model // 2
    low, f32 = jnp.bfloat16, jnp.float32

    def kernel(*refs):
        rows_ref, dqkv_ref, weight_ref, resid_ref, slots_ref = refs[:5]
        part_refs, refs = refs[5 : 4 + count], refs[4 + count :]
        results = 6 if ringed else 2
        own_ref, grad_ref, *sum_refs = refs[:results]
        through, leaving, row_landing, row_send, row_recv, *refs = refs[results:]
        chip = Chip()
        neighbours = ({"tensor": chip.mate}, {"tensor": chip.peer})
        if ringed:
            local, landing, (held, *sems) = refs[0], refs[1 : 1 + count], refs[1 + count :]
            ring = Ring(size)
            early = RingScatter(ring, part_refs, landing[: count - 1], *sems[:2])
            late = RingScatter(ring, (local,), landing[count - 1 :], *sems[2:4])
            meet = Meet(chip, held, *sems[4:])
            neighbours += ({"tensor": chip.across},)
            neighbours += ({"dp": ring.targets[0]}, {"dp": ring.targets[1]})
        greet(neighbours)
        scatter = RowScatter(chip, leaving, row_landing, row_send, row_recv)
        if ringed:
            early.start()
        half = group // 2

        def spread(part, carry):
            here = pl.ds(pl.multiple_of(part * half, half), half)
            through[here] = times_transposed(dqkv_ref[here], weight_ref[...]).astype(low)
            return carry

        lax.fori_loop(0, 2, spread, 0)
        mine = pl.ds(pl.multiple_of(chip.me * own_rows, own_rows), own_rows)
        through[mine] = (
            times_transposed(dqkv_ref[mine], weight_ref[...]) + resid_ref[...]
        ).astype(low)
        step = own_rows // pieces
        slot = lax.broadcasted_iota(jnp.int32, (step, group), 1)

        def leave(owner, piece):
            first = pl.multiple_of(owner * own_rows + piece * step, step)
            pick = jnp.where(slots_ref[pl.ds(first, step)] == slot, 1.0, 0.0).astype(low)
            moved = jnp.dot(pick, through[...], preferred_element_type=f32).astype(low)
            leaving[owner, scatter.rows(piece)] = moved

        def outward(piece, carry):
            leave(chip.across, piece)
            scatter.copy(0, piece).start()
            leave(chip.peer, piece)
            scatter.relay(piece)
            return carry

        def inward(piece, carry):
            leave(chip.mate, piece)
            scatter.copy(2, piece).start()
            leave(chip.me, piece)
            return carry

        lax.fori_loop(0, 1, outward, 0)
        if ringed:
            early.relay(1)
        for tile in range(2):
            grad = turned(rows_ref[:, tile * band : (tile + 1) * band], dqkv_ref[...]).astype(low)
            if ringed:
                half_ring = size // 2
                local[tile * half_ring : (tile + 1) * half_ring] = grad.reshape(
                    half_ring, band // half_ring, columns
                )
            else:
                grad_ref[tile * band : (tile + 1) * band] = grad
        if ringed:
            late.start()
            early.relay(2)
        lax.fori_loop(1, pieces, outward, 0)
        if ringed:
            early.relay(3)
            late.relay(1)
        lax.fori_loop(0, pieces, inward, 0)
        if ringed:
            early.relay(4)
            meet.start(early.total(1))
            for hop in range(2, size // 2 + 1):
                late.relay(hop)
            out_sum, gain_sum, bias_sum, shift_sum = sum_refs
            out_sum[...] = early.total(0).T
            side = meet.total()
            gain_sum[...] = side[:2]
            bias_sum[...] = side[2:8]
            shift_sum[...] = side[8:]
        for piece in range(pieces):
            own_ref[scatter.rows(piece)] = scatter.total(piece)
        if ringed:
            total = late.total(0)
            for c in range(3):
                grad_ref[c] = total[:, c * columns // 3 : (c + 1) * columns // 3]
            meet.finish()
            early.finish()
            late.finish()
        scatter.finish()

    scratch = [
        pltpu.VMEM((group, model), low),
        pltpu.VMEM((4, own_rows, model), low),
        pltpu.VMEM((3, own_rows, model), low),
        *row_sems(pieces),
    ]
    if ringed:
        local = jax.ShapeDtypeStruct((size, model // size, columns), low)
        scratch += [pltpu.VMEM(local.shape, low)]
        scratch += [pltpu.VMEM((size - 1, *p.shape[1:]), p.dtype) for p in (*parts, local)]
        scratch += [pltpu.VMEM((4, *parts[-1].shape[1:]), f32)]
        scratch += ring_sems(count - 1, size) + ring_sems(1, size) + meet_sems()
        shapes = [(3, model // size, columns // 3), parts[0].shape[:0:-1]]
        shapes += [(k, model // size) for k in (2, 6, parts[1].shape[1] - 8)]
        results = [jax.ShapeDtypeStruct(shape, f32) for shape in shapes]
    else:
        results = [jax.ShapeDtypeStruct((model, columns), low)]
    own, grad, *summed = pl.pallas_call(
        kernel,
        out_shape=[jax.ShapeDtypeStruct((own_rows, model), f32), *results],
        in_specs=[VMEM] * (4 + count),
        out_specs=[VMEM] * (1 + len(results)),
        scratch_shapes=scratch,
        compiler_params=comm_params(collective_id),
        name="finish",
    )(rows, dqkv, weight, resid, slots.reshape(group, 1), *given)
    if not ringed:
        grad = grad.astype(f32).reshape(size, model // size, columns)
        grad, *summed = [lax.psum_scatter(p.astype(f32), "dp", scatter_dimension=0) for p in (grad, *parts)]
        side = lax.psum(summed[1], "tensor")
        grad = grad.reshape(model // size, 3, columns // 3).transpose(1, 0, 2)
        summed = [summed[0].T, side[:2], side[2:8], side[8:]]
    return own, grad, summed


def head(first_norm, ffn_part, vectors, proj_weight, cotangent, keep):
    rows, width = first_norm.shape
    proj = proj_weight.shape[1]
    low, f32 = jnp.bfloat16, jnp.float32
    tile = 128

    def kernel(
        norm_ref, part_ref, vector_ref, weight_ref, cot_ref, keep_ref, emb_ref, dsum_ref, low_ref, grad_ref, side_ref
    ):
        grad_ref[...] = jnp.zeros_like(grad_ref)
        side_ref[...] = jnp.zeros_like(side_ref)
        extra, gain, shift = (vector_ref[i : i + 1] for i in range(3))

        def one(piece, carry):
            at = piece_rows(piece, tile)
            values = norm_ref[at] + part_ref[at] + extra
            center = values - jnp.mean(values, axis=-1, keepdims=True)
            spread = jnp.mean(center * center, axis=-1, keepdims=True)
            scale = lax.rsqrt(spread + EPS_NORM)
            unit = center * scale
            second = (unit * gain + shift).astype(low)
            e = jnp.dot(second, weight_ref[...], preferred_element_type=f32)
            keep_rows = keep_ref[at]
            inverse = lax.rsqrt(jnp.sum(e * e, axis=-1, keepdims=True) + EPS_UNIT)
            emb_ref[at] = e * inverse * keep_rows
            cot = cot_ref[at].astype(f32) * keep_rows
            along = jnp.sum(cot * e, axis=-1, keepdims=True)
            de = (cot * inverse - e * (inverse * inverse * inverse * along)).astype(low)
            grad_ref[...] += turned(second, de)
            dnorm = times_transposed(de, weight_ref[...])
            dunit = dnorm * gain
            dsum = scale * (
                dunit
                - jnp.mean(dunit, axis=-1, keepdims=True)
                - unit * jnp.mean(dunit * unit, axis=-1, keepdims=True)
            )
            dsum_ref[at] = dsum
            low_ref[at] = dsum.astype(low)
            for i, term in enumerate((dnorm * unit, dnorm, dsum)):
                side_ref[i : i + 1] += jnp.sum(term, axis=0, keepdims=True)
            return carry

        lax.fori_loop(0, rows // tile, one, 0)

    return pl.pallas_call(
        kernel,
        out_shape=[
            jax.ShapeDtypeStruct((rows, proj), f32),
            jax.ShapeDtypeStruct((rows, width), f32),
            jax.ShapeDtypeStruct((rows, width), low),
            jax.ShapeDtypeStruct((width, proj), f32),
            jax.ShapeDtypeStruct((3, width), f32),
        ],
        in_specs=[VMEM] * 6,
        out_specs=[VMEM] * 5,
        compiler_params=pltpu.CompilerParams(vmem_limit_bytes=16 << 20),
        name="head",
    )(first_norm, ffn_part, vectors, proj_weight, cotangent, keep)


def body(
    tokens,
    lengths,
    arrival_slots,
    w_qkv,
    w_out,
    w_up,
    w_down,
    w_proj,
    norm_gains,
    biases,
    up_bias,
    cotangent,
):
    tensor_size = lax.axis_size("tensor")
    tensor_pos = lax.axis_index("tensor")
    own_rows = tokens.shape[0]
    group_rows = own_rows * tensor_size
    slot_order = arrival_slots[0]
    size = lax.axis_size("dp")
    part_rows, width_local = w_qkv.shape[1:]
    low = jnp.bfloat16
    width = size * part_rows
    flat = lambda full: full.reshape(width, full.shape[2])
    shards = [
        w_qkv.astype(low).transpose(1, 0, 2).reshape(part_rows, 3 * width_local),
        w_up.astype(low),
        w_out.astype(low).T,
        jnp.concatenate(
            [norm_gains.astype(low), biases.astype(low), up_bias.astype(low).reshape(-1, part_rows)]
        ),
    ]
    ringed = size <= RING_MAX
    if ringed:
        gathered, slotted, qkv_all = enter(slot_order, tokens, shards, ((0, 2), (2, 3)), size, 0)
    else:
        gathered = [lax.all_gather(shard, "dp") for shard in shards]
    qkv_weight, up_weight, out_weight = (flat(full) for full in gathered[:3])
    small = gathered[3].astype(jnp.float32)
    side = small[:, :8].transpose(1, 0, 2).reshape(8, width)
    gain_full, bias_full = side[:2], side[2:]
    upbias_full = small[:, 8:].reshape(-1)
    hidden_local = up_weight.shape[1]
    col_start = tensor_pos * width_local
    if not ringed:
        query_bias = lax.dynamic_slice_in_dim(bias_full[0], col_start, width_local)
        value_bias = lax.dynamic_slice_in_dim(bias_full[1], col_start, width_local)
        qkv_bias = jnp.concatenate([query_bias, jnp.zeros_like(query_bias), value_bias])
        arrived = gather_rows(tokens, 0)
        slotted, qkv_all = enter_slots(slot_order, arrived, qkv_weight, qkv_bias)
    row_start = tensor_pos * own_rows
    resid_input = lax.dynamic_slice_in_dim(slotted, row_start, own_rows, 0).astype(jnp.float32)
    positions = row_start + jnp.arange(own_rows, dtype=jnp.int32)
    row_keep = (positions % SLOT < lengths[positions // SLOT]).astype(jnp.float32)
    context, exact, totals, attn_part, gathered = attend(
        qkv_all, lengths, out_weight, [w_down.astype(low).T, w_proj.astype(low)], size, 1
    )
    down_weight, proj_weight = (flat(full) for full in gathered)
    first_sum = resid_input + attn_part + bias_full[2]
    first_norm, back_first = jax.vjp(norm_rows, first_sum, gain_full[0], bias_full[3])
    first_low = first_norm.astype(jnp.bfloat16)
    upbias_own = lax.dynamic_slice_in_dim(upbias_full, tensor_pos * hidden_local, hidden_local)
    mid_rows, hidden, slope, ffn_part = feed_forward(first_low, up_weight, upbias_own, down_weight, 2)
    vectors = jnp.stack([bias_full[4], gain_full[1], bias_full[5]])
    embeddings, dsecond, dsecond_low, grad_proj, second_side = head(
        first_norm, ffn_part, vectors, proj_weight, cotangent, row_keep[:, None]
    )
    dfirst_norm, grad_up, grad_down, dshift = feed_back(
        dsecond_low, slope, mid_rows, hidden, up_weight, down_weight, 4
    )
    grad_upbias = lax.dynamic_update_slice_in_dim(
        jnp.zeros(upbias_full.shape, jnp.float32), dshift[0], tensor_pos * hidden_local, 0
    )
    dfirst, grad_gain_one, grad_shift_one = back_first(dfirst_norm + dsecond)
    dfirst_low = dfirst.astype(jnp.bfloat16)
    cut = lambda grad: grad.astype(low).reshape(size, part_rows, grad.shape[1])
    dqkv, column_sums, grad_out, (sum_up, sum_down, sum_proj) = attend_back(
        dfirst_low,
        out_weight,
        context,
        qkv_all,
        exact,
        totals,
        lengths,
        [cut(grad_up), cut(grad_down), cut(grad_proj)],
        size,
        6,
    )
    column_sums = column_sums.reshape(3, width_local)
    zero_row = jnp.zeros((bias_full.shape[1],), jnp.float32)
    grad_biases = jnp.stack(
        [
            lax.dynamic_update_slice_in_dim(zero_row, column_sums[0], col_start, 0),
            lax.dynamic_update_slice_in_dim(zero_row, column_sums[2], col_start, 0),
            jnp.sum(dfirst, axis=0),
            grad_shift_one,
            second_side[2],
            second_side[1],
        ]
    )
    grad_gains = jnp.stack([grad_gain_one, second_side[0]])
    small_grad = jnp.concatenate([grad_gains, grad_biases]).reshape(8, size, part_rows).transpose(1, 0, 2)
    small_grad = jnp.concatenate([small_grad, grad_upbias.reshape(size, -1, part_rows)], axis=1)
    grad_tokens, sum_qkv, (sum_out, sum_gains, sum_biases, sum_shift) = finish(
        slotted, dqkv, qkv_weight, dfirst, slot_order, [cut(grad_out), small_grad], size, 7
    )
    return (
        embeddings,
        grad_tokens,
        sum_qkv,
        sum_out,
        sum_up,
        sum_down,
        sum_proj,
        sum_gains,
        sum_biases,
        sum_shift.reshape(-1),
    )


def solution(mesh):
    return jax.shard_map(
        body,
        mesh=mesh,
        in_specs=(
            P(("dp", "tensor"), None),
            P("dp"),
            P("dp", None),
            P(None, "dp", "tensor"),
            P("tensor", "dp"),
            P("dp", "tensor"),
            P("tensor", "dp"),
            P("dp", None),
            P(None, "dp"),
            P(None, "dp"),
            P("dp"),
            P(("dp", "tensor"), None),
        ),
        out_specs=(
            P(("dp", "tensor"), None),
            P(("dp", "tensor"), None),
            P(None, "dp", "tensor"),
            P("tensor", "dp"),
            P("dp", "tensor"),
            P("tensor", "dp"),
            P("dp", None),
            P(None, "dp"),
            P(None, "dp"),
            P("dp"),
        ),
        check_vma=False,
    )
```

```python
import jax
import jax.numpy as jnp
from jax import lax
from jax.experimental import pallas as pl
from jax.experimental.pallas import tpu as pltpu
from jax.sharding import PartitionSpec as P

HEAD_DIM = 64


EPS_NORM = 1e-06
EPS_UNIT = 1e-06
NEG_FILL = -1e30


def norm_parts(values):
    center = values - jnp.mean(values, axis=-1, keepdims=True)
    scale = lax.rsqrt(jnp.mean(center * center, axis=-1, keepdims=True) + EPS_NORM)
    return center * scale, scale


def norm_back(dunit, unit, scale):
    middle = jnp.mean(dunit, axis=-1, keepdims=True)
    along = jnp.mean(dunit * unit, axis=-1, keepdims=True)
    return scale * (dunit - middle - unit * along)


def times_transposed(left, right):
    return lax.dot_general(
        left, right, (((1,), (1,)), ((), ())), preferred_element_type=jnp.float32
    )


MESH = pl.DeviceIdType.MESH
VMEM = pl.BlockSpec(memory_space=pltpu.VMEM)
WIDE = 128


def lane_index(rows):
    return lax.broadcasted_iota(jnp.int32, (rows, WIDE - HEAD_DIM), 1)


def thirds(column):
    parts = []
    for _ in range(3):
        part = column.astype(jnp.bfloat16).astype(jnp.float32)
        parts.append(part)
        column = column - part
    return parts


def beside(rows, columns):
    lane = lane_index(rows)
    out = jnp.zeros(lane.shape, jnp.float32)
    for i, column in enumerate(columns):
        out = jnp.where(lane == i, column, out)
    return out.astype(jnp.bfloat16)


def key_fill(length, keys):
    position = lax.broadcasted_iota(jnp.int32, (keys, 1), 0)
    return jnp.where(position < length, 0.0, NEG_FILL)


RING_MAX = 8
VMEM_GRANT = 26
ROW_PIECES = 4


def ring_place(position, size):
    far = position // (size // 2)
    return 2 * ((1 - far) * position + far * (size - 1 - position)) + far


def ring_position(index, size):
    row, far = index // 2, index % 2
    return (1 - far) * row + far * (size - 1 - row)


def ring_hops(index, size):
    longer, shorter = size // 2, size - 1 - size // 2
    return (longer, shorter) if index % 2 == 0 else (shorter, longer)


class Ring:
    def __init__(self, size):
        self.size = size
        self.me = lax.axis_index("dp")
        self.position = ring_position(self.me, size)
        self.targets = (self.at(1), self.at(-1))

    def at(self, offset):
        return ring_place(lax.rem(self.position + (offset + self.size), self.size), self.size)


class Chip:
    def __init__(self):
        self.me = lax.axis_index("tensor")
        chip, core = self.me // 2, self.me % 2
        self.mate = 2 * chip + (1 - core)
        self.peer = 2 * (1 - chip) + core
        self.across = 2 * (1 - chip) + (1 - core)


def greet(devices):
    barrier = pltpu.get_barrier_semaphore()
    for device in devices:
        pl.semaphore_signal(barrier, inc=1, device_id=device, device_id_type=MESH)
    pl.semaphore_wait(barrier, len(devices))


def remote(source, target, send, recv, device):
    return pltpu.make_async_remote_copy(
        src_ref=source,
        dst_ref=target,
        send_sem=send,
        recv_sem=recv,
        device_id=device,
        device_id_type=MESH,
    )


class RingGather:
    def __init__(self, ring, shards, outs, send, recv):
        self.ring, self.shards, self.outs, self.send, self.recv = ring, shards, outs, send, recv

    def copy(self, i, way, hop):
        owner = self.ring.at(-hop if way == 0 else hop)
        target = self.outs[i].at[owner]
        return remote(
            self.shards[i] if hop == 0 else target,
            target,
            self.send.at[i, way, hop],
            self.recv.at[i, way, hop],
            {"dp": self.ring.targets[way]},
        )

    def each(self, hop):
        for i in range(len(self.shards)):
            for way in (0, 1):
                if hop < ring_hops(i, self.ring.size)[way]:
                    yield i, way

    def start(self):
        for i, way in self.each(0):
            self.copy(i, way, 0).start()
        for shard, out in zip(self.shards, self.outs):
            out[self.ring.me] = shard[...]

    def relay(self, hop, only=None):
        for i, way in self.each(hop - 1):
            if only is not None and i not in only:
                continue
            self.copy(i, way, hop - 1).wait_recv()
            if hop < ring_hops(i, self.ring.size)[way]:
                self.copy(i, way, hop).start()

    def finish(self):
        for hop in range(self.ring.size // 2):
            for i, way in self.each(hop):
                self.copy(i, way, hop).wait_send()


class RingScatter:
    def __init__(self, ring, parts, landing, send, recv):
        self.ring, self.parts, self.landing, self.send, self.recv = ring, parts, landing, send, recv

    def slot(self, i, way, hop):
        return self.landing[i].at[hop + (0 if way == 0 else ring_hops(i, self.ring.size)[0])]

    def owner(self, i, way, hop):
        left = ring_hops(i, self.ring.size)[way] - hop
        return self.ring.at(left if way == 0 else -left)

    def copy(self, i, way, hop):
        source = self.parts[i].at[self.owner(i, way, 0)] if hop == 0 else self.slot(i, way, hop - 1)
        return remote(
            source,
            self.slot(i, way, hop),
            self.send.at[i, way, hop],
            self.recv.at[i, way, hop],
            {"dp": self.ring.targets[way]},
        )

    def each(self, hop):
        for i in range(len(self.parts)):
            for way in (0, 1):
                if hop < ring_hops(i, self.ring.size)[way]:
                    yield i, way

    def start(self):
        for i, way in self.each(0):
            self.copy(i, way, 0).start()

    def relay(self, hop):
        for i, way in self.each(hop - 1):
            self.copy(i, way, hop - 1).wait_recv()
            if hop < ring_hops(i, self.ring.size)[way]:
                slot = self.slot(i, way, hop - 1)
                own = self.parts[i][self.owner(i, way, hop)]
                slot[...] = (slot[...].astype(jnp.float32) + own.astype(jnp.float32)).astype(slot.dtype)
                self.copy(i, way, hop).start()

    def total(self, i):
        up, down = ring_hops(i, self.ring.size)
        return (
            self.parts[i][self.ring.me].astype(jnp.float32)
            + self.slot(i, 0, up - 1)[...].astype(jnp.float32)
            + self.slot(i, 1, down - 1)[...].astype(jnp.float32)
        )

    def finish(self):
        for hop in range(self.ring.size // 2):
            for i, way in self.each(hop):
                self.copy(i, way, hop).wait_send()


def piece_rows(piece, step):
    return pl.ds(piece * step if isinstance(piece, int) else pl.multiple_of(piece * step, step), step)


class RowGather:
    def __init__(self, chip, own, out, send, recv):
        self.chip, self.own, self.out, self.send, self.recv = chip, own, out, send, recv
        self.step = own.shape[0] // ROW_PIECES

    def copy(self, kind, piece):
        rows = piece_rows(piece, self.step)
        chip = self.chip
        owner = chip.peer if kind == 2 else chip.me
        target = self.out.at[owner, rows]
        device = chip.peer if kind == 0 else chip.mate
        return remote(
            target if kind == 2 else self.own.at[rows],
            target,
            self.send.at[kind, piece],
            self.recv.at[kind, piece],
            {"tensor": device},
        )

    def start(self):
        for kind in (0, 1):
            for piece in range(ROW_PIECES):
                self.copy(kind, piece).start()
        self.out[self.chip.me] = self.own[...]

    def relay(self, piece):
        self.copy(0, piece).wait_recv()
        self.copy(2, piece).start()

    def finish(self):
        for kind in (1, 2):
            for piece in range(ROW_PIECES):
                self.copy(kind, piece).wait_recv()
        for kind in (0, 1, 2):
            for piece in range(ROW_PIECES):
                self.copy(kind, piece).wait_send()


class RowScatter:
    def __init__(self, chip, parts, landing, send, recv):
        self.chip, self.parts, self.landing, self.send, self.recv = chip, parts, landing, send, recv
        self.pieces = send.shape[1]
        self.step = parts.shape[1] // self.pieces

    def rows(self, piece):
        return piece_rows(piece, self.step)

    def copy(self, kind, piece):
        chip, rows = self.chip, self.rows(piece)
        source = (
            self.parts.at[chip.across, rows],
            self.landing.at[0, rows],
            self.parts.at[chip.mate, rows],
        )[kind]
        return remote(
            source,
            self.landing.at[kind, rows],
            self.send.at[kind, piece],
            self.recv.at[kind, piece],
            {"tensor": chip.peer if kind == 1 else chip.mate},
        )

    def start(self):
        for kind in (0, 2):
            for piece in range(ROW_PIECES):
                self.copy(kind, piece).start()

    def relay(self, piece):
        rows = self.rows(piece)
        self.copy(0, piece).wait_recv()
        total = self.landing[0, rows].astype(jnp.float32) + self.parts[self.chip.peer, rows].astype(
            jnp.float32
        )
        self.landing[0, rows] = total.astype(self.landing.dtype)
        self.copy(1, piece).start()

    def total(self, piece):
        rows = self.rows(piece)
        self.copy(2, piece).wait_recv()
        self.copy(1, piece).wait_recv()
        return (
            self.parts[self.chip.me, rows].astype(jnp.float32)
            + self.landing[1, rows].astype(jnp.float32)
            + self.landing[2, rows].astype(jnp.float32)
        )

    def finish(self):
        for kind in (0, 1, 2):
            for piece in range(self.pieces):
                self.copy(kind, piece).wait_send()


class Meet:
    def __init__(self, chip, held, send, recv):
        self.chip, self.held, self.send, self.recv = chip, held, send, recv
        self.others = (chip.mate, chip.peer, chip.across)

    def copies(self):
        own = self.held.at[self.chip.me]
        for k, other in enumerate(self.others):
            yield remote(own, own, self.send.at[k], self.recv.at[k], {"tensor": other})

    def start(self, value):
        self.held[self.chip.me] = value
        for copy in self.copies():
            copy.start()

    def total(self):
        for copy in self.copies():
            copy.wait_recv()
        return (self.held[0] + self.held[1]) + (self.held[2] + self.held[3])

    def finish(self):
        for copy in self.copies():
            copy.wait_send()


def meet_sems():
    return [pltpu.SemaphoreType.DMA((3,))] * 2


def row_sems(pieces=ROW_PIECES):
    return [pltpu.SemaphoreType.DMA((3, pieces))] * 2


def ring_sems(count, size):
    return [pltpu.SemaphoreType.DMA((count, 2, size // 2))] * 2


def comm_params(collective_id, grant=VMEM_GRANT):
    return pltpu.CompilerParams(
        collective_id=collective_id, has_side_effects=True, vmem_limit_bytes=grant << 20
    )


def gather_rows(own, collective_id):
    def kernel(own_ref, out_ref, send, recv):
        chip = Chip()
        greet(({"tensor": chip.mate}, {"tensor": chip.peer}))
        rows = RowGather(chip, own_ref, out_ref, send, recv)
        rows.start()
        for piece in range(ROW_PIECES):
            rows.relay(piece)
        rows.finish()

    out = pl.pallas_call(
        kernel,
        out_shape=jax.ShapeDtypeStruct((4, *own.shape), own.dtype),
        in_specs=[VMEM],
        out_specs=VMEM,
        scratch_shapes=row_sems(),
        compiler_params=comm_params(collective_id),
        name="gather_rows",
    )(own)
    return out.reshape(4 * own.shape[0], own.shape[1])


def enter(slots, own, shards, shift_rows, size, collective_id):
    count = len(shards) - 1
    block, model = own.shape
    group = 4 * block
    wide = shards[1].shape[1]
    width = shards[0].shape[1] // 3
    tile = 256
    tiles = group // tile
    low, f32 = jnp.bfloat16, jnp.float32

    def kernel(*refs):
        slots_ref, own_ref, shard_refs = refs[0], refs[1], refs[2 : 3 + count]
        refs = refs[3 + count :]
        out_refs, refs = refs[:count], refs[count:]
        side, slotted_ref, qkv_ref, resid_ref, vector_ref, wide_ref, *refs = refs
        rows_ref, total, shift, ring_send, ring_recv, row_send, row_recv = refs
        ring, chip = Ring(size), Chip()
        greet(
            (
                {"dp": ring.targets[0]},
                {"dp": ring.targets[1]},
                {"tensor": chip.mate},
                {"tensor": chip.peer},
            )
        )
        rows = RowGather(chip, own_ref, rows_ref, row_send, row_recv)
        weights = RingGather(ring, shard_refs, (*out_refs, side), ring_send, ring_recv)
        rows.start()
        weights.start()

        half = block // 2

        def pick(here, owner, start, length):
            first = pl.multiple_of(owner * block, block) + start
            wanted = here * tile + lax.broadcasted_iota(jnp.int32, (tile, length), 0)
            chosen = jnp.where(slots_ref[:, pl.ds(first, length)] == wanted, 1.0, 0.0).astype(low)
            return jnp.dot(chosen, rows_ref[owner, start : start + length], preferred_element_type=f32)

        def near(here, carry):
            @pl.when(here == tiles // 2)
            def _():
                rows.relay(0)

            total[piece_rows(here, tile)] = pick(here, chip.me, 0, block) + pick(here, chip.mate, 0, block)
            return carry

        def middle(here, carry):
            total[piece_rows(here, tile)] += pick(here, chip.peer, 0, half) + pick(here, chip.across, 0, half)
            return carry

        def far(here, carry):
            @pl.when(here == tiles // 2)
            def _():
                weights.relay(3)

            at = piece_rows(here, tile)
            moved = pick(here, chip.peer, half, half) + pick(here, chip.across, half, half)
            slotted_ref[at] = (total[at] + moved).astype(low)
            return carry

        for piece in range(ROW_PIECES):
            rows.copy(1, piece).wait_recv()
        lax.fori_loop(0, tiles, near, 0)
        rows.relay(1)
        weights.relay(1)
        for piece in range(ROW_PIECES // 2):
            rows.copy(2, piece).wait_recv()
        lax.fori_loop(0, tiles, middle, 0)
        rows.relay(2)
        weights.relay(2)
        rows.relay(3)
        for piece in range(ROW_PIECES // 2, ROW_PIECES):
            rows.copy(2, piece).wait_recv()
        lax.fori_loop(0, tiles, far, 0)
        weights.relay(4, (0, count))
        span, last = shards[-1].shape[1], shards[-1].shape[0]
        resid_ref[...] = slotted_ref[pl.ds(pl.multiple_of(chip.me * block, block), block)]
        for d in range(size):
            vector_ref[:, d * span : (d + 1) * span] = side[d, :8].astype(f32)
        shift[...] = jnp.zeros_like(shift)
        for j in range(width // span):
            owner = chip.me * (width // span) + j
            for part, row in shift_rows:
                at = part * width + j * span
                shift[:, at : at + span] = side[owner, row : row + 1].astype(f32)
            for k in range(last - 8):
                at = (j * (last - 8) + k) * span
                wide_ref[:, at : at + span] = side[owner, 8 + k : 9 + k].astype(f32)

        def project(here, carry):
            at = piece_rows(here, block)
            weight = out_refs[0][...].reshape(model, 3 * width)
            out = jnp.dot(slotted_ref[at], weight, preferred_element_type=f32) + shift[...]
            qkv_ref[at] = out.astype(low)
            return carry

        lax.fori_loop(0, 4, project, 0)
        weights.relay(4, tuple(range(1, count)))
        for kind in (0, 1, 2):
            for piece in range(ROW_PIECES):
                rows.copy(kind, piece).wait_send()
        weights.finish()

    full = [jax.ShapeDtypeStruct((size, *s.shape), s.dtype) for s in shards]
    outs = pl.pallas_call(
        kernel,
        out_shape=full
        + [
            jax.ShapeDtypeStruct((group, model), low),
            jax.ShapeDtypeStruct((group, 3 * width), low),
            jax.ShapeDtypeStruct((block, model), low),
            jax.ShapeDtypeStruct((8, model), f32),
            jax.ShapeDtypeStruct((1, wide), f32),
        ],
        in_specs=[VMEM] * (count + 3),
        out_specs=[VMEM] * (count + 6),
        scratch_shapes=[
            pltpu.VMEM((4, block, model), low),
            pltpu.VMEM((group, model), f32),
            pltpu.VMEM((1, 3 * width), f32),
        ]
        + ring_sems(count + 1, size)
        + row_sems(),
        compiler_params=comm_params(collective_id, 16),
        name="enter",
    )(slots.reshape(1, group), own, *shards)
    return outs[:count], *outs[count + 1 :]


def attend(qkv, lengths, out_weight, resid, vectors, shards, size, collective_id):
    ringed = size <= RING_MAX
    given = shards if ringed else []
    count = len(given)
    keys, width = qkv.shape[0], qkv.shape[1] // 3
    heads, model = width // HEAD_DIM, out_weight.shape[0]
    own_rows, pieces = keys // 4, 2
    block = own_rows // pieces
    factor = HEAD_DIM ** (-0.5)
    low, f32 = jnp.bfloat16, jnp.float32

    def kernel(*refs):
        len_ref, qkv_ref, weight_ref, resid_ref, vector_ref = refs[:5]
        shard_refs, refs = refs[5 : 5 + count], refs[5 + count :]
        out_ref, exact_ref, total_ref, norm_ref, low_ref, unit_ref, scale_ref = refs[:7]
        full_refs, refs = refs[7 : 7 + count], refs[7 + count :]
        key_side, value_side, parts, landing, row_send, row_recv, *refs = refs
        chip = Chip()
        neighbours = ({"tensor": chip.mate}, {"tensor": chip.peer})
        if ringed:
            ring = Ring(size)
            weights = RingGather(ring, shard_refs, full_refs, *refs)
            neighbours += ({"dp": ring.targets[0]}, {"dp": ring.targets[1]})
        greet(neighbours)
        scatter = RowScatter(chip, parts, landing, row_send, row_recv)
        if ringed:
            weights.start()
        fill = key_fill(len_ref[0], keys)
        for h in range(heads):
            at = width + h * HEAD_DIM
            key_side[h, :, :HEAD_DIM] = qkv_ref[:, at : at + HEAD_DIM]
            key_side[h, :, HEAD_DIM:] = beside(keys, [fill])
            value_side[h, :, :HEAD_DIM] = qkv_ref[:, at + width : at + width + HEAD_DIM]
            value_side[h, :, HEAD_DIM:] = beside(keys, [1.0])
        ones = beside(block, [1.0])
        lane = lax.broadcasted_iota(jnp.int32, (block, WIDE), 1)

        def one(step, carry):
            near, odd = step // 4, lax.rem(step, 2)
            piece = lax.rem(step, 4) // 2
            owner = 2 * lax.rem(chip.me // 2 + 1 - near, 2) + lax.rem(lax.rem(chip.me, 2) + 1 - odd, 2)
            here = pl.ds(pl.multiple_of(owner * own_rows + piece * block, block), block)
            totals = jnp.zeros((block, WIDE), f32)
            for h in range(heads):
                lanes = slice(h * HEAD_DIM, (h + 1) * HEAD_DIM)
                query = jnp.concatenate([qkv_ref[here, lanes] * low(factor), ones], axis=1)
                scores = times_transposed(query, key_side[h])
                top = jnp.max(scores, axis=-1, keepdims=True)
                soft = jnp.exp(scores - top).astype(low)
                mixed = jnp.dot(soft, value_side[h], preferred_element_type=f32)
                total = mixed[:, HEAD_DIM : HEAD_DIM + 1]
                result = mixed[:, :HEAD_DIM] / total
                exact_ref[here, lanes] = result
                out_ref[here, lanes] = result.astype(low)
                totals = jnp.where(lane == h, top + jnp.log(total), totals)
            total_ref[here] = totals
            parts[owner, scatter.rows(piece)] = times_transposed(out_ref[here], weight_ref[...]).astype(low)

            @pl.when((near == 0) & (odd == 0))
            def _():
                scatter.copy(0, piece).start()

            @pl.when((near == 0) & (odd == 1))
            def _():
                scatter.relay(piece)

            @pl.when((near == 1) & (odd == 0))
            def _():
                scatter.copy(2, piece).start()

            if ringed:
                for hop in range(1, size // 2 + 1):

                    @pl.when(step == 2 * hop - 1)
                    def _():
                        weights.relay(hop)

            return carry

        lax.fori_loop(0, 4 * pieces, one, 0)
        for piece in range(pieces):
            at = scatter.rows(piece)
            unit, scale = norm_parts(scatter.total(piece) + resid_ref[at].astype(f32) + vector_ref[4:5])
            norm = unit * vector_ref[0:1] + vector_ref[5:6]
            norm_ref[at] = norm
            low_ref[at] = norm.astype(low)
            unit_ref[at] = unit
            scale_ref[at] = scale
        scatter.finish()
        if ringed:
            weights.finish()

    context, exact, totals, norm, norm_low, unit, scale, *gathered = pl.pallas_call(
        kernel,
        out_shape=[
            jax.ShapeDtypeStruct((keys, width), low),
            jax.ShapeDtypeStruct((keys, width), f32),
            jax.ShapeDtypeStruct((keys, WIDE), f32),
            jax.ShapeDtypeStruct((own_rows, model), f32),
            jax.ShapeDtypeStruct((own_rows, model), low),
            jax.ShapeDtypeStruct((own_rows, model), f32),
            jax.ShapeDtypeStruct((own_rows, 1), f32),
        ]
        + [jax.ShapeDtypeStruct((size, *s.shape), s.dtype) for s in given],
        in_specs=[pl.BlockSpec(memory_space=pltpu.SMEM)] + [VMEM] * (4 + count),
        out_specs=[VMEM] * (7 + count),
        scratch_shapes=[
            pltpu.VMEM((heads, keys, WIDE), low),
            pltpu.VMEM((heads, keys, WIDE), low),
            pltpu.VMEM((4, own_rows, model), low),
            pltpu.VMEM((3, own_rows, model), low),
        ]
        + row_sems(pieces)
        + (ring_sems(count, size) if ringed else []),
        compiler_params=comm_params(collective_id, 16),
        name="attend",
    )(lengths, qkv, out_weight, resid, vectors, *given)
    if not ringed:
        gathered = [lax.all_gather(shard, "dp") for shard in shards]
    return context, exact, totals, norm, norm_low, unit, scale, gathered


def turned(left, right):
    return lax.dot_general(
        left, right, (((0,), (0,)), ((), ())), preferred_element_type=jnp.float32
    )


def around_rows(chip, gather, scatter, work, keep, middle=None, end=None):
    parts = scatter.parts

    def own(piece, carry):
        rows = scatter.rows(piece)
        keep[rows] = work(chip.me, rows)
        return carry

    def near(piece, carry):
        rows = scatter.rows(piece)
        gather.copy(1, piece).wait_recv()
        parts[chip.mate, rows] = work(chip.mate, rows).astype(parts.dtype)
        scatter.copy(2, piece).start()
        return carry

    def far(piece, carry):
        rows = scatter.rows(piece)
        gather.relay(piece)
        parts[chip.peer, rows] = work(chip.peer, rows).astype(parts.dtype)

        @pl.when(piece > 0)
        def _():
            scatter.relay(piece - 1)

        gather.copy(2, piece).wait_recv()
        parts[chip.across, rows] = work(chip.across, rows).astype(parts.dtype)
        scatter.copy(0, piece).start()
        return carry

    def last(piece, carry):
        rows = scatter.rows(piece)
        scatter.copy(2, piece).wait_recv()
        scatter.copy(1, piece).wait_recv()
        keep[rows] += scatter.landing[1, rows].astype(jnp.float32) + scatter.landing[2, rows].astype(
            jnp.float32
        )
        return carry

    gather.start()
    lax.fori_loop(0, ROW_PIECES, own, 0)
    lax.fori_loop(0, ROW_PIECES, near, 0)
    if middle is not None:
        middle()
    lax.fori_loop(0, ROW_PIECES, far, 0)
    scatter.relay(ROW_PIECES - 1)
    if end is not None:
        end()
    lax.fori_loop(0, ROW_PIECES, last, 0)
    for copies in (gather, scatter):
        for kind in (0, 1, 2):
            for piece in range(ROW_PIECES):
                copies.copy(kind, piece).wait_send()


def feed_forward(own, up_weight, shift, down_weight, collective_id):
    rows, width = own.shape
    hidden_width = up_weight.shape[1]
    low, f32 = jnp.bfloat16, jnp.float32

    def kernel(
        own_ref, up_ref, shift_ref, down_ref, rows_ref, hidden_ref, slope_ref, out_ref, parts, landing, *sems
    ):
        chip = Chip()
        greet(({"tensor": chip.mate}, {"tensor": chip.peer}))
        gather = RowGather(chip, own_ref, rows_ref, *sems[:2])
        scatter = RowScatter(chip, parts, landing, *sems[2:])

        def work(owner, rows):
            pre = jnp.dot(rows_ref[owner, rows], up_ref[...], preferred_element_type=f32) + shift_ref[...]
            cdf = 0.5 * (1.0 + lax.erf(pre * 0.7071067811865476))
            hidden = (pre * cdf).astype(low)
            hidden_ref[owner, rows] = hidden
            slope = cdf + pre * (jnp.exp(-0.5 * pre * pre) * 0.3989422804014327)
            slope_ref[owner, rows] = slope.astype(low)
            return times_transposed(hidden, down_ref[...])

        around_rows(chip, gather, scatter, work, out_ref)

    return pl.pallas_call(
        kernel,
        out_shape=[
            jax.ShapeDtypeStruct((4, rows, width), low),
            jax.ShapeDtypeStruct((4, rows, hidden_width), low),
            jax.ShapeDtypeStruct((4, rows, hidden_width), low),
            jax.ShapeDtypeStruct((rows, width), f32),
        ],
        in_specs=[VMEM] * 4,
        out_specs=[VMEM] * 4,
        scratch_shapes=[pltpu.VMEM((4, rows, width), low), pltpu.VMEM((3, rows, width), low)]
        + row_sems() * 2,
        compiler_params=comm_params(collective_id, 12),
        name="feed_forward",
    )(own, up_weight, shift, down_weight)


def feed_back(own, slope, mid_rows, hidden, up_weight, down_weight, collective_id):
    rows, width = own.shape
    hidden_width = up_weight.shape[1]
    low, f32 = jnp.bfloat16, jnp.float32
    band = 256

    def kernel(
        own_ref,
        slope_ref,
        mid_ref,
        hidden_ref,
        up_ref,
        down_ref,
        out_ref,
        grad_up_ref,
        grad_down_ref,
        shift_ref,
        rows_ref,
        dpre_ref,
        up_sum,
        down_sum,
        parts,
        landing,
        *sems,
    ):
        chip = Chip()
        greet(({"tensor": chip.mate}, {"tensor": chip.peer}))
        gather = RowGather(chip, own_ref, rows_ref, *sems[:2])
        scatter = RowScatter(chip, parts, landing, *sems[2:])
        shift_ref[...] = jnp.zeros_like(shift_ref)

        def work(owner, rows):
            dhidden = jnp.dot(rows_ref[owner, rows], down_ref[...], preferred_element_type=f32)
            dpre = (dhidden * slope_ref[owner, rows].astype(f32)).astype(low)
            dpre_ref[owner, rows] = dpre
            shift_ref[...] += jnp.sum(dpre.astype(f32), axis=0, keepdims=True)
            return times_transposed(dpre, up_ref[...])

        def grads(owners, first):
            def one(tile, carry):
                columns = pl.ds(pl.multiple_of(tile * band, band), band)
                for left, right, total in (
                    (mid_ref, dpre_ref, up_sum),
                    (rows_ref, hidden_ref, down_sum),
                ):
                    term = turned(left[owners[0], :, columns], right[owners[0]])
                    term += turned(left[owners[1], :, columns], right[owners[1]])
                    total[columns] = term if first else total[columns] + term
                return carry

            return lambda: lax.fori_loop(0, width // band, one, 0)

        around_rows(
            chip,
            gather,
            scatter,
            work,
            out_ref,
            grads((chip.me, chip.mate), True),
            grads((chip.peer, chip.across), False),
        )
        grad_up_ref[...] = up_sum[...].astype(low)
        grad_down_ref[...] = down_sum[...].astype(low)

    return pl.pallas_call(
        kernel,
        out_shape=[
            jax.ShapeDtypeStruct((rows, width), f32),
            jax.ShapeDtypeStruct((width, hidden_width), low),
            jax.ShapeDtypeStruct((width, hidden_width), low),
            jax.ShapeDtypeStruct((1, hidden_width), f32),
        ],
        in_specs=[VMEM] * 6,
        out_specs=[VMEM] * 4,
        scratch_shapes=[
            pltpu.VMEM((4, rows, width), low),
            pltpu.VMEM((4, rows, hidden_width), low),
            pltpu.VMEM((width, hidden_width), f32),
            pltpu.VMEM((width, hidden_width), f32),
            pltpu.VMEM((4, rows, width), low),
            pltpu.VMEM((3, rows, width), low),
        ]
        + row_sems() * 2,
        compiler_params=comm_params(collective_id, 22),
        name="feed_back",
    )(own, slope, mid_rows, hidden, up_weight, down_weight)


def enter_slots(slots, arrived, weight, shift):
    group, width = arrived.shape
    block = 256

    def kernel(slots_ref, arrived_ref, weight_ref, shift_ref, rows_ref, out_ref):
        first = pl.program_id(0) * block
        wanted = first + lax.broadcasted_iota(jnp.int32, (block, group), 0)
        pick = jnp.where(slots_ref[...] == wanted, 1.0, 0.0).astype(jnp.bfloat16)
        rows = jnp.dot(pick, arrived_ref[...], preferred_element_type=jnp.float32).astype(jnp.bfloat16)
        rows_ref[...] = rows
        out = jnp.dot(rows, weight_ref[...], preferred_element_type=jnp.float32) + shift_ref[...]
        out_ref[...] = out.astype(jnp.bfloat16)

    return pl.pallas_call(
        kernel,
        grid=(group // block,),
        in_specs=[VMEM] * 4,
        out_specs=[
            pl.BlockSpec((block, width), lambda i: (i, 0)),
            pl.BlockSpec((block, weight.shape[1]), lambda i: (i, 0)),
        ],
        out_shape=[
            jax.ShapeDtypeStruct((group, width), jnp.bfloat16),
            jax.ShapeDtypeStruct((group, weight.shape[1]), jnp.bfloat16),
        ],
        name="enter_slots",
    )(slots.reshape(1, group), arrived, weight, shift.reshape(1, -1))


def attend_back(dpart, dnext, unit, scale, vectors, out_weight, context, qkv, exact, totals, lengths, parts, size, collective_id):
    ringed = size <= RING_MAX
    given = parts if ringed else []
    count = len(given)
    block, model = dpart.shape
    keys, width = qkv.shape[0], qkv.shape[1] // 3
    heads = width // HEAD_DIM
    factor = HEAD_DIM ** (-0.5)
    low, f32 = jnp.bfloat16, jnp.float32

    def kernel(*refs):
        len_ref, dpart_ref, dnext_ref, unit_ref, scale_ref, vector_ref = refs[:6]
        weight_ref, context_ref, qkv_ref, exact_ref, total_ref = refs[6:11]
        part_refs, refs = refs[11 : 11 + count], refs[11 + count :]
        out_ref, column_ref, grad_ref, dsum_ref, side_ref = refs[:5]
        sum_refs, refs = refs[5 : 5 + count], refs[5 + count :]
        own_ref, *refs = refs
        rows_ref, key_side, value_side, key_turned, sums, grad_sum, row_send, row_recv = refs[:8]
        refs = refs[8:]
        chip = Chip()
        neighbours = ({"tensor": chip.mate}, {"tensor": chip.peer})
        if ringed:
            landing, (held, ring_send, ring_recv, meet_send, meet_recv) = refs[:count], refs[count:]
            ring = Ring(size)
            meet = Meet(chip, held, meet_send, meet_recv)
            grads = RingScatter(ring, part_refs, landing, ring_send, ring_recv)
            neighbours += ({"tensor": chip.across},)
            neighbours += ({"dp": ring.targets[0]}, {"dp": ring.targets[1]})
        greet(neighbours)
        rows = RowGather(chip, own_ref, rows_ref, row_send, row_recv)
        if ringed:
            grads.start()
        side_ref[...] = jnp.zeros_like(side_ref)

        def inner(piece, carry):
            at = piece_rows(piece, rows.step)
            dnorm = dpart_ref[at] + dnext_ref[at]
            dsum = norm_back(dnorm * vector_ref[0:1], unit_ref[at], scale_ref[at])
            dsum_ref[at] = dsum
            own_ref[at] = dsum.astype(low)
            rows.copy(0, piece).start()
            rows.copy(1, piece).start()
            for i, term in enumerate((dnorm * unit_ref[at], dnorm, dsum)):
                side_ref[i : i + 1] += jnp.sum(term, axis=0, keepdims=True)
            return carry

        lax.fori_loop(0, ROW_PIECES, inner, 0)
        rows_ref[chip.me] = own_ref[...]
        fill = key_fill(len_ref[0], keys)
        for h in range(heads):
            at = width + h * HEAD_DIM
            key = qkv_ref[:, at : at + HEAD_DIM]
            key_side[h, :, :HEAD_DIM] = key
            key_side[h, :, HEAD_DIM:] = beside(keys, [fill, 1.0, 1.0, 1.0])
            key_turned[h] = (key * low(factor)).T
            value_side[h, :, :HEAD_DIM] = qkv_ref[:, at + width : at + width + HEAD_DIM]
            value_side[h, :, HEAD_DIM:] = beside(keys, [1.0, 1.0, 1.0])
        sums[...] = jnp.zeros_like(sums)
        grad_sum[...] = jnp.zeros_like(grad_sum)

        def one(step, carry):
            owner = 2 * lax.rem(chip.me // 2 + step // 2, 2) + lax.rem(lax.rem(chip.me, 2) + step, 2)

            @pl.when(step == 1)
            def _():
                for piece in range(ROW_PIECES):
                    rows.copy(1, piece).wait_recv()

            @pl.when(step == 3)
            def _():
                for piece in range(ROW_PIECES):
                    rows.copy(2, piece).wait_recv()

            first = pl.multiple_of(owner * block, block)
            here = pl.ds(first, block)
            drows = rows_ref[owner]
            dcontext = jnp.dot(drows, weight_ref[...], preferred_element_type=f32).astype(low)
            grad_sum[...] += turned(drows, context_ref[here])
            blank = jnp.zeros((block, HEAD_DIM), low)
            for h in range(heads):
                lanes = slice(h * HEAD_DIM, (h + 1) * HEAD_DIM)
                dout = dcontext[:, lanes]
                delta = jnp.sum(dout.astype(f32) * exact_ref[here, lanes], axis=-1, keepdims=True)
                query = qkv_ref[here, lanes] * low(factor)
                query_wide = jnp.concatenate(
                    [query, beside(block, [1.0, *thirds(-total_ref[here, h : h + 1])])], axis=1
                )
                dout_wide = jnp.concatenate([dout, beside(block, thirds(-delta))], axis=1)
                soft = jnp.exp(times_transposed(key_side[h], query_wide))
                dsoft = times_transposed(value_side[h], dout_wide)
                dscore = (soft * dsoft).astype(low)
                soft = soft.astype(low)
                sums[h] += jnp.dot(
                    soft, jnp.concatenate([dout, blank], axis=1), preferred_element_type=f32
                ) + jnp.dot(
                    dscore, jnp.concatenate([blank, query], axis=1), preferred_element_type=f32
                )
                dquery = jnp.dot(key_turned[h], dscore, preferred_element_type=f32)
                out_ref[here, lanes] = dquery.T.astype(low)
                if ringed and h == 0:

                    @pl.when(step == 3)
                    def _():
                        grads.relay(size // 2)
                        meet.start(grads.total(count - 1))

                if ringed and h == heads - 1:
                    for hop in range(1, size // 2):

                        @pl.when(step == hop - 1)
                        def _():
                            grads.relay(hop)

            @pl.when(step < 2)
            def _():
                rows.relay(2 * step)
                rows.relay(2 * step + 1)

            return carry

        lax.fori_loop(0, 4, one, 0)
        for h in range(heads):
            both = sums[h].astype(low)
            at = width + h * HEAD_DIM
            out_ref[:, at : at + HEAD_DIM] = both[:, HEAD_DIM:]
            out_ref[:, at + width : at + width + HEAD_DIM] = both[:, :HEAD_DIM]
        column_ref[...] = jnp.sum(out_ref[...].astype(f32), axis=0, keepdims=True)
        grad_ref[...] = grad_sum[...].astype(low)
        if ringed:
            sum_refs[0][...] = grads.total(0)
            sum_refs[1][...] = grads.total(1).T
            sum_refs[2][...] = meet.total()
            meet.finish()
            grads.finish()
        for kind in (0, 1, 2):
            for piece in range(ROW_PIECES):
                rows.copy(kind, piece).wait_send()

    scratch = [
        pltpu.VMEM((block, model), low),
        pltpu.VMEM((4, block, model), low),
        pltpu.VMEM((heads, keys, WIDE), low),
        pltpu.VMEM((heads, keys, WIDE), low),
        pltpu.VMEM((heads, HEAD_DIM, keys), low),
        pltpu.VMEM((heads, keys, WIDE), f32),
        pltpu.VMEM((model, width), f32),
        *row_sems(),
    ]
    if ringed:
        scratch += [pltpu.VMEM((size - 1, *p.shape[1:]), p.dtype) for p in parts]
        scratch += [pltpu.VMEM((4, *parts[-1].shape[1:]), f32)]
        scratch += ring_sems(count, size) + meet_sems()
    dqkv, columns, grad_out, dsum, sides, *summed = pl.pallas_call(
        kernel,
        out_shape=[
            jax.ShapeDtypeStruct((keys, 3 * width), low),
            jax.ShapeDtypeStruct((1, 3 * width), f32),
            jax.ShapeDtypeStruct((model, width), low),
            jax.ShapeDtypeStruct((block, model), f32),
            jax.ShapeDtypeStruct((3, model), f32),
        ]
        + [
            jax.ShapeDtypeStruct(p.shape[:0:-1] if i == 1 else p.shape[1:], f32)
            for i, p in enumerate(given)
        ],
        in_specs=[pl.BlockSpec(memory_space=pltpu.SMEM)] + [VMEM] * (10 + count),
        out_specs=[VMEM] * (5 + count),
        scratch_shapes=scratch,
        compiler_params=comm_params(collective_id, 26),
        name="attend_back",
    )(lengths, dpart, dnext, unit, scale, vectors, out_weight, context, qkv, exact, totals, *given)
    if not ringed:
        summed = [lax.psum_scatter(p.astype(f32), "dp", scatter_dimension=0) for p in parts]
        summed = [summed[0], summed[1].T, lax.psum(summed[2], "tensor")]
    return dqkv, columns, grad_out, dsum, sides, summed


def finish(rows, dqkv, weight, resid, slots, grad_out, vectors, size, collective_id):
    ringed = size <= RING_MAX
    span = grad_out.shape[1]
    first_side, second_side, column_sums, dshift = vectors
    hidden_rows = dshift.shape[1] * 4 // (size * span)
    small_shape = jax.ShapeDtypeStruct((size, 8 + hidden_rows, span), jnp.float32)
    parts = [grad_out, small_shape]
    given = [grad_out, *vectors] if ringed else []
    count = 3
    group, model = rows.shape
    columns = dqkv.shape[1]
    own_rows = group // 4
    pieces, band = 2, model // 2
    low, f32 = jnp.bfloat16, jnp.float32

    def kernel(*refs):
        rows_ref, dqkv_ref, weight_ref, resid_ref, slots_ref = refs[:5]
        given_refs, refs = refs[5 : 5 + len(given)], refs[5 + len(given) :]
        results = 6 if ringed else 2
        own_ref, grad_ref, *sum_refs = refs[:results]
        through, leaving, row_landing, row_send, row_recv, *refs = refs[results:]
        chip = Chip()
        neighbours = ({"tensor": chip.mate}, {"tensor": chip.peer})
        if ringed:
            local, small, landing = refs[0], refs[1], refs[2 : 2 + count]
            held, *sems = refs[2 + count :]
            ring = Ring(size)
            early = RingScatter(ring, (given_refs[0], small), landing[: count - 1], *sems[:2])
            late = RingScatter(ring, (local,), landing[count - 1 :], *sems[2:4])
            meet = Meet(chip, held, *sems[4:])
            neighbours += ({"tensor": chip.across},)
            neighbours += ({"dp": ring.targets[0]}, {"dp": ring.targets[1]})
        greet(neighbours)
        scatter = RowScatter(chip, leaving, row_landing, row_send, row_recv)
        if ringed:
            first_ref, second_ref, column_ref, shift_ref = given_refs[1:]
            small[...] = jnp.zeros_like(small)
            rows_of = ((0, first_ref, 0), (1, second_ref, 0), (4, first_ref, 2), (5, first_ref, 1))
            for row, source, i in (*rows_of, (6, second_ref, 2), (7, second_ref, 1)):
                for d in range(size):
                    small[d, row : row + 1] = source[i : i + 1, d * span : (d + 1) * span]
            width = columns // 3
            for j in range(width // span):
                owner = chip.me * (width // span) + j
                for row, part in ((2, 0), (3, 2)):
                    at = part * width + j * span
                    small[owner, row : row + 1] = column_ref[:, at : at + span]
                for k in range(hidden_rows):
                    at = (j * hidden_rows + k) * span
                    small[owner, 8 + k : 9 + k] = shift_ref[:, at : at + span]
            early.start()
        half = group // 2

        def spread(part, carry):
            here = pl.ds(pl.multiple_of(part * half, half), half)
            through[here] = times_transposed(dqkv_ref[here], weight_ref[...]).astype(low)
            return carry

        lax.fori_loop(0, 2, spread, 0)
        mine = pl.ds(pl.multiple_of(chip.me * own_rows, own_rows), own_rows)
        through[mine] = (
            times_transposed(dqkv_ref[mine], weight_ref[...]) + resid_ref[...]
        ).astype(low)
        step = own_rows // pieces
        slot = lax.broadcasted_iota(jnp.int32, (step, group), 1)

        def leave(owner, piece):
            first = pl.multiple_of(owner * own_rows + piece * step, step)
            pick = jnp.where(slots_ref[pl.ds(first, step)] == slot, 1.0, 0.0).astype(low)
            moved = jnp.dot(pick, through[...], preferred_element_type=f32).astype(low)
            leaving[owner, scatter.rows(piece)] = moved

        def outward(piece, carry):
            leave(chip.across, piece)
            scatter.copy(0, piece).start()
            leave(chip.peer, piece)
            scatter.relay(piece)
            return carry

        def inward(piece, carry):
            leave(chip.mate, piece)
            scatter.copy(2, piece).start()
            leave(chip.me, piece)
            return carry

        lax.fori_loop(0, 1, outward, 0)
        if ringed:
            early.relay(1)
        for tile in range(2):
            grad = turned(rows_ref[:, tile * band : (tile + 1) * band], dqkv_ref[...]).astype(low)
            if ringed:
                half_ring = size // 2
                local[tile * half_ring : (tile + 1) * half_ring] = grad.reshape(
                    half_ring, band // half_ring, columns
                )
            else:
                grad_ref[tile * band : (tile + 1) * band] = grad
        if ringed:
            late.start()
            early.relay(2)
        lax.fori_loop(1, pieces, outward, 0)
        if ringed:
            early.relay(3)
            late.relay(1)
        lax.fori_loop(0, pieces, inward, 0)
        if ringed:
            early.relay(4)
            meet.start(early.total(1))
            for hop in range(2, size // 2 + 1):
                late.relay(hop)
            out_sum, gain_sum, bias_sum, shift_sum = sum_refs
            out_sum[...] = early.total(0).T
            side = meet.total()
            gain_sum[...] = side[:2]
            bias_sum[...] = side[2:8]
            shift_sum[...] = side[8:]
        for piece in range(pieces):
            own_ref[scatter.rows(piece)] = scatter.total(piece)
        if ringed:
            total = late.total(0)
            for c in range(3):
                grad_ref[c] = total[:, c * columns // 3 : (c + 1) * columns // 3]
            meet.finish()
            early.finish()
            late.finish()
        scatter.finish()

    scratch = [
        pltpu.VMEM((group, model), low),
        pltpu.VMEM((4, own_rows, model), low),
        pltpu.VMEM((3, own_rows, model), low),
        *row_sems(pieces),
    ]
    if ringed:
        local = jax.ShapeDtypeStruct((size, model // size, columns), low)
        scratch += [pltpu.VMEM(local.shape, low), pltpu.VMEM(small_shape.shape, f32)]
        scratch += [pltpu.VMEM((size - 1, *p.shape[1:]), p.dtype) for p in (*parts, local)]
        scratch += [pltpu.VMEM((4, *parts[-1].shape[1:]), f32)]
        scratch += ring_sems(count - 1, size) + ring_sems(1, size) + meet_sems()
        shapes = [(3, model // size, columns // 3), parts[0].shape[:0:-1]]
        shapes += [(k, model // size) for k in (2, 6, parts[1].shape[1] - 8)]
        results = [jax.ShapeDtypeStruct(shape, f32) for shape in shapes]
    else:
        results = [jax.ShapeDtypeStruct((model, columns), low)]
    own, grad, *summed = pl.pallas_call(
        kernel,
        out_shape=[jax.ShapeDtypeStruct((own_rows, model), f32), *results],
        in_specs=[VMEM] * (5 + len(given)),
        out_specs=[VMEM] * (1 + len(results)),
        scratch_shapes=scratch,
        compiler_params=comm_params(collective_id, 18),
        name="finish",
    )(rows, dqkv, weight, resid, slots.reshape(group, 1), *given)
    if not ringed:
        place = lax.axis_index("tensor")
        wide = lambda part, length: lax.dynamic_update_slice_in_dim(
            jnp.zeros((length,), f32), part, place * part.shape[0], 0
        )
        sums = column_sums.reshape(3, -1)
        sides = [first_side[0], second_side[0], wide(sums[0], model), wide(sums[2], model)]
        sides += [first_side[2], first_side[1], second_side[2], second_side[1]]
        small = jnp.stack(sides).reshape(8, size, span).transpose(1, 0, 2)
        hidden = wide(dshift[0], 4 * dshift.shape[1]).reshape(size, hidden_rows, span)
        parts = [grad_out, jnp.concatenate([small, hidden], axis=1)]
        grad = grad.astype(f32).reshape(size, model // size, columns)
        grad, *summed = [lax.psum_scatter(p.astype(f32), "dp", scatter_dimension=0) for p in (grad, *parts)]
        side = lax.psum(summed[1], "tensor")
        grad = grad.reshape(model // size, 3, columns // 3).transpose(1, 0, 2)
        summed = [summed[0].T, side[:2], side[2:8], side[8:]]
    return own, grad, summed


def head(first_norm, ffn_part, vectors, proj_weight, cotangent, lengths):
    rows, width = first_norm.shape
    proj = proj_weight.shape[1]
    low, f32 = jnp.bfloat16, jnp.float32
    tile = 128

    def kernel(
        len_ref, norm_ref, part_ref, vector_ref, weight_ref, cot_ref, emb_ref, dsum_ref, low_ref, grad_ref, side_ref, grad_sum
    ):
        start = lax.axis_index("tensor") * rows
        grad_sum[...] = jnp.zeros_like(grad_sum)
        side_ref[...] = jnp.zeros_like(side_ref)
        extra, gain, shift = (vector_ref[i : i + 1] for i in (6, 1, 7))

        def one(piece, carry):
            at = piece_rows(piece, tile)
            unit, scale = norm_parts(norm_ref[at] + part_ref[at] + extra)
            second = (unit * gain + shift).astype(low)
            e = jnp.dot(second, weight_ref[...], preferred_element_type=f32)
            position = start + piece * tile + lax.broadcasted_iota(jnp.int32, (tile, 1), 0)
            keep_rows = jnp.where(position < len_ref[0], 1.0, 0.0)
            inverse = lax.rsqrt(jnp.sum(e * e, axis=-1, keepdims=True) + EPS_UNIT)
            emb_ref[at] = e * inverse * keep_rows
            cot = cot_ref[at].astype(f32) * keep_rows
            along = jnp.sum(cot * e, axis=-1, keepdims=True)
            de = (cot * inverse - e * (inverse * inverse * inverse * along)).astype(low)
            grad_sum[...] += turned(second, de)
            dnorm = times_transposed(de, weight_ref[...])
            dsum = norm_back(dnorm * gain, unit, scale)
            dsum_ref[at] = dsum
            low_ref[at] = dsum.astype(low)
            for i, term in enumerate((dnorm * unit, dnorm, dsum)):
                side_ref[i : i + 1] += jnp.sum(term, axis=0, keepdims=True)
            return carry

        lax.fori_loop(0, rows // tile, one, 0)
        grad_ref[...] = grad_sum[...].astype(low)

    return pl.pallas_call(
        kernel,
        out_shape=[
            jax.ShapeDtypeStruct((rows, proj), f32),
            jax.ShapeDtypeStruct((rows, width), f32),
            jax.ShapeDtypeStruct((rows, width), low),
            jax.ShapeDtypeStruct((width, proj), low),
            jax.ShapeDtypeStruct((3, width), f32),
        ],
        in_specs=[pl.BlockSpec(memory_space=pltpu.SMEM)] + [VMEM] * 5,
        out_specs=[VMEM] * 5,
        scratch_shapes=[pltpu.VMEM((width, proj), f32)],
        compiler_params=pltpu.CompilerParams(vmem_limit_bytes=16 << 20),
        name="head",
    )(lengths, first_norm, ffn_part, vectors, proj_weight, cotangent)


def settle(*arrays):
    def kernel(*refs):
        for source, target in zip(refs[: len(arrays)], refs[len(arrays) :]):
            target[...] = source[...]

    return pl.pallas_call(
        kernel,
        out_shape=[jax.ShapeDtypeStruct(a.shape, a.dtype) for a in arrays],
        in_specs=[VMEM] * len(arrays),
        out_specs=[VMEM] * len(arrays),
        compiler_params=pltpu.CompilerParams(vmem_limit_bytes=16 << 20),
        name="settle",
    )(*arrays)


def body(
    tokens,
    lengths,
    arrival_slots,
    w_qkv,
    w_out,
    w_up,
    w_down,
    w_proj,
    norm_gains,
    biases,
    up_bias,
    cotangent,
):
    own_rows = tokens.shape[0]
    tensor_pos = lax.axis_index("tensor")
    slot_order = arrival_slots[0]
    size = lax.axis_size("dp")
    part_rows, width_local = w_qkv.shape[1:]
    low = jnp.bfloat16
    width = size * part_rows
    flat = lambda full: full.reshape(width, full.shape[2])
    cut = lambda grad: grad.reshape(size, part_rows, grad.shape[1])
    shards = [
        w_qkv.astype(low).transpose(1, 0, 2).reshape(part_rows, 3 * width_local),
        w_up.astype(low),
        w_out.astype(low).T,
        jnp.concatenate(
            [norm_gains.astype(low), biases.astype(low), up_bias.astype(low).reshape(-1, part_rows)]
        ),
    ]
    ringed = size <= RING_MAX
    if ringed:
        gathered, slotted, qkv_all, resid, vectors, shift_own = enter(
            slot_order, tokens, shards, ((0, 2), (2, 3)), size, 0
        )
        qkv_weight, up_weight, out_weight = (flat(full) for full in gathered)
    else:
        gathered = [lax.all_gather(shard, "dp") for shard in shards]
        qkv_weight, up_weight, out_weight = (flat(full) for full in gathered[:3])
        small = gathered[3].astype(jnp.float32)
        vectors = small[:, :8].transpose(1, 0, 2).reshape(8, width)
        hidden_local = up_weight.shape[1]
        shift_own = lax.dynamic_slice_in_dim(
            small[:, 8:].reshape(1, -1), tensor_pos * hidden_local, hidden_local, 1
        )
        own_bias = lax.dynamic_slice_in_dim(vectors, tensor_pos * width_local, width_local, 1)
        qkv_bias = jnp.concatenate([own_bias[2], jnp.zeros_like(own_bias[2]), own_bias[3]])
        arrived = gather_rows(tokens, 0)
        slotted, qkv_all = enter_slots(slot_order, arrived, qkv_weight, qkv_bias)
        resid = lax.dynamic_slice_in_dim(slotted, tensor_pos * own_rows, own_rows, 0)
    context, exact, totals, first_norm, first_low, unit, scale, gathered = attend(
        qkv_all, lengths, out_weight, resid, vectors, [w_down.astype(low).T, w_proj.astype(low)], size, 1
    )
    down_weight, proj_weight = (flat(full) for full in gathered)
    mid_rows, hidden, slope, ffn_part = feed_forward(first_low, up_weight, shift_own, down_weight, 2)
    embeddings, dsecond, dsecond_low, grad_proj, second_side = head(
        first_norm, ffn_part, vectors, proj_weight, cotangent, lengths
    )
    dfirst_norm, grad_up, grad_down, dshift = feed_back(
        dsecond_low, slope, mid_rows, hidden, up_weight, down_weight, 4
    )
    dqkv, column_sums, grad_out, dfirst, first_side, (sum_up, sum_down, sum_proj) = attend_back(
        dfirst_norm,
        dsecond,
        unit,
        scale,
        vectors,
        out_weight,
        context,
        qkv_all,
        exact,
        totals,
        lengths,
        [cut(grad_up), cut(grad_down), cut(grad_proj)],
        size,
        6,
    )
    grad_tokens, sum_qkv, (sum_out, sum_gains, sum_biases, sum_shift) = finish(
        slotted,
        dqkv,
        qkv_weight,
        dfirst,
        slot_order,
        cut(grad_out),
        (first_side, second_side, column_sums, dshift),
        size,
        7,
    )
    sums = (grad_tokens, sum_qkv, sum_out, sum_up, sum_down, sum_proj, sum_gains, sum_biases, sum_shift)
    *sums, sum_shift = settle(*sums) if ringed else sums
    return (embeddings, *sums, sum_shift.reshape(-1))


def solution(mesh):
    return jax.shard_map(
        body,
        mesh=mesh,
        in_specs=(
            P(("dp", "tensor"), None),
            P("dp"),
            P("dp", None),
            P(None, "dp", "tensor"),
            P("tensor", "dp"),
            P("dp", "tensor"),
            P("tensor", "dp"),
            P("dp", None),
            P(None, "dp"),
            P(None, "dp"),
            P("dp"),
            P(("dp", "tensor"), None),
        ),
        out_specs=(
            P(("dp", "tensor"), None),
            P(("dp", "tensor"), None),
            P(None, "dp", "tensor"),
            P("tensor", "dp"),
            P("dp", "tensor"),
            P("tensor", "dp"),
            P("dp", None),
            P(None, "dp"),
            P(None, "dp"),
            P("dp"),
        ),
        check_vma=False,
    )
```
